128 devices in a mesh: dp: 32 (over x_hi, y, z), pipe: 4 (over x_lo, core).
Axes of the slice: x: 4 (x_hi: 2, x_lo: 2; x = x_hi * 2 + x_lo), y: 4, z: 4, core: 2. Of those that a mesh axis runs over, the one named last changes fastest.
Arguments:
- inputs: bfloat16 [16, 256, 1024], P(None, 'dp'), may hold values from -6 to 6
- input_weight: bfloat16 [4, 1024, 4096], P('pipe'), may hold values from -0.1875 to 0.1875
- recurrent_weight: bfloat16 [4, 1024, 4096], P('pipe'), may hold values from -0.1875 to 0.1875
- gate_bias: float32 [4, 4096], P('pipe'), may hold values from -4 to 4
- lengths: int32 [256], P('dp'), may hold values from 1 to 16
- cotangent: bfloat16 [4, 16, 256, 1024], P('pipe', None, 'dp'), may hold values from -6 to 6
Outputs:
- grad_input: float32 [4, 1024, 4096], P('pipe', 'dp')
- grad_recurrent: float32 [4, 1024, 4096], P('pipe', 'dp')
- grad_bias: float32 [4, 4096], P('pipe', 'dp')
- final_hidden: bfloat16 [4, 256, 1024], P('pipe', 'dp')
- final_cell: float32 [4, 256, 1024], P('pipe', 'dp')
The draws below stay inside these ranges and needn't reach their ends.
All inputs are finite; a program needn't handle non-finite values.
Results may differ from the reference program's by a relative error of at most 0.004.
Values may be sent and summed in bfloat16 or wider, within the bound.
No kernel may reach another device: no remote copies, remote signals or barrier semaphores. Data moves between devices by JAX's collectives and lax.ppermute only.
A program may use at most 128 MiB of HBM per device.

```python
from functools import partial
import jax
import jax.numpy as jnp
from jax import lax

H = 1024
G = 4096
FRAMES = 16
LAYERS = 4
BATCH = 256


def plant(values, stream_key, least, largest):
    spot = [jax.random.randint(jax.random.fold_in(stream_key, axis), (), 0, length) for axis, length in enumerate(values.shape)]
    longest = values.shape.index(max(values.shape))
    neighbour = spot[:longest] + [(spot[longest] + 1) % values.shape[longest]] + spot[longest + 1:]
    return values.at[tuple(spot)].set(least).at[tuple(neighbour)].set(largest)


def with_spikes(array, key, source, target, blocks, factor):
    owner, partner = [(jnp.arange(array.shape[dim]) // (array.shape[dim] // blocks)).reshape([-1 if axis == dim else 1 for axis in range(array.ndim)]) for dim in (source, target)]
    chosen = jax.random.permutation(key, blocks)[partner]
    strong = (owner == chosen) | (owner == (partner + blocks // 2) % blocks)
    return jnp.where(strong, factor * array, array)


def levels(own_key, extent, split, least, high):
    level, own = 1.0, jax.random.fold_in(own_key, 6)
    for dim, shards_of in split:
        heights = jnp.exp(jax.random.uniform(jax.random.fold_in(own, dim), (shards_of,), jnp.float32, least / len(split), high / len(split)))
        level = level * jnp.repeat(heights, extent[dim] // shards_of).reshape([-1 if axis == dim else 1 for axis in range(len(extent))])
    return level


def normal_values(rng, shape, width, reach, cuts=(), kind=jnp.bfloat16):
    loudness = levels(rng, shape, cuts, -0.22, 0.18) if cuts else 1.0
    drawn = jax.random.normal(rng, shape, jnp.float32) * width * loudness
    return jnp.minimum(jnp.maximum(drawn, -reach), reach).astype(kind)


def noise_with(rng, extent, scale, reach, pieces, heavy, kind=jnp.bfloat16):
    values = scale * jax.random.normal(rng, extent, jnp.float32)
    if pieces:
        values = values * levels(rng, extent, pieces, -0.22, 0.18)
    return jnp.clip(with_spikes(values, jax.random.fold_in(rng, 3), *heavy), -reach, reach).astype(kind)


def setup_inputs(seed: int = 0) -> dict:
    keys = jax.random.split(jax.random.key(seed), 7)
    inputs = noise_with(keys[0], (FRAMES, BATCH, H), 1.0, 6.0, ((1, 32),), (1, 2, 32, 2.75))
    input_weight = normal_values(keys[1], (LAYERS, H, G), H ** -0.5, 0.1875, ((0, 4),))
    recurrent_weight = normal_values(keys[2], (LAYERS, H, G), H ** -0.5, 0.1875, ((0, 4),))
    gate_bias = normal_values(keys[3], (LAYERS, G), 1.0, 4.0, ((0, 4),), jnp.float32)
    lengths = plant(jax.random.randint(keys[4], (BATCH,), 1, FRAMES + 1), jax.random.fold_in(keys[4], 1), 1, FRAMES).astype(jnp.int32)
    cotangent = normal_values(keys[5], (LAYERS, FRAMES, BATCH, H), 1.0, 6.0, ((0, 4), (2, 32)))
    return {"inputs": inputs, "input_weight": input_weight, "recurrent_weight": recurrent_weight, "gate_bias": gate_bias, "lengths": lengths, "cotangent": cotangent}


def squash(value):
    return 1.0 / (1.0 + jnp.exp(-value))


def activate(pre_act, hidden_width):
    return jnp.concatenate([squash(pre_act[:, :2 * hidden_width]), jnp.tanh(pre_act[:, 2 * hidden_width:3 * hidden_width]), squash(pre_act[:, 3 * hidden_width:])], axis=1)


def forward_step(recurrent_weight, gate_bias, carry_state, step_inputs):
    hidden, cell_state = carry_state
    projected, alive_mask = step_inputs
    hidden_width = hidden.shape[1]
    pre_act = projected + jnp.dot(hidden, recurrent_weight, preferred_element_type=jnp.float32) + gate_bias
    gate_values = activate(pre_act, hidden_width)
    input_gate = gate_values[:, :hidden_width]
    forget_gate = gate_values[:, hidden_width:2 * hidden_width]
    cell_gate = gate_values[:, 2 * hidden_width:3 * hidden_width]
    output_gate = gate_values[:, 3 * hidden_width:]
    new_cell = forget_gate * cell_state + input_gate * cell_gate
    cand_hidden = (output_gate * jnp.tanh(new_cell)).astype(jnp.bfloat16)
    kept_cell = alive_mask * new_cell + (1.0 - alive_mask) * cell_state
    kept_hidden = jnp.where(alive_mask > 0, cand_hidden, hidden)
    emitted = jnp.where(alive_mask > 0, cand_hidden, jnp.zeros_like(cand_hidden))
    return (kept_hidden, kept_cell), (emitted, gate_values, kept_cell, hidden, cell_state)


def backward_step(recurrent_weight, carry_state, step_inputs):
    hidden_grad, cell_grad = carry_state
    upper_grad, own_grad, gate_values, cell_now, cell_prev, alive_mask = step_inputs
    hidden_width = hidden_grad.shape[1]
    input_gate = gate_values[:, :hidden_width]
    forget_gate = gate_values[:, hidden_width:2 * hidden_width]
    cell_gate = gate_values[:, 2 * hidden_width:3 * hidden_width]
    output_gate = gate_values[:, 3 * hidden_width:]
    out_grad = alive_mask * (hidden_grad + upper_grad.astype(jnp.float32) + own_grad.astype(jnp.float32))
    cell_tanh = jnp.tanh(cell_now)
    through_cell = alive_mask * cell_grad + out_grad * output_gate * (1.0 - cell_tanh * cell_tanh)
    pre_grad = jnp.concatenate([through_cell * cell_gate * input_gate * (1.0 - input_gate), through_cell * cell_prev * forget_gate * (1.0 - forget_gate), through_cell * input_gate * (1.0 - cell_gate * cell_gate), out_grad * cell_tanh * output_gate * (1.0 - output_gate)], axis=1).astype(jnp.bfloat16)
    back_hidden = (1.0 - alive_mask) * hidden_grad + lax.dot_general(pre_grad, recurrent_weight, (((1,), (1,)), ((), ())), preferred_element_type=jnp.float32)
    back_cell = (1.0 - alive_mask) * cell_grad + through_cell * forget_gate
    return (back_hidden, back_cell), pre_grad


def contract_rows(left, right):
    return lax.dot_general(left, right, (((0,), (0,)), ((), ())), preferred_element_type=jnp.float32)


def reference(inputs, input_weight, recurrent_weight, gate_bias, lengths, cotangent):
    frame_total, utterances, hidden_width = inputs.shape
    gate_width = 4 * hidden_width
    alive_all = (jnp.arange(frame_total, dtype=jnp.int32)[:, None] < lengths[None, :]).astype(jnp.float32)[:, :, None]
    layer_in = inputs
    saved = []
    last_hidden = []
    last_cell = []
    for layer_number in range(LAYERS):
        projected = jnp.dot(layer_in.reshape(-1, hidden_width), input_weight[layer_number], preferred_element_type=jnp.float32).reshape(frame_total, utterances, gate_width)
        start_state = (jnp.zeros((utterances, hidden_width), jnp.bfloat16), jnp.zeros((utterances, hidden_width), jnp.float32))
        (hidden, cell_state), records = lax.scan(partial(forward_step, recurrent_weight[layer_number], gate_bias[layer_number]), start_state, (projected, alive_all))
        emitted, gate_values, kept_cells, hidden_prev, cell_prev = records
        saved.append((layer_in, gate_values, kept_cells, hidden_prev, cell_prev))
        last_hidden.append(hidden)
        last_cell.append(cell_state)
        layer_in = emitted
    upper_grad = jnp.zeros((frame_total, utterances, hidden_width), jnp.bfloat16)
    grads_in = []
    grads_rec = []
    grads_bias = []
    for layer_number in reversed(range(LAYERS)):
        layer_in, gate_values, kept_cells, hidden_prev, cell_prev = saved[layer_number]
        zero_state = (jnp.zeros((utterances, hidden_width), jnp.float32), jnp.zeros((utterances, hidden_width), jnp.float32))
        final_carry, pre_grad = lax.scan(partial(backward_step, recurrent_weight[layer_number]), zero_state, (upper_grad, cotangent[layer_number], gate_values, kept_cells, cell_prev, alive_all), reverse=True)
        flat_grad = pre_grad.reshape(-1, gate_width)
        grads_in.append(contract_rows(layer_in.reshape(-1, hidden_width), flat_grad))
        grads_rec.append(contract_rows(hidden_prev.reshape(-1, hidden_width), flat_grad))
        grads_bias.append(jnp.sum(flat_grad.astype(jnp.float32), axis=0))
        upper_grad = lax.dot_general(flat_grad, input_weight[layer_number], (((1,), (1,)), ((), ())), preferred_element_type=jnp.float32).astype(jnp.bfloat16).reshape(frame_total, utterances, hidden_width)
    grad_input = jnp.stack(grads_in[::-1])
    grad_recurrent = jnp.stack(grads_rec[::-1])
    grad_bias = jnp.stack(grads_bias[::-1])
    return (grad_input, grad_recurrent, grad_bias, jnp.stack(last_hidden), jnp.stack(last_cell))
```

```python
from functools import partial

import jax
import jax.numpy as jnp
from jax import lax
from jax.experimental import pallas as pl
from jax.experimental.pallas import tpu as pltpu
from jax.sharding import Mesh, PartitionSpec as P

BLOCK = 4
CHUNK = 256
DP = ("xh", "y", "z")
VMEM = pl.BlockSpec(memory_space=pltpu.VMEM)
SMEM = pl.BlockSpec(memory_space=pltpu.SMEM)
LIMIT = 60 * 2**20


def squash(value):
    return 0.5 * jnp.tanh(0.5 * value) + 0.5


def dot(a, b):
    return jnp.dot(a, b, preferred_element_type=jnp.float32)


def dot_t(a, b):
    return lax.dot_general(a, b, (((1,), (1,)), ((), ())), preferred_element_type=jnp.float32)


def forward_kernel(info, own, arrived, wi, wr, bias, lens, _x, _g, _c, _h, emitted, xs, gates, cells, hs, proj):
    active, fs, first = info[0], info[1], info[2]
    span, rows, width = arrived.shape

    @pl.when(active == 1)
    def _():
        @pl.when(first == 1)
        def _():
            xs[pl.ds(fs, span)] = own[pl.ds(fs, span)]

        @pl.when(first == 0)
        def _():
            xs[pl.ds(fs, span)] = arrived[...]

        x = xs[pl.ds(fs, span)].reshape(span * rows, width)
        proj[...] = (dot(x, wi[...]) + bias[...]).reshape(span, rows, 4 * width)

        @pl.when(fs == 0)
        def _():
            hs[0] = jnp.zeros((rows, width), jnp.bfloat16)
            cells[0] = jnp.zeros((rows, width), jnp.float32)

        def frame(t, carry):
            fr = fs + t
            h = hs[fr]
            for j in range(0, width, CHUNK):
                part = pl.ds(j, CHUNK)

                def pre(gate):
                    col = pl.ds(gate * width + j, CHUNK)
                    return proj[t, :, col] + dot(h, wr[:, col])

                alive = fr < lens[:, part]
                i, f, g, o = squash(pre(0)), squash(pre(1)), jnp.tanh(pre(2)), squash(pre(3))
                c = cells[fr, :, part]
                new_c = f * c + i * g
                new_h = (o * jnp.tanh(new_c)).astype(jnp.bfloat16)
                old_h = hs[fr, :, part]
                gates[fr, :, pl.ds(j, CHUNK)] = i
                gates[fr, :, pl.ds(width + j, CHUNK)] = f
                gates[fr, :, pl.ds(2 * width + j, CHUNK)] = g
                gates[fr, :, pl.ds(3 * width + j, CHUNK)] = o
                cells[fr + 1, :, part] = jnp.where(alive, new_c, c)
                hs[fr + 1, :, part] = jnp.where(alive, new_h, old_h)
                emitted[t, :, part] = jnp.where(alive, new_h, jnp.zeros_like(new_h))
            return carry

        lax.fori_loop(0, span, frame, 0)


def backward_kernel(info, gates, cells, cot, arrived, wi, wr, lens, _dh, _dc, rows_out, lower, dh, dc):
    active, fs, top, bottom = info[0], info[1], info[2], info[3]
    span, rows, width = arrived.shape
    total = gates.shape[0]

    @pl.when(active == 1)
    def _():
        @pl.when(fs + span == total)
        def _():
            dh[...] = jnp.zeros((rows, width), jnp.float32)
            dc[...] = jnp.zeros((rows, width), jnp.float32)

        def frame(n, carry):
            t = span - 1 - n
            fr = fs + t
            acc = None
            for j in range(0, width, CHUNK):
                part = pl.ds(j, CHUNK)
                alive = fr < lens[:, part]
                i = gates[fr, :, pl.ds(j, CHUNK)]
                f = gates[fr, :, pl.ds(width + j, CHUNK)]
                g = gates[fr, :, pl.ds(2 * width + j, CHUNK)]
                o = gates[fr, :, pl.ds(3 * width + j, CHUNK)]
                u = jnp.where(top == 1, 0.0, arrived[t, :, part].astype(jnp.float32))
                e = jnp.where(alive, dh[:, part] + u + cot[fr, :, part].astype(jnp.float32), 0.0)
                k = jnp.tanh(cells[fr + 1, :, part])
                old_dc = dc[:, part]
                dcell = jnp.where(alive, old_dc, 0.0) + e * o * (1.0 - k * k)
                parts = (
                    dcell * g * i * (1.0 - i),
                    dcell * cells[fr, :, part] * f * (1.0 - f),
                    dcell * i * (1.0 - g * g),
                    e * k * o * (1.0 - o),
                )
                dc[:, part] = jnp.where(alive, 0.0, old_dc) + dcell * f
                dh[:, part] = jnp.where(alive, 0.0, dh[:, part])
                for gate, value in enumerate(parts):
                    col = pl.ds(gate * width + j, CHUNK)
                    d = value.astype(jnp.bfloat16)
                    rows_out[t, :, col] = d
                    term = dot_t(d, wr[:, col])
                    acc = term if acc is None else acc + term
            dh[...] = dh[...] + acc
            return carry

        lax.fori_loop(0, span, frame, 0)

        @pl.when(bottom == 0)
        def _():
            d = rows_out[...].reshape(span * rows, 4 * width)
            lower[...] = dot_t(d, wi[...]).astype(jnp.bfloat16).reshape(span, rows, width)


def shape(dims, kind):
    return jax.ShapeDtypeStruct(dims, kind)


def local(inputs, input_weight, recurrent_weight, gate_bias, lengths, cotangent):
    wi, wr, cot = input_weight[0], recurrent_weight[0], cotangent[0]
    total, rows, width = inputs.shape
    gated = 4 * width
    stages = lax.axis_size("pipe")
    stage = lax.axis_index("pipe")
    blocks = total // BLOCK
    ticks = blocks + stages - 1
    lens = jnp.broadcast_to(lengths[:, None], (rows, width))
    params = pltpu.CompilerParams(vmem_limit_bytes=LIMIT)
    bf16, f32 = jnp.bfloat16, jnp.float32

    forward = pl.pallas_call(
        forward_kernel,
        out_shape=(
            shape((BLOCK, rows, width), bf16),
            shape((total, rows, width), bf16),
            shape((total, rows, gated), f32),
            shape((total + 1, rows, width), f32),
            shape((total + 1, rows, width), bf16),
        ),
        in_specs=[SMEM] + [VMEM] * 10,
        out_specs=(VMEM,) * 5,
        scratch_shapes=[pltpu.VMEM((BLOCK, rows, gated), f32)],
        input_output_aliases={7: 1, 8: 2, 9: 3, 10: 4},
        compiler_params=params,
        name="forward_tick",
    )
    xs = jnp.zeros((total, rows, width), bf16)
    gates = jnp.zeros((total, rows, gated), f32)
    cells = jnp.zeros((total + 1, rows, width), f32)
    hs = jnp.zeros((total + 1, rows, width), bf16)
    arrived = jnp.zeros((BLOCK, rows, width), bf16)
    up = [(i, i + 1) for i in range(stages - 1)]
    down = [(i + 1, i) for i in range(stages - 1)]
    for tick in range(ticks):
        at = tick - stage
        active = (at >= 0) & (at < blocks)
        info = jnp.stack([active.astype(jnp.int32), jnp.clip(at, 0, blocks - 1) * BLOCK, (stage == 0).astype(jnp.int32)])
        emitted, xs, gates, cells, hs = forward(info, inputs, arrived, wi, wr, gate_bias, lens, xs, gates, cells, hs)
        if tick < ticks - 1:
            arrived = lax.ppermute(emitted, "pipe", up)

    backward = pl.pallas_call(
        backward_kernel,
        out_shape=(
            shape((BLOCK, rows, gated), bf16),
            shape((BLOCK, rows, width), bf16),
            shape((rows, width), f32),
            shape((rows, width), f32),
        ),
        in_specs=[SMEM] + [VMEM] * 9,
        out_specs=(VMEM,) * 4,
        input_output_aliases={8: 2, 9: 3},
        compiler_params=params,
        name="backward_tick",
    )
    y, ny = lax.axis_index("y"), lax.axis_size("y")
    nx, nz = lax.axis_size("xh"), lax.axis_size("z")
    own = width // (nx * ny * nz)

    def pieces(block, to):
        return [block if d == 0 else lax.ppermute(to(d), "y", [(i, (i + d) % ny) for i in range(ny)]) for d in range(ny)]

    both = jnp.concatenate([xs.reshape(-1, width), hs[:total].reshape(-1, width)], axis=1)
    both = both.reshape(total * rows, 2, nx, ny, nz * own)

    def slice_for(d):
        return lax.dynamic_index_in_dim(both, (y + d) % ny, 3, keepdims=False).reshape(total * rows, -1)

    lefts = pieces(slice_for(0), slice_for)

    dh = jnp.zeros((rows, width), f32)
    dc = jnp.zeros((rows, width), f32)
    arrived = jnp.zeros((BLOCK, rows, width), bf16)
    records = [None] * ticks
    for tick in range(ticks):
        offset = tick - (stages - 1 - stage)
        active = (offset >= 0) & (offset < blocks)
        at = blocks - 1 - jnp.clip(offset, 0, blocks - 1)
        info = jnp.stack([
            active.astype(jnp.int32),
            at * BLOCK,
            (stage == stages - 1).astype(jnp.int32),
            (stage == 0).astype(jnp.int32),
        ])
        records[tick], lower, dh, dc = backward(info, gates, cells, cot, arrived, wi, wr, lens, dh, dc)
        if tick < ticks - 1:
            arrived = lax.ppermute(lower, "pipe", down)
    rows_all = jnp.concatenate(records[::-1], axis=0)
    rows_all = lax.dynamic_slice_in_dim(rows_all, stage * BLOCK, total, 0)
    mine = rows_all.reshape(total * rows, gated)
    bias_part = jnp.sum(mine.astype(f32), axis=0).reshape(nx * ny * nz, -1)
    bias_all = lax.all_to_all(bias_part, DP, 0, 0, tiled=True)
    grad_bias = jnp.sum(bias_all, axis=0)

    rights = pieces(mine, lambda d: mine)
    left = jnp.concatenate(lefts, axis=0)
    right = jnp.concatenate(rights, axis=0)
    part = lax.dot_general(left, right, (((0,), (0,)), ((), ())), preferred_element_type=f32).astype(bf16)
    part = part.reshape(2 * nx, nz, own, gated)
    part = jnp.swapaxes(part, 0, 1)
    got = lax.all_to_all(part, "z", 0, 0, tiled=True)
    summed = jnp.sum(got.astype(f32), axis=0).reshape(2, nx, own, gated)
    xh = lax.axis_index("xh")
    keep = lax.dynamic_index_in_dim(summed, xh, 1, keepdims=False)
    give = lax.dynamic_index_in_dim(summed, (xh + 1) % nx, 1, keepdims=False).astype(bf16)
    grads = keep + lax.ppermute(give, "xh", [(i, (i + 1) % nx) for i in range(nx)]).astype(f32)
    return (grads[0][None], grads[1][None], grad_bias[None], hs[total][None], cells[total][None])


def solution(mesh):
    fine = Mesh(mesh.devices.reshape(2, 4, 4, 4), ("xh", "y", "z", "pipe"))
    return jax.shard_map(
        local,
        mesh=fine,
        in_specs=(
            P(None, DP, None),
            P("pipe", None, None),
            P("pipe", None, None),
            P("pipe", None),
            P(DP),
            P("pipe", None, DP, None),
        ),
        out_specs=(
            P("pipe", DP, None),
            P("pipe", DP, None),
            P("pipe", DP),
            P("pipe", DP, None),
            P("pipe", DP, None),
        ),
        check_vma=False,
    )
```

```python
from functools import partial

import jax
import jax.numpy as jnp
from jax import lax
from jax.experimental import pallas as pl
from jax.experimental.pallas import tpu as pltpu
from jax.sharding import Mesh, PartitionSpec as P

BLOCK = 4
CHUNK = 256
PANEL = 256
SLOTS = 4
DP = ("xh", "y", "z")
VMEM = pl.BlockSpec(memory_space=pltpu.VMEM)
SMEM = pl.BlockSpec(memory_space=pltpu.SMEM)
HBM = pl.BlockSpec(memory_space=pltpu.HBM)
LIMIT = 8 * 2**20


def squash(value):
    return 0.5 * jnp.tanh(0.5 * value) + 0.5


def dot(a, b):
    return jnp.dot(a, b, preferred_element_type=jnp.float32)


def setup_kernel(wi_far, wr_far, _a, _p, _h, _c, wi, wr, *rest):
    sems = rest[-1]
    copies = [pltpu.make_async_copy(a, b, sems.at[n]) for n, (a, b) in enumerate(((wi_far, wi), (wr_far, wr)))]
    for c in copies:
        c.start()
    for c in copies:
        c.wait()


def turn(share, shares, pairs, stage, sems):
    panels = pairs[0][1].shape[0] // PANEL
    groups = panels // SLOTS
    low = share * 2 * groups // shares
    high = (share + 1) * 2 * groups // shares

    for n, (source, target) in enumerate(pairs):

        def body(group, carry, source=source, target=target):
            copies = []
            for slot in range(SLOTS):
                at = pl.multiple_of((group * SLOTS + slot) * PANEL, PANEL)
                stage[slot] = source[:, pl.ds(at, PANEL)].T
                copies.append(pltpu.make_async_copy(stage.at[slot], target.at[pl.ds(at, PANEL)], sems.at[slot]))
                copies[-1].start()
            for c in copies:
                c.wait()
            return carry

        begin, end = (jnp.clip(v - n * groups, 0, groups) for v in (low, high))
        lax.fori_loop(begin, end, body, 0)


def forward_kernel(place, own, arrived, bias, lens, *rest, tick, stages):
    emitted, wi, wr, xs, gates, cells, hs, wit_far, wrt_far = rest[8:17]
    proj, staged, sems, load_sems = rest[-4:]
    span, rows, width = arrived.shape
    stage = place[0]
    blocks = own.shape[0] // span
    at = tick - stage
    active = (at >= 0) & (at < blocks)
    fs = at * span
    last = tick == blocks + stages - 2
    pairs = ((wr, wrt_far), (wi, wit_far))
    loads = []
    if last:
        wit, wrt = rest[17:19]
        loads = [pltpu.make_async_copy(far, to, load_sems.at[n]) for n, (far, to) in enumerate(((wit_far, wit), (wrt_far, wrt)))]

    @pl.when(jnp.logical_not(active))
    def _():
        turn(jnp.where(at < 0, tick, tick - blocks), stages - 1, pairs, staged, sems)

    for c in loads:
        c.start()

    @pl.when(active)
    def _():
        @pl.when(stage == 0)
        def _():
            xs[pl.ds(fs, span)] = own[pl.ds(fs, span)]

        @pl.when(stage > 0)
        def _():
            xs[pl.ds(fs, span)] = arrived[...]

        x = xs[pl.ds(fs, span)].reshape(span * rows, width)
        proj[...] = (dot(x, wi[...]) + bias[...]).reshape(span, rows, 4 * width)

        @pl.when(fs == 0)
        def _():
            hs[0] = jnp.zeros((rows, width), jnp.bfloat16)
            cells[0] = jnp.zeros((rows, width), jnp.float32)

        def frame(t, carry):
            fr = fs + t
            h = hs[fr]
            for j in range(0, width, CHUNK):
                part = pl.ds(j, CHUNK)

                def pre(gate):
                    col = pl.ds(gate * width + j, CHUNK)
                    return proj[t, :, col] + dot(h, wr[:, col])

                alive = fr < lens[:, part]
                i, f, g, o = squash(pre(0)), squash(pre(1)), jnp.tanh(pre(2)), squash(pre(3))
                c = cells[fr, :, part]
                new_c = f * c + i * g
                new_h = (o * jnp.tanh(new_c)).astype(jnp.bfloat16)
                old_h = hs[fr, :, part]
                gates[fr, :, pl.ds(j, CHUNK)] = i
                gates[fr, :, pl.ds(width + j, CHUNK)] = f
                gates[fr, :, pl.ds(2 * width + j, CHUNK)] = g
                gates[fr, :, pl.ds(3 * width + j, CHUNK)] = o
                cells[fr + 1, :, part] = jnp.where(alive, new_c, c)
                hs[fr + 1, :, part] = jnp.where(alive, new_h, old_h)
                emitted[t, :, part] = jnp.where(alive, new_h, jnp.zeros_like(new_h))
            return carry

        lax.fori_loop(0, span, frame, 0)

    for c in loads:
        c.wait()


def backward_kernel(place, cot, arrived, lens, *rest, tick, stages):
    lower, dps, gates, cells, wit, wrt, dh, dc = rest[7:]
    span, rows, width = arrived.shape
    total = gates.shape[0]
    stage = place[0]
    blocks = total // span
    offset = tick - (stages - 1 - stage)
    fs = (blocks - 1 - offset) * span

    @pl.when((offset >= 0) & (offset < blocks))
    def _():
        @pl.when(fs + span == total)
        def _():
            dh[...] = jnp.zeros((rows, width), jnp.float32)
            dc[...] = jnp.zeros((rows, width), jnp.float32)

        def frame(n, carry):
            t = span - 1 - n
            fr = fs + t
            acc = None
            for j in range(0, width, CHUNK):
                part = pl.ds(j, CHUNK)
                alive = fr < lens[:, part]
                i = gates[fr, :, pl.ds(j, CHUNK)]
                f = gates[fr, :, pl.ds(width + j, CHUNK)]
                g = gates[fr, :, pl.ds(2 * width + j, CHUNK)]
                o = gates[fr, :, pl.ds(3 * width + j, CHUNK)]
                u = jnp.where(stage == stages - 1, 0.0, arrived[t, :, part].astype(jnp.float32))
                e = jnp.where(alive, dh[:, part] + u + cot[fr, :, part].astype(jnp.float32), 0.0)
                k = jnp.tanh(cells[fr + 1, :, part])
                old_dc = dc[:, part]
                dcell = jnp.where(alive, old_dc, 0.0) + e * o * (1.0 - k * k)
                parts = (
                    dcell * g * i * (1.0 - i),
                    dcell * cells[fr, :, part] * f * (1.0 - f),
                    dcell * i * (1.0 - g * g),
                    e * k * o * (1.0 - o),
                )
                dc[:, part] = jnp.where(alive, 0.0, old_dc) + dcell * f
                dh[:, part] = jnp.where(alive, 0.0, dh[:, part])
                for gate, value in enumerate(parts):
                    col = pl.ds(gate * width + j, CHUNK)
                    d = value.astype(jnp.bfloat16)
                    dps[fr, :, col] = d
                    term = dot(d, wrt[col, :])
                    acc = term if acc is None else acc + term
            dh[...] = dh[...] + acc
            return carry

        lax.fori_loop(0, span, frame, 0)

        @pl.when(stage > 0)
        def _():
            d = dps[pl.ds(fs, span)].reshape(span * rows, 4 * width)
            lower[...] = dot(d, wit[...]).astype(jnp.bfloat16).reshape(span, rows, width)


def shape(dims, kind):
    return pltpu.VMEM(dims, kind)


def near(array):
    return pltpu.with_memory_space_constraint(array, pltpu.VMEM)


def local(inputs, input_weight, recurrent_weight, gate_bias, lengths, cotangent):
    total, rows, width = inputs.shape
    gated = 4 * width
    stages = lax.axis_size("pipe")
    stage = lax.axis_index("pipe")
    blocks = total // BLOCK
    ticks = blocks + stages - 1
    lens = near(jnp.broadcast_to(lengths[:, None], (rows, width)))
    cot, inputs, gate_bias = near(cotangent[0]), near(inputs), near(gate_bias)
    params = pltpu.CompilerParams(vmem_limit_bytes=LIMIT)
    bf16, f32 = jnp.bfloat16, jnp.float32

    flat, turned = shape((width, gated), bf16), shape((gated, width), bf16)
    kept_gates, kept_cells = shape((total, rows, gated), f32), shape((total + 1, rows, width), f32)
    kept_rows, one = shape((total, rows, gated), bf16), shape((rows, width), f32)
    state = (flat, flat, shape((total, rows, width), bf16), kept_gates, kept_cells)
    far = pltpu.HBM((gated, width), bf16)
    state += (shape((total + 1, rows, width), bf16), far, far)
    arrived, dps, dh, dc, *held = pl.pallas_call(
        setup_kernel,
        out_shape=(shape((BLOCK, rows, width), bf16), kept_rows, one, one) + state,
        in_specs=[HBM] * 2,
        out_specs=(VMEM,) * 10 + (HBM,) * 2,
        scratch_shapes=[pltpu.SemaphoreType.DMA((2,))],
        compiler_params=params,
        name="setup",
    )(*(pltpu.with_memory_space_constraint(w[0], pltpu.HBM) for w in (input_weight, recurrent_weight)))
    def forward(tick):
        extra = (turned, turned) if tick == ticks - 1 else ()
        return pl.pallas_call(
            partial(forward_kernel, tick=tick, stages=stages),
            out_shape=(shape((BLOCK, rows, width), bf16),) + state + extra,
            in_specs=[SMEM] + [VMEM] * 10 + [HBM] * 2,
            out_specs=(VMEM,) * 7 + (HBM,) * 2 + (VMEM,) * len(extra),
            scratch_shapes=[
                pltpu.VMEM((BLOCK, rows, gated), f32),
                pltpu.VMEM((SLOTS, PANEL, width), bf16),
                pltpu.SemaphoreType.DMA((SLOTS,)),
                pltpu.SemaphoreType.DMA((2,)),
            ],
            input_output_aliases={5 + n: 1 + n for n in range(8)},
            compiler_params=params,
            name="forward_tick",
        )

    place = jnp.reshape(stage, (1,)).astype(jnp.int32)
    up = [(i, i + 1) for i in range(stages - 1)]
    down = [(i + 1, i) for i in range(stages - 1)]
    for tick in range(ticks):
        emitted, *held = forward(tick)(place, inputs, near(arrived), gate_bias, lens, *held)
        if tick < ticks - 1:
            arrived = lax.ppermute(emitted, "pipe", up)

    _, _, xs, gates, cells, hs, _, _, wit, wrt = held

    def backward(tick):
        return pl.pallas_call(
            partial(backward_kernel, tick=tick, stages=stages),
            out_shape=(shape((BLOCK, rows, width), bf16), kept_rows, kept_gates, kept_cells, turned, turned, one, one),
            in_specs=[SMEM] + [VMEM] * 10,
            out_specs=(VMEM,) * 8,
            input_output_aliases={4 + n: 1 + n for n in range(7)},
            compiler_params=params,
            name="backward_tick",
        )

    y, ny = lax.axis_index("y"), lax.axis_size("y")
    nx, nz = lax.axis_size("xh"), lax.axis_size("z")
    own = width // (nx * ny * nz)

    def pieces(block, to):
        return [block if d == 0 else lax.ppermute(to(d), "y", [(i, (i + d) % ny) for i in range(ny)]) for d in range(ny)]

    both = jnp.concatenate([xs.reshape(-1, width), hs[:total].reshape(-1, width)], axis=1)
    both = both.reshape(total * rows, 2, nx, ny, nz * own)

    def slice_for(d):
        return lax.dynamic_index_in_dim(both, (y + d) % ny, 3, keepdims=False).reshape(total * rows, -1)

    lefts = pieces(slice_for(0), slice_for)

    final_hidden, final_cell = hs[total], cells[total]
    held = [dps, gates, cells, wit, wrt, dh, dc]
    arrived = emitted
    for tick in range(ticks):
        lower, *held = backward(tick)(place, cot, near(arrived), lens, *held)
        if tick < ticks - 1:
            arrived = lax.ppermute(lower, "pipe", down)
    mine = held[0].reshape(total * rows, gated)
    bias_part = jnp.sum(mine.astype(f32), axis=0).reshape(nx * ny * nz, -1)
    bias_all = lax.all_to_all(bias_part, DP, 0, 0, tiled=True)
    grad_bias = jnp.sum(bias_all, axis=0)

    rights = pieces(mine, lambda d: mine)
    left = jnp.concatenate(lefts, axis=0)
    right = jnp.concatenate(rights, axis=0)
    part = lax.dot_general(left, right, (((0,), (0,)), ((), ())), preferred_element_type=f32).astype(bf16)
    part = part.reshape(2 * nx, nz, own, gated)
    part = jnp.swapaxes(part, 0, 1)
    got = lax.all_to_all(part, "z", 0, 0, tiled=True)
    summed = jnp.sum(got.astype(f32), axis=0).reshape(2, nx, own, gated)
    xh = lax.axis_index("xh")
    keep = lax.dynamic_index_in_dim(summed, xh, 1, keepdims=False)
    give = lax.dynamic_index_in_dim(summed, (xh + 1) % nx, 1, keepdims=False).astype(bf16)
    grads = keep + lax.ppermute(give, "xh", [(i, (i + 1) % nx) for i in range(nx)]).astype(f32)
    return (grads[0][None], grads[1][None], grad_bias[None], final_hidden[None], final_cell[None])


def solution(mesh):
    fine = Mesh(mesh.devices.reshape(2, 4, 4, 4), ("xh", "y", "z", "pipe"))
    return jax.shard_map(
        local,
        mesh=fine,
        in_specs=(
            P(None, DP, None),
            P("pipe", None, None),
            P("pipe", None, None),
            P("pipe", None),
            P(DP),
            P("pipe", None, DP, None),
        ),
        out_specs=(
            P("pipe", DP, None),
            P("pipe", DP, None),
            P("pipe", DP),
            P("pipe", DP, None),
            P("pipe", DP, None),
        ),
        check_vma=False,
    )
```

```python
from functools import partial

import jax
import jax.numpy as jnp
from jax import lax
from jax.experimental import pallas as pl
from jax.experimental.pallas import tpu as pltpu
from jax.sharding import Mesh, PartitionSpec as P

BLOCK = 4
CHUNK = 256
PANEL = 256
SLOTS = 4
DP = ("xh", "y", "z")
VMEM = pl.BlockSpec(memory_space=pltpu.VMEM)
SMEM = pl.BlockSpec(memory_space=pltpu.SMEM)
HBM = pl.BlockSpec(memory_space=pltpu.HBM)
LIMIT = 8 * 2**20


def squash(value):
    return 0.5 * jnp.tanh(0.5 * value) + 0.5


def dot(a, b):
    return jnp.dot(a, b, preferred_element_type=jnp.float32)


def setup_kernel(wi_far, wr_far, _a, _y, _z, _p, _h, _c, wi, wr, *rest):
    sems = rest[-1]
    copies = [pltpu.make_async_copy(a, b, sems.at[n]) for n, (a, b) in enumerate(((wi_far, wi), (wr_far, wr)))]
    for c in copies:
        c.start()
    for c in copies:
        c.wait()


def turn(share, shares, pairs, stage, sems):
    panels = pairs[0][1].shape[0] // PANEL
    groups = panels // SLOTS
    low = share * 2 * groups // shares
    high = (share + 1) * 2 * groups // shares

    for n, (source, target) in enumerate(pairs):

        def body(group, carry, source=source, target=target):
            copies = []
            for slot in range(SLOTS):
                at = pl.multiple_of((group * SLOTS + slot) * PANEL, PANEL)
                stage[slot] = source[:, pl.ds(at, PANEL)].T
                copies.append(pltpu.make_async_copy(stage.at[slot], target.at[pl.ds(at, PANEL)], sems.at[slot]))
                copies[-1].start()
            for c in copies:
                c.wait()
            return carry

        begin, end = (jnp.clip(v - n * groups, 0, groups) for v in (low, high))
        lax.fori_loop(begin, end, body, 0)


def forward_kernel(place, own, arrived, bias, lens, *rest, tick, stages):
    emitted, wi, wr, xs, gates, cells, hs, wit_far, wrt_far = rest[8:17]
    proj, staged, sems, load_sems = rest[-4:]
    span, rows, width = arrived.shape
    stage = place[0]
    blocks = own.shape[0] // span
    at = tick - stage
    active = (at >= 0) & (at < blocks)
    fs = at * span
    last = tick == blocks + stages - 2
    pairs = ((wr, wrt_far), (wi, wit_far))
    loads = []
    if last:
        wit, wrt = rest[17:19]
        loads = [pltpu.make_async_copy(far, to, load_sems.at[n]) for n, (far, to) in enumerate(((wit_far, wit), (wrt_far, wrt)))]

    @pl.when(jnp.logical_not(active))
    def _():
        turn(jnp.where(at < 0, tick, tick - blocks), stages - 1, pairs, staged, sems)

    for c in loads:
        c.start()

    @pl.when(active)
    def _():
        @pl.when(stage == 0)
        def _():
            xs[pl.ds(fs, span)] = own[pl.ds(fs, span)]

        @pl.when(stage > 0)
        def _():
            xs[pl.ds(fs, span)] = arrived[...]

        x = xs[pl.ds(fs, span)].reshape(span * rows, width)
        proj[...] = (dot(x, wi[...]) + bias[...]).reshape(span, rows, 4 * width)

        @pl.when(fs == 0)
        def _():
            hs[0] = jnp.zeros((rows, width), jnp.bfloat16)
            cells[0] = jnp.zeros((rows, width), jnp.float32)

        def frame(t, carry):
            fr = fs + t
            h = hs[fr]
            for j in range(0, width, CHUNK):
                part = pl.ds(j, CHUNK)

                def pre(gate):
                    col = pl.ds(gate * width + j, CHUNK)
                    return proj[t, :, col] + dot(h, wr[:, col])

                alive = fr < lens[:, part]
                i, f, g, o = squash(pre(0)), squash(pre(1)), jnp.tanh(pre(2)), squash(pre(3))
                c = cells[fr, :, part]
                new_c = f * c + i * g
                new_h = (o * jnp.tanh(new_c)).astype(jnp.bfloat16)
                old_h = hs[fr, :, part]
                gates[fr, :, pl.ds(j, CHUNK)] = i
                gates[fr, :, pl.ds(width + j, CHUNK)] = f
                gates[fr, :, pl.ds(2 * width + j, CHUNK)] = g
                gates[fr, :, pl.ds(3 * width + j, CHUNK)] = o
                cells[fr + 1, :, part] = jnp.where(alive, new_c, c)
                hs[fr + 1, :, part] = jnp.where(alive, new_h, old_h)
                emitted[t, :, part] = jnp.where(alive, new_h, jnp.zeros_like(new_h))
            return carry

        lax.fori_loop(0, span, frame, 0)

    for c in loads:
        c.wait()


def block_at(tick, stage, stages, blocks):
    offset = tick - (stages - 1 - stage)
    return blocks - 1 - offset, (offset >= 0) & (offset < blocks)


def keep_arrived(arrivals, stores, tick, stage, stages):
    if not arrivals:
        return
    span = arrivals[0].shape[0]
    at, valid = block_at(tick, stage, stages, stores[0].shape[1] // span)

    @pl.when(valid)
    def _():
        n = len(arrivals) // 2
        for side, store in enumerate(stores):
            for d in range(n):
                store[d, pl.ds(at * span, span)] = arrivals[side * n + d][...]


def backward_kernel(place, cot, arrived, lens, *rest, tick, stages, late):
    arrivals = rest[:late]
    lower, send_y, send_z, gy, gz, dps, gates, cells, wit, wrt, dh, dc = rest[late + 9 :]
    span, rows, width = arrived.shape
    total = gates.shape[0]
    half = 2 * width
    stage = place[0]
    blocks = total // span
    at, active = block_at(tick, stage, stages, blocks)
    fs = at * span
    keep_arrived(arrivals, (gy, gz), tick - 2, stage, stages)

    @pl.when(active)
    def _():
        @pl.when(fs + span == total)
        def _():
            dh[...] = jnp.zeros((rows, width), jnp.float32)
            dc[...] = jnp.zeros((rows, width), jnp.float32)

        def frame(n, carry):
            t = span - 1 - n
            fr = fs + t
            acc = None
            for j in range(0, width, CHUNK):
                part = pl.ds(j, CHUNK)
                alive = fr < lens[:, part]
                i = gates[fr, :, pl.ds(j, CHUNK)]
                f = gates[fr, :, pl.ds(width + j, CHUNK)]
                g = gates[fr, :, pl.ds(2 * width + j, CHUNK)]
                o = gates[fr, :, pl.ds(3 * width + j, CHUNK)]
                u = jnp.where(stage == stages - 1, 0.0, arrived[t, :, part].astype(jnp.float32))
                e = jnp.where(alive, dh[:, part] + u + cot[fr, :, part].astype(jnp.float32), 0.0)
                k = jnp.tanh(cells[fr + 1, :, part])
                old_dc = dc[:, part]
                dcell = jnp.where(alive, old_dc, 0.0) + e * o * (1.0 - k * k)
                parts = (
                    dcell * g * i * (1.0 - i),
                    dcell * cells[fr, :, part] * f * (1.0 - f),
                    dcell * i * (1.0 - g * g),
                    e * k * o * (1.0 - o),
                )
                dc[:, part] = jnp.where(alive, 0.0, old_dc) + dcell * f
                dh[:, part] = jnp.where(alive, 0.0, dh[:, part])
                for gate, value in enumerate(parts):
                    col = pl.ds(gate * width + j, CHUNK)
                    d = value.astype(jnp.bfloat16)
                    dps[fr, :, col] = d
                    if gate < 2:
                        send_y[t, :, col] = d
                    else:
                        send_z[t, :, pl.ds(gate * width + j - half, CHUNK)] = d
                    term = dot(d, wrt[col, :])
                    acc = term if acc is None else acc + term
            dh[...] = dh[...] + acc
            return carry

        lax.fori_loop(0, span, frame, 0)

        @pl.when(stage > 0)
        def _():
            d = dps[pl.ds(fs, span)].reshape(span * rows, 4 * width)
            lower[...] = dot(d, wit[...]).astype(jnp.bfloat16).reshape(span, rows, width)


def prepare_kernel(place, xs, hs, own_y, own_z, *rest):
    sends, whole = rest[:6], rest[6]
    total, rows, width = xs.shape
    y, z = place[1], place[2]
    for n, source in enumerate((xs, hs)):
        flat = source[pl.ds(0, total)].reshape(total * rows, width)
        whole[pl.ds(2 * n, 2)] = flat.T.reshape((2,) + whole.shape[1:])
    for d in range(4):
        to_y = own_y if d == 0 else sends[d - 1]
        to_z = own_z if d == 0 else sends[d + 2]
        for g in range(4):
            to_y[g] = whole[g, lax.rem(y + d, 4)]
            for i in range(4):
                to_z[g, i] = whole[g, i, lax.rem(z + d, 4)]


def combine_kernel(place, *rest, stages, ticks, late):
    a_y, a_z, dps = rest[:4], rest[4:8], rest[8]
    arrivals = rest[9 : 9 + 2 * late]
    gy, gz, bias, own_y, own_z, *sends = rest[11 + 2 * late : -2]
    left_all, right = rest[-2:]
    stage, y, z = place[0], place[1], place[2]
    total, rows, gated = dps.shape
    half = gated // 2
    n = total * rows
    fine = left_all.shape[2]
    keep_arrived(arrivals[:late], (gy, gz), ticks - 2, stage, stages)
    keep_arrived(arrivals[late:], (gy, gz), ticks - 1, stage, stages)
    bias[...] = jnp.sum(dps[...].reshape(n, gated).astype(jnp.float32), axis=0, keepdims=True)
    for side, (pieces, store, me, own) in enumerate(((a_y, gy, z, own_y), (a_z, gz, y, own_z))):
        for d in range(4):
            for g in range(4):
                left_all[g, :, :, pl.ds(d * n, n)] = pieces[d][g]
        right[pl.ds(0, n)] = dps[:, :, pl.ds(side * half, half)].reshape(n, half)
        right[pl.ds(n, 3 * n)] = store[...].reshape(3 * n, half)
        for d in range(4):
            left = left_all[:, lax.rem(me + d, 4)].reshape(4 * fine, 4 * n)
            part = dot(left, right[...]).reshape(4, fine, half)
            if d == 0:
                own[...] = part
            else:
                sends[3 * side + d - 1][...] = part.astype(jnp.bfloat16)


def finish_kernel(place, own_y, own_z, *rest):
    arrivals, keep, give = rest[:6], rest[6], rest[7]
    xh = place[3]
    half = own_y.shape[2]
    for side, own in enumerate((own_y, own_z)):
        cols = pl.ds(side * half, half)
        for n in range(2):
            for target, index in ((keep, 2 * n + xh), (give, 2 * n + 1 - xh)):
                value = own[index]
                for d in range(3):
                    value += arrivals[3 * side + d][index].astype(jnp.float32)
                target[n, :, cols] = value.astype(target.dtype)


def shape(dims, kind):
    return pltpu.VMEM(dims, kind)


def near(array):
    return pltpu.with_memory_space_constraint(array, pltpu.VMEM)


def local(inputs, input_weight, recurrent_weight, gate_bias, lengths, cotangent):
    total, rows, width = inputs.shape
    gated = 4 * width
    stages = lax.axis_size("pipe")
    stage = lax.axis_index("pipe")
    blocks = total // BLOCK
    ticks = blocks + stages - 1
    lens = near(jnp.broadcast_to(lengths[:, None], (rows, width)))
    cot, inputs, gate_bias = near(cotangent[0]), near(inputs), near(gate_bias)
    params = pltpu.CompilerParams(vmem_limit_bytes=LIMIT)
    bf16, f32 = jnp.bfloat16, jnp.float32

    flat, turned = shape((width, gated), bf16), shape((gated, width), bf16)
    kept_gates, kept_cells = shape((total, rows, gated), f32), shape((total + 1, rows, width), f32)
    kept_rows, one = shape((total, rows, gated), bf16), shape((rows, width), f32)
    state = (flat, flat, shape((total, rows, width), bf16), kept_gates, kept_cells)
    fine, half, late = width // 32, gated // 2, 6
    group = shape((4, 4, fine, total * rows), bf16)
    store, sent = shape((3, total, rows, half), bf16), shape((BLOCK, rows, half), bf16)
    block = shape((BLOCK, rows, width), bf16)
    far = pltpu.HBM((gated, width), bf16)
    state += (shape((total + 1, rows, width), bf16), far, far)
    arrived, gy, gz, dps, dh, dc, *held = pl.pallas_call(
        setup_kernel,
        out_shape=(block, store, store, kept_rows, one, one) + state,
        in_specs=[HBM] * 2,
        out_specs=(VMEM,) * 12 + (HBM,) * 2,
        scratch_shapes=[pltpu.SemaphoreType.DMA((2,))],
        compiler_params=params,
        name="setup",
    )(*(pltpu.with_memory_space_constraint(w[0], pltpu.HBM) for w in (input_weight, recurrent_weight)))
    def forward(tick):
        extra = (turned, turned) if tick == ticks - 1 else ()
        return pl.pallas_call(
            partial(forward_kernel, tick=tick, stages=stages),
            out_shape=(block,) + state + extra,
            in_specs=[SMEM] + [VMEM] * 10 + [HBM] * 2,
            out_specs=(VMEM,) * 7 + (HBM,) * 2 + (VMEM,) * len(extra),
            scratch_shapes=[
                pltpu.VMEM((BLOCK, rows, gated), f32),
                pltpu.VMEM((SLOTS, PANEL, width), bf16),
                pltpu.SemaphoreType.DMA((SLOTS,)),
                pltpu.SemaphoreType.DMA((2,)),
            ],
            input_output_aliases={5 + n: 1 + n for n in range(8)},
            compiler_params=params,
            name="forward_tick",
        )

    place = jnp.stack([stage] + [lax.axis_index(a) for a in ("y", "z", "xh")]).astype(jnp.int32)
    for tick in range(ticks):
        emitted, *held = forward(tick)(place, inputs, near(arrived), gate_bias, lens, *held)
        if tick < ticks - 1:
            on = [s for s in range(stages - 1) if 0 <= tick - s < blocks]
            arrived = lax.ppermute(emitted, "pipe", [(s, s + 1) for s in on])

    _, _, xs, gates, cells, hs, _, _, wit, wrt = held

    def backward(tick):
        n = late if tick >= 2 else 0
        return pl.pallas_call(
            partial(backward_kernel, tick=tick, stages=stages, late=n),
            out_shape=(block, sent, sent, store, store, kept_rows, kept_gates, kept_cells, turned, turned, one, one),
            in_specs=[SMEM] + [VMEM] * (12 + n),
            out_specs=(VMEM,) * 12,
            input_output_aliases={4 + n + i: 3 + i for i in range(9)},
            compiler_params=params,
            name="backward_tick",
        )

    def passed(blocks_y, blocks_z, on):
        out = []
        for axis, made in (("y", blocks_y), ("z", blocks_z)):
            for d in range(1, 4):
                route = [(i * stages + s, (i + d) % 4 * stages + s) for i in range(4) for s in on]
                out.append(near(lax.ppermute(made[d - 1], (axis, "pipe"), route)))
        return out

    final_hidden, final_cell = hs[total], cells[total]
    held = [gy, gz, dps, gates, cells, wit, wrt, dh, dc]
    arrived = emitted
    waiting = []
    for tick in range(ticks):
        extra = waiting[tick - 2] if tick >= 2 else []
        lower, send_y, send_z, *held = backward(tick)(place, cot, near(arrived), lens, *extra, *held)
        if tick == 0:
            xs, hs, lower = lax.optimization_barrier((xs, hs, lower))
            own_y, own_z, *spread = pl.pallas_call(
                prepare_kernel,
                out_shape=(group,) * 8,
                in_specs=[SMEM] + [VMEM] * 2,
                out_specs=(VMEM,) * 8,
                scratch_shapes=[pltpu.VMEM((4, 4, 4, fine, total * rows), bf16)],
                compiler_params=params,
                name="prepare",
            )(place, near(xs), near(hs))
        on = [s for s in range(stages) if 0 <= tick - (stages - 1 - s) < blocks]
        if tick < ticks - 1:
            arrived = lax.ppermute(lower, "pipe", [(s, s - 1) for s in on if s > 0])
        if tick == 0:
            lefts = passed(spread[:3], spread[3:], range(stages))
        waiting.append(passed([send_y] * 3, [send_z] * 3, on))
    gy, gz, dps = held[:3]
    part, whole = shape((4, fine, half), bf16), shape((4, fine, half), f32)
    _, _, bias_part, mine_y, mine_z, *sends = pl.pallas_call(
        partial(combine_kernel, stages=stages, ticks=ticks, late=late),
        out_shape=(store, store, shape((1, gated), f32), whole, whole) + (part,) * 6,
        in_specs=[SMEM] + [VMEM] * 23,
        out_specs=(VMEM,) * 11,
        scratch_shapes=[
            pltpu.VMEM((4, 4, fine, 4 * total * rows), bf16),
            pltpu.VMEM((4 * total * rows, half), bf16),
        ],
        input_output_aliases={22: 0, 23: 1},
        compiler_params=params,
        name="combine",
    )(place, own_y, *lefts[:3], own_z, *lefts[3:], dps, *waiting[-2], *waiting[-1], gy, gz)
    routes = [[(i, (i + d) % 4) for i in range(4)] for d in range(1, 4)]
    got = [near(lax.ppermute(sends[n], "z" if n < 3 else "y", routes[n % 3])) for n in range(6)]
    bias_all = lax.all_to_all(bias_part.reshape(32, 1, -1), DP, 0, 0, tiled=True)
    grad_bias = jnp.sum(bias_all, axis=(0, 1))
    keep, give = pl.pallas_call(
        finish_kernel,
        out_shape=(shape((2, fine, gated), f32), shape((2, fine, gated), bf16)),
        in_specs=[SMEM] + [VMEM] * 8,
        out_specs=(VMEM,) * 2,
        compiler_params=params,
        name="finish",
    )(place, mine_y, mine_z, *got)
    grads = keep + lax.ppermute(give, "xh", [(0, 1), (1, 0)]).astype(f32)
    return (grads[0][None], grads[1][None], grad_bias[None], final_hidden[None], final_cell[None])


def solution(mesh):
    fine = Mesh(mesh.devices.reshape(2, 4, 4, 4), ("xh", "y", "z", "pipe"))
    return jax.shard_map(
        local,
        mesh=fine,
        in_specs=(
            P(None, DP, None),
            P("pipe", None, None),
            P("pipe", None, None),
            P("pipe", None),
            P(DP),
            P("pipe", None, DP, None),
        ),
        out_specs=(
            P("pipe", DP, None),
            P("pipe", DP, None),
            P("pipe", DP),
            P("pipe", DP, None),
            P("pipe", DP, None),
        ),
        check_vma=False,
    )
```

```python
from functools import partial

import jax
import jax.numpy as jnp
from jax import lax
from jax.experimental import pallas as pl
from jax.experimental.pallas import tpu as pltpu
from jax.sharding import Mesh, PartitionSpec as P

BLOCK = 4
CHUNK = 256
PANEL = 256
SLOTS = 4
EXTRA = 16
DP = ("xh", "y", "z")
VMEM = pl.BlockSpec(memory_space=pltpu.VMEM)
SMEM = pl.BlockSpec(memory_space=pltpu.SMEM)
HBM = pl.BlockSpec(memory_space=pltpu.HBM)
LIMIT = 8 * 2**20


def squash(value):
    return 0.5 * jnp.tanh(0.5 * value) + 0.5


def dot(a, b):
    return jnp.dot(a, b, preferred_element_type=jnp.float32)


def setup_kernel(wi_far, wr_far, _a, _y, _z, _h, _c, wi, wr, *rest):
    sems = rest[-1]
    copies = [pltpu.make_async_copy(a, b, sems.at[n]) for n, (a, b) in enumerate(((wi_far, wi), (wr_far, wr)))]
    for c in copies:
        c.start()
    for c in copies:
        c.wait()


def turn(share, shares, pairs, stage, sems):
    panels = pairs[0][1].shape[0] // PANEL
    groups = panels // SLOTS
    low = share * 2 * groups // shares
    high = (share + 1) * 2 * groups // shares

    for n, (source, target) in enumerate(pairs):

        def body(group, carry, source=source, target=target):
            copies = []
            for slot in range(SLOTS):
                at = pl.multiple_of((group * SLOTS + slot) * PANEL, PANEL)
                stage[slot] = source[:, pl.ds(at, PANEL)].T
                copies.append(pltpu.make_async_copy(stage.at[slot], target.at[pl.ds(at, PANEL)], sems.at[slot]))
                copies[-1].start()
            for c in copies:
                c.wait()
            return carry

        begin, end = (jnp.clip(v - n * groups, 0, groups) for v in (low, high))
        lax.fori_loop(begin, end, body, 0)


def forward_kernel(place, own, arrived, bias, lens, *rest, tick, stages):
    emitted, wi, wr, xs, gates, cells, hs, wit_far, wrt_far = rest[8:17]
    proj, staged, sems, load_sems = rest[-4:]
    span, rows, width = arrived.shape
    stage = place[0]
    blocks = own.shape[0] // span
    at = tick - stage
    active = (at >= 0) & (at < blocks)
    fs = at * span
    last = tick == blocks + stages - 2
    pairs = ((wr, wrt_far), (wi, wit_far))
    loads = []
    if last:
        wit, wrt = rest[17:19]
        loads = [pltpu.make_async_copy(far, to, load_sems.at[n]) for n, (far, to) in enumerate(((wit_far, wit), (wrt_far, wrt)))]

    @pl.when(jnp.logical_not(active))
    def _():
        turn(jnp.where(at < 0, tick, tick - blocks), stages - 1, pairs, staged, sems)

    for c in loads:
        c.start()

    @pl.when(active)
    def _():
        @pl.when(stage == 0)
        def _():
            xs[pl.ds(fs, span)] = own[pl.ds(fs, span)]

        @pl.when(stage > 0)
        def _():
            xs[pl.ds(fs, span)] = arrived[...]

        x = xs[pl.ds(fs, span)].reshape(span * rows, width)
        proj[...] = (dot(x, wi[...]) + bias[...]).reshape(span, rows, 4 * width)

        @pl.when(fs == 0)
        def _():
            hs[0] = jnp.zeros((rows, width), jnp.bfloat16)
            cells[0] = jnp.zeros((rows, width), jnp.float32)

        def frame(t, carry):
            fr = fs + t
            h = hs[fr]
            for j in range(0, width, CHUNK):
                part = pl.ds(j, CHUNK)

                def pre(gate):
                    col = pl.ds(gate * width + j, CHUNK)
                    return proj[t, :, col] + dot(h, wr[:, col])

                alive = fr < lens[:, part]
                i, f, g, o = squash(pre(0)), squash(pre(1)), jnp.tanh(pre(2)), squash(pre(3))
                c = cells[fr, :, part]
                new_c = f * c + i * g
                new_h = (o * jnp.tanh(new_c)).astype(jnp.bfloat16)
                old_h = hs[fr, :, part]
                gates[fr, :, pl.ds(j, CHUNK)] = i
                gates[fr, :, pl.ds(width + j, CHUNK)] = f
                gates[fr, :, pl.ds(2 * width + j, CHUNK)] = g
                gates[fr, :, pl.ds(3 * width + j, CHUNK)] = o
                cells[fr + 1, :, part] = jnp.where(alive, new_c, c)
                hs[fr + 1, :, part] = jnp.where(alive, new_h, old_h)
                emitted[t, :, part] = jnp.where(alive, new_h, jnp.zeros_like(new_h))
            return carry

        lax.fori_loop(0, span, frame, 0)

    for c in loads:
        c.wait()


def block_at(tick, stage, stages, blocks):
    offset = tick - (stages - 1 - stage)
    return blocks - 1 - offset, (offset >= 0) & (offset < blocks)


def backward_kernel(place, cot, arrived, lens, *rest, tick, stages):
    lower, dy, dz, gates, cells, wit, wrt, dh, dc = rest[8:]
    span, rows, width = arrived.shape
    total = gates.shape[0]
    half = 2 * width
    stage = place[0]
    blocks = total // span
    at, active = block_at(tick, stage, stages, blocks)
    fs = at * span

    @pl.when(active)
    def _():
        @pl.when(fs + span == total)
        def _():
            dh[...] = jnp.zeros((rows, width), jnp.float32)
            dc[...] = jnp.zeros((rows, width), jnp.float32)

        def frame(n, carry):
            t = span - 1 - n
            fr = fs + t
            acc = None
            for j in range(0, width, CHUNK):
                part = pl.ds(j, CHUNK)
                alive = fr < lens[:, part]
                i = gates[fr, :, pl.ds(j, CHUNK)]
                f = gates[fr, :, pl.ds(width + j, CHUNK)]
                g = gates[fr, :, pl.ds(2 * width + j, CHUNK)]
                o = gates[fr, :, pl.ds(3 * width + j, CHUNK)]
                u = jnp.where(stage == stages - 1, 0.0, arrived[t, :, part].astype(jnp.float32))
                e = jnp.where(alive, dh[:, part] + u + cot[fr, :, part].astype(jnp.float32), 0.0)
                k = jnp.tanh(cells[fr + 1, :, part])
                old_dc = dc[:, part]
                dcell = jnp.where(alive, old_dc, 0.0) + e * o * (1.0 - k * k)
                parts = (
                    dcell * g * i * (1.0 - i),
                    dcell * cells[fr, :, part] * f * (1.0 - f),
                    dcell * i * (1.0 - g * g),
                    e * k * o * (1.0 - o),
                )
                dc[:, part] = jnp.where(alive, 0.0, old_dc) + dcell * f
                dh[:, part] = jnp.where(alive, 0.0, dh[:, part])
                for gate, value in enumerate(parts):
                    col = pl.ds(gate * width + j, CHUNK)
                    d = value.astype(jnp.bfloat16)
                    if gate < 2:
                        dy[fr, :, col] = d
                    else:
                        dz[fr, :, pl.ds(gate * width + j - half, CHUNK)] = d
                    term = dot(d, wrt[col, :])
                    acc = term if acc is None else acc + term
            dh[...] = dh[...] + acc
            return carry

        lax.fori_loop(0, span, frame, 0)

        @pl.when(stage > 0)
        def _():
            left, right = (v[pl.ds(fs, span)].reshape(span * rows, half) for v in (dy, dz))
            u = dot(left, wit[pl.ds(0, half), :]) + dot(right, wit[pl.ds(half, half), :])
            lower[...] = u.astype(jnp.bfloat16).reshape(span, rows, width)


def prepare_kernel(place, xs, hs, *rest):
    to_y, to_z, whole = rest[:4], rest[4:8], rest[8]
    total, rows, width = xs.shape
    y, z = place[1], place[2]
    for n, source in enumerate((xs, hs)):
        flat = source[pl.ds(0, total)].reshape(total * rows, width)
        whole[pl.ds(2 * n, 2)] = flat.T.reshape((2,) + whole.shape[1:])
    for d in range(4):
        for g in range(4):
            to_y[d][g] = whole[g, lax.rem(y + d, 4)]
            for i in range(4):
                to_z[d][g, i] = whole[g, i, lax.rem(z + d, 4)]


def as_rows(value):
    high = value.astype(jnp.bfloat16)
    rest = value - high.astype(jnp.float32)
    middle = rest.astype(jnp.bfloat16)
    low = (rest - middle.astype(jnp.float32)).astype(jnp.bfloat16)
    at = lax.broadcasted_iota(jnp.int32, (EXTRA, value.shape[1]), 0)
    out = jnp.zeros(at.shape, jnp.float32)
    for n, part in enumerate((high, middle, low)):
        out = jnp.where(at == n, part.astype(jnp.float32), out)
    return out.astype(jnp.bfloat16)


def from_rows(block):
    return jnp.sum(block.astype(jnp.float32), axis=0, keepdims=True)


def combine_kernel(place, *rest):
    lefts = (rest[:4], rest[4:8])
    dy, dz = rest[8:10]
    arrivals = (rest[10:13], rest[13:16])
    own_y, own_z, bias, *sends = rest[16:-2]
    left_all, right = rest[-2:]
    y, z = place[1], place[2]
    total, rows, half = dy.shape
    n = total * rows
    fine = left_all.shape[2]
    ones = jnp.ones((EXTRA, 4 * n), jnp.bfloat16)
    for side, (mine, other, own) in enumerate(((dy, z, own_y), (dz, y, own_z))):
        for d in range(4):
            block = mine if d == 0 else arrivals[side][d - 1]
            right[pl.ds(d * n, n)] = block[...].reshape(n, half)
            for g in range(4):
                left_all[g, :, :, pl.ds(d * n, n)] = lefts[side][d][g]
        sums = dot(ones, right[...])[:1]
        bias[:, pl.ds(side * half, half)] = sums
        extra = as_rows(sums)
        for d in range(4):
            left = left_all[:, lax.rem(other + d, 4)].reshape(4 * fine, 4 * n)
            part = dot(left, right[...])
            if d == 0:
                own[...] = part.reshape(4, fine, half)
            else:
                to = sends[3 * side + d - 1]
                to[pl.ds(0, 4 * fine)] = part.astype(jnp.bfloat16)
                to[pl.ds(4 * fine, EXTRA)] = extra


def finish_kernel(place, own_y, own_z, bias, *rest):
    arrivals, keep, kept_bias, give = rest[:6], rest[6], rest[7], rest[8]
    xh = place[3]
    fine, half = own_y.shape[1:]
    for side, own in enumerate((own_y, own_z)):
        cols = pl.ds(side * half, half)
        blocks = arrivals[3 * side : 3 * side + 3]
        for n in range(2):
            mine, other = 2 * n + xh, 2 * n + 1 - xh
            kept, given = own[mine], own[other]
            for block in blocks:
                kept += block[pl.ds(pl.multiple_of(mine * fine, fine), fine)].astype(jnp.float32)
                given += block[pl.ds(pl.multiple_of(other * fine, fine), fine)].astype(jnp.float32)
            keep[n, :, cols] = kept
            give[pl.ds(n * fine, fine), cols] = given.astype(jnp.bfloat16)
        total = bias[:, cols]
        for block in blocks:
            total += from_rows(block[pl.ds(4 * fine, EXTRA)])
        kept_bias[:, cols] = total
        give[pl.ds(2 * fine, EXTRA), cols] = as_rows(total)


def last_kernel(place, keep, bias, arrived, grad_i, grad_r, grad_b):
    fine = keep.shape[1]
    for n, out in enumerate((grad_i, grad_r)):
        out[...] = keep[n] + arrived[pl.ds(n * fine, fine)].astype(jnp.float32)
    width = grad_b.shape[1]
    cols = pl.ds(pl.multiple_of(((place[3] * 4 + place[1]) * 4 + place[2]) * width, width), width)
    grad_b[...] = bias[:, cols] + from_rows(arrived[pl.ds(2 * fine, EXTRA), cols])


def shape(dims, kind):
    return pltpu.VMEM(dims, kind)


def near(array):
    return pltpu.with_memory_space_constraint(array, pltpu.VMEM)


def local(inputs, input_weight, recurrent_weight, gate_bias, lengths, cotangent):
    total, rows, width = inputs.shape
    gated = 4 * width
    stages = lax.axis_size("pipe")
    stage = lax.axis_index("pipe")
    blocks = total // BLOCK
    ticks = blocks + stages - 1
    lens = near(jnp.broadcast_to(lengths[:, None], (rows, width)))
    cot, inputs, gate_bias = near(cotangent[0]), near(inputs), near(gate_bias)
    params = pltpu.CompilerParams(vmem_limit_bytes=LIMIT)
    bf16, f32 = jnp.bfloat16, jnp.float32

    flat, turned = shape((width, gated), bf16), shape((gated, width), bf16)
    kept_gates, kept_cells = shape((total, rows, gated), f32), shape((total + 1, rows, width), f32)
    one = shape((rows, width), f32)
    state = (flat, flat, shape((total, rows, width), bf16), kept_gates, kept_cells)
    fine, half = width // 32, gated // 2
    store = shape((total, rows, half), bf16)
    block = shape((BLOCK, rows, width), bf16)
    far = pltpu.HBM((gated, width), bf16)
    state += (shape((total + 1, rows, width), bf16), far, far)
    arrived, dy, dz, dh, dc, *held = pl.pallas_call(
        setup_kernel,
        out_shape=(block, store, store, one, one) + state,
        in_specs=[HBM] * 2,
        out_specs=(VMEM,) * 11 + (HBM,) * 2,
        scratch_shapes=[pltpu.SemaphoreType.DMA((2,))],
        compiler_params=params,
        name="setup",
    )(*(pltpu.with_memory_space_constraint(w[0], pltpu.HBM) for w in (input_weight, recurrent_weight)))
    def forward(tick):
        extra = (turned, turned) if tick == ticks - 1 else ()
        return pl.pallas_call(
            partial(forward_kernel, tick=tick, stages=stages),
            out_shape=(block,) + state + extra,
            in_specs=[SMEM] + [VMEM] * 10 + [HBM] * 2,
            out_specs=(VMEM,) * 7 + (HBM,) * 2 + (VMEM,) * len(extra),
            scratch_shapes=[
                pltpu.VMEM((BLOCK, rows, gated), f32),
                pltpu.VMEM((SLOTS, PANEL, width), bf16),
                pltpu.SemaphoreType.DMA((SLOTS,)),
                pltpu.SemaphoreType.DMA((2,)),
            ],
            input_output_aliases={5 + n: 1 + n for n in range(8)},
            compiler_params=params,
            name="forward_tick",
        )

    place = jnp.stack([stage] + [lax.axis_index(a) for a in ("y", "z", "xh")]).astype(jnp.int32)
    for tick in range(ticks):
        emitted, *held = forward(tick)(place, inputs, near(arrived), gate_bias, lens, *held)
        if tick < ticks - 1:
            on = [s for s in range(stages - 1) if 0 <= tick - s < blocks]
            arrived = lax.ppermute(emitted, "pipe", [(s, s + 1) for s in on])

    _, _, xs, gates, cells, hs, _, _, wit, wrt = held

    def backward(tick):
        return pl.pallas_call(
            partial(backward_kernel, tick=tick, stages=stages),
            out_shape=(block, store, store, kept_gates, kept_cells, turned, turned, one, one),
            in_specs=[SMEM] + [VMEM] * 11,
            out_specs=(VMEM,) * 9,
            input_output_aliases={4 + i: 1 + i for i in range(8)},
            compiler_params=params,
            name="backward_tick",
        )

    def simple(kernel, name, outs, count, scratch=()):
        return pl.pallas_call(
            kernel,
            out_shape=outs,
            in_specs=[SMEM] + [VMEM] * count,
            out_specs=jax.tree.map(lambda _: VMEM, outs),
            scratch_shapes=scratch,
            compiler_params=params,
            name=name,
        )

    final_hidden, final_cell = hs[total], cells[total]
    held = [dy, dz, gates, cells, wit, wrt, dh, dc]
    arrived = emitted
    routes = [[(i, (i + d) % 4) for i in range(4)] for d in range(1, 4)]

    def passed(made):
        return [near(lax.ppermute(made[n], "y" if n < 3 else "z", routes[n % 3])) for n in range(6)]

    group = shape((4, 4, fine, total * rows), bf16)
    lefts = []
    for tick in range(ticks):
        lower, *held = backward(tick)(place, cot, near(arrived), lens, *held)
        if tick == 0:
            xs, hs, lower = lax.optimization_barrier((xs, hs, lower))
            spread = simple(prepare_kernel, "prepare", (group,) * 8, 2, [pltpu.VMEM((4, 4, 4, fine, total * rows), bf16)])(
                place, near(xs), near(hs)
            )
        if tick < ticks - 1:
            on = [s for s in range(1, stages) if 0 <= tick - (stages - 1 - s) < blocks]
            arrived = lax.ppermute(lower, "pipe", [(s, s - 1) for s in on])
            if 1 <= tick <= 3:
                pair = lax.optimization_barrier((spread[tick], spread[4 + tick], lower))[:2]
                pair = [lax.ppermute(v, axis, routes[tick - 1]) for v, axis in zip(pair, ("y", "z"))]
                arrived, *pair = lax.optimization_barrier((arrived, *pair))
                lefts.append([near(v) for v in pair])
    dy, dz = held[:2]
    part, whole = shape((4 * fine + EXTRA, half), bf16), shape((4, fine, half), f32)
    mine_y, mine_z, bias, *sends = simple(
        combine_kernel,
        "combine",
        (whole, whole, shape((1, gated), f32)) + (part,) * 6,
        16,
        [pltpu.VMEM((4, 4, fine, 4 * total * rows), bf16), pltpu.VMEM((4 * total * rows, half), bf16)],
    )(place, spread[0], *(v for v, _ in lefts), spread[4], *(v for _, v in lefts), dy, dz, *passed([dy] * 3 + [dz] * 3))
    got = passed(sends[3:] + sends[:3])
    keep, bias, give = simple(
        finish_kernel,
        "finish",
        (shape((2, fine, gated), f32), shape((1, gated), f32), shape((2 * fine + EXTRA, gated), bf16)),
        9,
    )(place, mine_y, mine_z, bias, *got[3:], *got[:3])
    other = near(lax.ppermute(give, "xh", [(0, 1), (1, 0)]))
    made = jax.ShapeDtypeStruct
    grad_i, grad_r, grad_b = simple(
        last_kernel,
        "last",
        (made((fine, gated), f32), made((fine, gated), f32), made((1, gated // 32), f32)),
        3,
    )(place, keep, bias, other)
    return (grad_i[None], grad_r[None], grad_b, final_hidden[None], final_cell[None])


def solution(mesh):
    fine = Mesh(mesh.devices.reshape(2, 4, 4, 4), ("xh", "y", "z", "pipe"))
    return jax.shard_map(
        local,
        mesh=fine,
        in_specs=(
            P(None, DP, None),
            P("pipe", None, None),
            P("pipe", None, None),
            P("pipe", None),
            P(DP),
            P("pipe", None, DP, None),
        ),
        out_specs=(
            P("pipe", DP, None),
            P("pipe", DP, None),
            P("pipe", DP),
            P("pipe", DP, None),
            P("pipe", DP, None),
        ),
        check_vma=False,
    )
```

```python
from functools import partial

import jax
import jax.numpy as jnp
from jax import lax
from jax.experimental import pallas as pl
from jax.experimental.pallas import tpu as pltpu
from jax.sharding import Mesh, PartitionSpec as P

BLOCK = 8
CHUNK = 256
PANEL = 256
SLOTS = 4
EXTRA = 16
DP = ("xh", "y", "z")
VMEM = pl.BlockSpec(memory_space=pltpu.VMEM)
SMEM = pl.BlockSpec(memory_space=pltpu.SMEM)
HBM = pl.BlockSpec(memory_space=pltpu.HBM)
LIMIT = 8 * 2**20


def squash(value):
    return 0.5 * jnp.tanh(0.5 * value) + 0.5


def dot(a, b):
    return jnp.dot(a, b, preferred_element_type=jnp.float32)


def turn(share, shares, pairs, stage, sems):
    panels = pairs[0][1].shape[0] // PANEL
    groups = panels // SLOTS
    low = share * 2 * groups // shares
    high = (share + 1) * 2 * groups // shares

    for n, (source, target) in enumerate(pairs):

        def copy(at, slot, target=target):
            at = pl.multiple_of(at * PANEL, PANEL)
            return pltpu.make_async_copy(stage.at[slot], target.at[pl.ds(at, PANEL)], sems.at[slot])

        def body(group, carry, source=source, copy=copy):
            def move(slot, carry):
                at = group * SLOTS + slot
                stage[slot] = source[:, pl.ds(pl.multiple_of(at * PANEL, PANEL), PANEL)].T
                copy(at, slot).start()
                return carry

            def settle(slot, carry):
                copy(group * SLOTS + slot, slot).wait()
                return carry

            lax.fori_loop(0, SLOTS, move, 0)
            lax.fori_loop(0, SLOTS, settle, 0)
            return carry

        begin, end = (jnp.clip(v - n * groups, 0, groups) for v in (low, high))
        lax.fori_loop(begin, end, body, 0)


def forward_kernel(place, own, bias, lens, *rest, tick, stages):
    if tick == 0:
        (wi_in, wr_in), rest = rest[:2], rest[2:]
    else:
        arrived, rest = rest[0], rest[9:]
    emitted, wi, wr, xs, gates, cells, hs, wit_far, wrt_far = rest[:9]
    proj, staged, sems, load_sems = rest[-4:]
    span, rows, width = emitted.shape
    stage = place[0]
    blocks = own.shape[0] // span
    at = tick - stage
    active = (at >= 0) & (at < blocks)
    fs = at * span
    last = tick == blocks + stages - 2
    pairs = ((wr, wrt_far), (wi, wit_far))
    if tick == 0:
        load_wi = pltpu.make_async_copy(wi_in, wi, load_sems.at[0])
        load_wr = pltpu.make_async_copy(wr_in, wr, load_sems.at[1])
        load_wi.start()
        load_wr.start()
        load_wi.wait()

    @pl.when(active)
    def _():
        if tick == 0:
            xs[pl.ds(fs, span)] = own[pl.ds(fs, span)]
        else:

            @pl.when(stage == 0)
            def _():
                xs[pl.ds(fs, span)] = own[pl.ds(fs, span)]

            @pl.when(stage > 0)
            def _():
                xs[pl.ds(fs, span)] = arrived[...]

        x = xs[pl.ds(fs, span)].reshape(span * rows, width)
        proj[...] = (dot(x, wi[...]) + bias[...]).reshape(span, rows, 4 * width)

    if tick == 0:
        load_wr.wait()

    @pl.when(jnp.logical_not(active))
    def _():
        turn(jnp.where(at < 0, tick, tick - blocks), stages - 1, pairs, staged, sems)

    if last:
        load = pltpu.make_async_copy(wrt_far, rest[9], load_sems.at[0])
        load.start()

    @pl.when(active)
    def _():
        @pl.when(fs == 0)
        def _():
            hs[0] = jnp.zeros((rows, width), jnp.bfloat16)
            cells[0] = jnp.zeros((rows, width), jnp.float32)

        def frame(t, carry):
            fr = fs + t
            h = hs[fr]
            for j in range(0, width, CHUNK):
                part = pl.ds(j, CHUNK)

                def pre(gate):
                    col = pl.ds(gate * width + j, CHUNK)
                    return proj[t, :, col] + dot(h, wr[:, col])

                alive = fr < lens[:, part]
                i, f, g, o = squash(pre(0)), squash(pre(1)), jnp.tanh(pre(2)), squash(pre(3))
                c = cells[fr, :, part]
                new_c = f * c + i * g
                new_h = (o * jnp.tanh(new_c)).astype(jnp.bfloat16)
                old_h = hs[fr, :, part]
                gates[fr, :, pl.ds(j, CHUNK)] = i
                gates[fr, :, pl.ds(width + j, CHUNK)] = f
                gates[fr, :, pl.ds(2 * width + j, CHUNK)] = g
                gates[fr, :, pl.ds(3 * width + j, CHUNK)] = o
                cells[fr + 1, :, part] = jnp.where(alive, new_c, c)
                hs[fr + 1, :, part] = jnp.where(alive, new_h, old_h)
                emitted[t, :, part] = jnp.where(alive, new_h, jnp.zeros_like(new_h))
            return carry

        lax.fori_loop(0, span, frame, 0)

    if last:
        load.wait()


def block_at(tick, stage, stages, blocks):
    offset = tick - (stages - 1 - stage)
    return blocks - 1 - offset, (offset >= 0) & (offset < blocks)


def backward_kernel(place, cot, arrived, lens, *rest, tick, stages):
    if tick == 0:
        wit_far, gates_in, cells_in, wrt_in, lower, dy, dz, gates, cells, wit, wrt, dh, dc, sem = rest
        load = pltpu.make_async_copy(wit_far, wit, sem.at[0])
        load.start()
    else:
        lower, dy, dz, gates, cells, wit, wrt, dh, dc = rest[8:]
    span, rows, width = arrived.shape
    total = gates.shape[0]
    half = 2 * width
    stage = place[0]
    blocks = total // span
    at, active = block_at(tick, stage, stages, blocks)
    fs = at * span

    @pl.when(active)
    def _():
        @pl.when(fs + span == total)
        def _():
            dh[...] = jnp.zeros((rows, width), jnp.float32)
            dc[...] = jnp.zeros((rows, width), jnp.float32)

        def frame(n, carry):
            t = span - 1 - n
            fr = fs + t
            acc = None
            for j in range(0, width, CHUNK):
                part = pl.ds(j, CHUNK)
                alive = fr < lens[:, part]
                i = gates[fr, :, pl.ds(j, CHUNK)]
                f = gates[fr, :, pl.ds(width + j, CHUNK)]
                g = gates[fr, :, pl.ds(2 * width + j, CHUNK)]
                o = gates[fr, :, pl.ds(3 * width + j, CHUNK)]
                u = jnp.where(stage == stages - 1, 0.0, arrived[t, :, part].astype(jnp.float32))
                e = jnp.where(alive, dh[:, part] + u + cot[fr, :, part].astype(jnp.float32), 0.0)
                k = jnp.tanh(cells[fr + 1, :, part])
                old_dc = dc[:, part]
                dcell = jnp.where(alive, old_dc, 0.0) + e * o * (1.0 - k * k)
                parts = (
                    dcell * g * i * (1.0 - i),
                    dcell * cells[fr, :, part] * f * (1.0 - f),
                    dcell * i * (1.0 - g * g),
                    e * k * o * (1.0 - o),
                )
                dc[:, part] = jnp.where(alive, 0.0, old_dc) + dcell * f
                dh[:, part] = jnp.where(alive, 0.0, dh[:, part])
                for gate, value in enumerate(parts):
                    col = pl.ds(gate * width + j, CHUNK)
                    d = value.astype(jnp.bfloat16)
                    if gate < 2:
                        dy[fr, :, col] = d
                    else:
                        dz[fr, :, pl.ds(gate * width + j - half, CHUNK)] = d
                    term = dot(d, wrt[col, :])
                    acc = term if acc is None else acc + term
            dh[...] = dh[...] + acc
            return carry

        lax.fori_loop(0, span, frame, 0)

    if tick == 0:
        load.wait()
    if tick < blocks + stages - 2:

        @pl.when(active & (stage > 0))
        def _():
            left, right = (v[pl.ds(fs, span)].reshape(span * rows, half) for v in (dy, dz))
            u = dot(left, wit[pl.ds(0, half), :]) + dot(right, wit[pl.ds(half, half), :])
            lower[...] = u.astype(jnp.bfloat16).reshape(span, rows, width)


def prepare_kernel(place, xs, hs, *rest):
    to_y, to_z, whole = rest[:4], rest[4:8], rest[8]
    total, rows, width = xs.shape
    y, z = place[1], place[2]
    for n, source in enumerate((xs, hs)):
        flat = source[pl.ds(0, total)].reshape(total * rows, width)
        whole[pl.ds(2 * n, 2)] = flat.T.reshape((2,) + whole.shape[1:])
    for d in range(4):
        for g in range(4):
            to_y[d][g] = whole[g, lax.rem(y + d, 4)]
            for i in range(4):
                to_z[d][g, i] = whole[g, i, lax.rem(z + d, 4)]


def as_rows(value):
    high = value.astype(jnp.bfloat16)
    rest = value - high.astype(jnp.float32)
    middle = rest.astype(jnp.bfloat16)
    low = (rest - middle.astype(jnp.float32)).astype(jnp.bfloat16)
    at = lax.broadcasted_iota(jnp.int32, (EXTRA, value.shape[1]), 0)
    out = jnp.zeros(at.shape, jnp.float32)
    for n, part in enumerate((high, middle, low)):
        out = jnp.where(at == n, part.astype(jnp.float32), out)
    return out.astype(jnp.bfloat16)


def from_rows(block):
    return jnp.sum(block.astype(jnp.float32), axis=0, keepdims=True)


def combine_kernel(place, *rest):
    lefts = (rest[:4], rest[4:8])
    dy, dz = rest[8:10]
    arrivals = (rest[10:13], rest[13:16])
    own_y, own_z, bias, *sends = rest[16:-2]
    left_all, right = rest[-2:]
    y, z = place[1], place[2]
    total, rows, half = dy.shape
    n = total * rows
    fine = left_all.shape[2]
    ones = jnp.ones((EXTRA, 4 * n), jnp.bfloat16)
    for side, (mine, other, own) in enumerate(((dy, z, own_y), (dz, y, own_z))):
        for d in range(4):
            block = mine if d == 0 else arrivals[side][d - 1]
            right[pl.ds(d * n, n)] = block[...].reshape(n, half)
            for g in range(4):
                left_all[g, :, :, pl.ds(d * n, n)] = lefts[side][d][g]
        sums = dot(ones, right[...])[:1]
        bias[:, pl.ds(side * half, half)] = sums
        extra = as_rows(sums)
        for d in range(4):
            left = left_all[:, lax.rem(other + d, 4)].reshape(4 * fine, 4 * n)
            part = dot(left, right[...])
            if d == 0:
                own[...] = part.reshape(4, fine, half)
            else:
                to = sends[3 * side + d - 1]
                to[pl.ds(0, 4 * fine)] = part.astype(jnp.bfloat16)
                to[pl.ds(4 * fine, EXTRA)] = extra


def finish_kernel(place, own_y, own_z, bias, *rest):
    arrivals, keep, kept_bias, give = rest[:6], rest[6], rest[7], rest[8]
    xh = place[3]
    fine, half = own_y.shape[1:]
    for side, own in enumerate((own_y, own_z)):
        cols = pl.ds(side * half, half)
        blocks = arrivals[3 * side : 3 * side + 3]
        for n in range(2):
            mine, other = 2 * n + xh, 2 * n + 1 - xh
            kept, given = own[mine], own[other]
            for block in blocks:
                kept += block[pl.ds(pl.multiple_of(mine * fine, fine), fine)].astype(jnp.float32)
                given += block[pl.ds(pl.multiple_of(other * fine, fine), fine)].astype(jnp.float32)
            keep[n, :, cols] = kept
            give[pl.ds(n * fine, fine), cols] = given.astype(jnp.bfloat16)
        total = bias[:, cols]
        for block in blocks:
            total += from_rows(block[pl.ds(4 * fine, EXTRA)])
        kept_bias[:, cols] = total
        give[pl.ds(2 * fine, EXTRA), cols] = as_rows(total)


def last_kernel(place, keep, bias, arrived, grad_i, grad_r, grad_b):
    fine = keep.shape[1]
    for n, out in enumerate((grad_i, grad_r)):
        out[...] = keep[n] + arrived[pl.ds(n * fine, fine)].astype(jnp.float32)
    width = grad_b.shape[1]
    cols = pl.ds(pl.multiple_of(((place[3] * 4 + place[1]) * 4 + place[2]) * width, width), width)
    grad_b[...] = bias[:, cols] + from_rows(arrived[pl.ds(2 * fine, EXTRA), cols])


def shape(dims, kind):
    return pltpu.VMEM(dims, kind)


def near(array):
    return pltpu.with_memory_space_constraint(array, pltpu.VMEM)


def local(inputs, input_weight, recurrent_weight, gate_bias, lengths, cotangent):
    total, rows, width = inputs.shape
    gated = 4 * width
    stages = lax.axis_size("pipe")
    stage = lax.axis_index("pipe")
    blocks = total // BLOCK
    ticks = blocks + stages - 1
    lens = near(jnp.broadcast_to(lengths[:, None], (rows, width)))
    cot, inputs, gate_bias = near(cotangent[0]), near(inputs), near(gate_bias)
    params = pltpu.CompilerParams(vmem_limit_bytes=LIMIT)
    bf16, f32 = jnp.bfloat16, jnp.float32

    flat, turned = shape((width, gated), bf16), shape((gated, width), bf16)
    kept_gates, kept_cells = shape((total, rows, gated), f32), shape((total + 1, rows, width), f32)
    one = shape((rows, width), f32)
    state = (flat, flat, shape((total, rows, width), bf16), kept_gates, kept_cells)
    fine, half = width // 32, gated // 2
    store = shape((total, rows, half), bf16)
    block = shape((BLOCK, rows, width), bf16)
    far = pltpu.HBM((gated, width), bf16)
    state += (shape((total + 1, rows, width), bf16), far, far)
    def forward(tick):
        first = tick == 0
        extra = (turned,) if tick == ticks - 1 else ()
        return pl.pallas_call(
            partial(forward_kernel, tick=tick, stages=stages),
            out_shape=(block,) + state + extra,
            in_specs=[SMEM] + [VMEM] * 3 + ([HBM] * 2 if first else [VMEM] * 7 + [HBM] * 2),
            out_specs=(VMEM,) * 7 + (HBM,) * 2 + (VMEM,) * len(extra),
            scratch_shapes=[
                pltpu.VMEM((BLOCK, rows, gated), f32),
                pltpu.VMEM((SLOTS, PANEL, width), bf16),
                pltpu.SemaphoreType.DMA((SLOTS,)),
                pltpu.SemaphoreType.DMA((2,)),
            ],
            input_output_aliases={} if first else {5 + n: 1 + n for n in range(8)},
            compiler_params=params,
            name="forward_tick",
        )

    place = jnp.stack([stage] + [lax.axis_index(a) for a in ("y", "z", "xh")]).astype(jnp.int32)
    for tick in range(ticks):
        got = [near(arrived), *held] if tick else [pltpu.with_memory_space_constraint(w[0], pltpu.HBM) for w in (input_weight, recurrent_weight)]
        emitted, *held = forward(tick)(place, inputs, gate_bias, lens, *got)
        if tick < ticks - 1:
            on = [s for s in range(stages - 1) if 0 <= tick - s < blocks]
            arrived = lax.ppermute(emitted, "pipe", [(s, s + 1) for s in on])

    _, _, xs, gates, cells, hs, wit_far, _, wrt = held

    def backward(tick):
        first = tick == 0
        aliases = {5: 3, 6: 4, 7: 6} if first else {4 + i: 1 + i for i in range(8)}
        return pl.pallas_call(
            partial(backward_kernel, tick=tick, stages=stages),
            out_shape=(block, store, store, kept_gates, kept_cells, turned, turned, one, one),
            in_specs=[SMEM] + [VMEM] * 3 + ([HBM] + [VMEM] * 3 if first else [VMEM] * 8),
            out_specs=(VMEM,) * 9,
            scratch_shapes=[pltpu.SemaphoreType.DMA((1,))] if first else [],
            input_output_aliases=aliases,
            compiler_params=params,
            name="backward_tick",
        )

    def simple(kernel, name, outs, count, scratch=()):
        return pl.pallas_call(
            kernel,
            out_shape=outs,
            in_specs=[SMEM] + [VMEM] * count,
            out_specs=jax.tree.map(lambda _: VMEM, outs),
            scratch_shapes=scratch,
            compiler_params=params,
            name=name,
        )

    final_hidden, final_cell = hs[total], cells[total]
    held = [pltpu.with_memory_space_constraint(wit_far, pltpu.HBM), gates, cells, wrt]
    arrived = emitted
    routes = [[(i, (i + d) % 4) for i in range(4)] for d in range(1, 4)]

    def passed(made):
        return [near(lax.ppermute(made[n], "y" if n < 3 else "z", routes[n % 3])) for n in range(6)]

    group = shape((4, 4, fine, total * rows), bf16)
    lefts = []
    for tick in range(ticks):
        lower, *held = backward(tick)(place, cot, near(arrived), lens, *held)
        if tick == 0:
            xs, hs, lower = lax.optimization_barrier((xs, hs, lower))
            spread = simple(prepare_kernel, "prepare", (group,) * 8, 2, [pltpu.VMEM((4, 4, 4, fine, total * rows), bf16)])(
                place, near(xs), near(hs)
            )
        if tick < ticks - 1:
            on = [s for s in range(1, stages) if 0 <= tick - (stages - 1 - s) < blocks]
            arrived = lax.ppermute(lower, "pipe", [(s, s - 1) for s in on])
            if 1 <= tick <= 3:
                pair = lax.optimization_barrier((spread[tick], spread[4 + tick], lower))[:2]
                pair = [lax.ppermute(v, axis, routes[tick - 1]) for v, axis in zip(pair, ("y", "z"))]
                arrived, *pair = lax.optimization_barrier((arrived, *pair))
                lefts.append([near(v) for v in pair])
    dy, dz = held[:2]
    part, whole = shape((4 * fine + EXTRA, half), bf16), shape((4, fine, half), f32)
    mine_y, mine_z, bias, *sends = simple(
        combine_kernel,
        "combine",
        (whole, whole, shape((1, gated), f32)) + (part,) * 6,
        16,
        [pltpu.VMEM((4, 4, fine, 4 * total * rows), bf16), pltpu.VMEM((4 * total * rows, half), bf16)],
    )(place, spread[0], *(v for v, _ in lefts), spread[4], *(v for _, v in lefts), dy, dz, *passed([dy] * 3 + [dz] * 3))
    got = passed(sends[3:] + sends[:3])
    keep, bias, give = simple(
        finish_kernel,
        "finish",
        (shape((2, fine, gated), f32), shape((1, gated), f32), shape((2 * fine + EXTRA, gated), bf16)),
        9,
    )(place, mine_y, mine_z, bias, *got[3:], *got[:3])
    other = near(lax.ppermute(give, "xh", [(0, 1), (1, 0)]))
    made = jax.ShapeDtypeStruct
    grad_i, grad_r, grad_b = simple(
        last_kernel,
        "last",
        (made((fine, gated), f32), made((fine, gated), f32), made((1, gated // 32), f32)),
        3,
    )(place, keep, bias, other)
    return (grad_i[None], grad_r[None], grad_b, final_hidden[None], final_cell[None])


def solution(mesh):
    fine = Mesh(mesh.devices.reshape(2, 4, 4, 4), ("xh", "y", "z", "pipe"))
    return jax.shard_map(
        local,
        mesh=fine,
        in_specs=(
            P(None, DP, None),
            P("pipe", None, None),
            P("pipe", None, None),
            P("pipe", None),
            P(DP),
            P("pipe", None, DP, None),
        ),
        out_specs=(
            P("pipe", DP, None),
            P("pipe", DP, None),
            P("pipe", DP),
            P("pipe", DP, None),
            P("pipe", DP, None),
        ),
        check_vma=False,
    )
```

```python
from functools import partial

import jax
import jax.numpy as jnp
from jax import lax
from jax.experimental import pallas as pl
from jax.experimental.pallas import tpu as pltpu
from jax.sharding import Mesh, PartitionSpec as P

BLOCK = 4
CHUNK = 256
PANEL = 256
SLOTS = 4
EXTRA = 16
DP = ("xh", "y", "z")
VMEM = pl.BlockSpec(memory_space=pltpu.VMEM)
SMEM = pl.BlockSpec(memory_space=pltpu.SMEM)
HBM = pl.BlockSpec(memory_space=pltpu.HBM)
LIMIT = 8 * 2**20


def squash(value):
    return 0.5 * jnp.tanh(0.5 * value) + 0.5


def dot(a, b):
    return jnp.dot(a, b, preferred_element_type=jnp.float32)


def turn(share, shares, pairs, stage, sems):
    panels = pairs[0][1].shape[0] // PANEL
    groups = panels // SLOTS
    low = share * 2 * groups // shares
    high = (share + 1) * 2 * groups // shares

    for n, (source, target) in enumerate(pairs):

        def copy(at, slot, target=target):
            at = pl.multiple_of(at * PANEL, PANEL)
            return pltpu.make_async_copy(stage.at[slot], target.at[pl.ds(at, PANEL)], sems.at[slot])

        def body(group, carry, source=source, copy=copy):
            def move(slot, carry):
                at = group * SLOTS + slot
                stage[slot] = source[:, pl.ds(pl.multiple_of(at * PANEL, PANEL), PANEL)].T
                copy(at, slot).start()
                return carry

            def settle(slot, carry):
                copy(group * SLOTS + slot, slot).wait()
                return carry

            lax.fori_loop(0, SLOTS, move, 0)
            lax.fori_loop(0, SLOTS, settle, 0)
            return carry

        begin, end = (jnp.clip(v - n * groups, 0, groups) for v in (low, high))
        lax.fori_loop(begin, end, body, 0)


def forward_kernel(place, own, bias, lens, *rest, tick, stages):
    if tick == 0:
        (wi_in, wr_in), rest = rest[:2], rest[2:]
    else:
        arrived, rest = rest[0], rest[9:]
    emitted, wi, wr, xs, gates, cells, hs, wit_far, wrt_far = rest[:9]
    proj, staged, sems, load_sems = rest[-4:]
    span, rows, width = emitted.shape
    stage = place[0]
    blocks = own.shape[0] // span
    at = tick - stage
    active = (at >= 0) & (at < blocks)
    fs = at * span
    last = tick == blocks + stages - 2
    pairs = ((wr, wrt_far), (wi, wit_far))
    if tick == 0:
        load_wi = pltpu.make_async_copy(wi_in, wi, load_sems.at[0])
        load_wr = pltpu.make_async_copy(wr_in, wr, load_sems.at[1])
        load_wi.start()
        load_wr.start()
        load_wi.wait()

    @pl.when(active)
    def _():
        if tick == 0:
            xs[pl.ds(fs, span)] = own[pl.ds(fs, span)]
        else:

            @pl.when(stage == 0)
            def _():
                xs[pl.ds(fs, span)] = own[pl.ds(fs, span)]

            @pl.when(stage > 0)
            def _():
                xs[pl.ds(fs, span)] = arrived[...]

        x = xs[pl.ds(fs, span)].reshape(span * rows, width)
        proj[...] = (dot(x, wi[...]) + bias[...]).reshape(span, rows, 4 * width)

    if tick == 0:
        load_wr.wait()

    @pl.when(jnp.logical_not(active))
    def _():
        turn(jnp.where(at < 0, tick, tick - blocks), stages - 1, pairs, staged, sems)

    if last:
        load = pltpu.make_async_copy(wrt_far, rest[9], load_sems.at[0])
        load.start()

    @pl.when(active)
    def _():
        @pl.when(fs == 0)
        def _():
            hs[0] = jnp.zeros((rows, width), jnp.bfloat16)
            cells[0] = jnp.zeros((rows, width), jnp.float32)

        def frame(t, carry):
            fr = fs + t
            h = hs[fr]
            for j in range(0, width, CHUNK):
                part = pl.ds(j, CHUNK)

                def pre(gate):
                    col = pl.ds(gate * width + j, CHUNK)
                    return proj[t, :, col] + dot(h, wr[:, col])

                alive = fr < lens[:, part]
                i, f, g, o = squash(pre(0)), squash(pre(1)), jnp.tanh(pre(2)), squash(pre(3))
                c = cells[fr, :, part]
                new_c = f * c + i * g
                new_h = (o * jnp.tanh(new_c)).astype(jnp.bfloat16)
                old_h = hs[fr, :, part]
                gates[fr, :, pl.ds(j, CHUNK)] = i
                gates[fr, :, pl.ds(width + j, CHUNK)] = f
                gates[fr, :, pl.ds(2 * width + j, CHUNK)] = g
                gates[fr, :, pl.ds(3 * width + j, CHUNK)] = o
                cells[fr + 1, :, part] = jnp.where(alive, new_c, c)
                hs[fr + 1, :, part] = jnp.where(alive, new_h, old_h)
                emitted[t, :, part] = jnp.where(alive, new_h, jnp.zeros_like(new_h))
            return carry

        lax.fori_loop(0, span, frame, 0)

    if last:
        load.wait()


def block_at(tick, stage, stages, blocks):
    offset = tick - (stages - 1 - stage)
    return blocks - 1 - offset, (offset >= 0) & (offset < blocks)


def backward_kernel(place, cot, arrived, lens, *rest, tick, stages):
    if tick == 0:
        wit_far, gates_in, cells_in, wrt_in, lower, dy, dz, gates, cells, wit, wrt, dh, dc, sem = rest
        load = pltpu.make_async_copy(wit_far, wit, sem.at[0])
        load.start()
    else:
        lower, dy, dz, gates, cells, wit, wrt, dh, dc = rest[8:]
    span, rows, width = arrived.shape
    total = gates.shape[0]
    half = 2 * width
    stage = place[0]
    blocks = total // span
    at, active = block_at(tick, stage, stages, blocks)
    fs = at * span

    @pl.when(active)
    def _():
        @pl.when(fs + span == total)
        def _():
            dh[...] = jnp.zeros((rows, width), jnp.float32)
            dc[...] = jnp.zeros((rows, width), jnp.float32)

        def frame(n, carry):
            t = span - 1 - n
            fr = fs + t
            acc = None
            for j in range(0, width, CHUNK):
                part = pl.ds(j, CHUNK)
                alive = fr < lens[:, part]
                i = gates[fr, :, pl.ds(j, CHUNK)]
                f = gates[fr, :, pl.ds(width + j, CHUNK)]
                g = gates[fr, :, pl.ds(2 * width + j, CHUNK)]
                o = gates[fr, :, pl.ds(3 * width + j, CHUNK)]
                u = jnp.where(stage == stages - 1, 0.0, arrived[t, :, part].astype(jnp.float32))
                e = jnp.where(alive, dh[:, part] + u + cot[fr, :, part].astype(jnp.float32), 0.0)
                k = jnp.tanh(cells[fr + 1, :, part])
                old_dc = dc[:, part]
                dcell = jnp.where(alive, old_dc, 0.0) + e * o * (1.0 - k * k)
                parts = (
                    dcell * g * i * (1.0 - i),
                    dcell * cells[fr, :, part] * f * (1.0 - f),
                    dcell * i * (1.0 - g * g),
                    e * k * o * (1.0 - o),
                )
                dc[:, part] = jnp.where(alive, 0.0, old_dc) + dcell * f
                dh[:, part] = jnp.where(alive, 0.0, dh[:, part])
                for gate, value in enumerate(parts):
                    col = pl.ds(gate * width + j, CHUNK)
                    d = value.astype(jnp.bfloat16)
                    if gate < 2:
                        dy[fr, :, col] = d
                    else:
                        dz[fr, :, pl.ds(gate * width + j - half, CHUNK)] = d
                    term = dot(d, wrt[col, :])
                    acc = term if acc is None else acc + term
            dh[...] = dh[...] + acc
            return carry

        lax.fori_loop(0, span, frame, 0)

    if tick == 0:
        load.wait()
    if tick < blocks + stages - 2:

        @pl.when(active & (stage > 0))
        def _():
            left, right = (v[pl.ds(fs, span)].reshape(span * rows, half) for v in (dy, dz))
            u = dot(left, wit[pl.ds(0, half), :]) + dot(right, wit[pl.ds(half, half), :])
            lower[...] = u.astype(jnp.bfloat16).reshape(span, rows, width)


def prepare_kernel(place, xs, hs, *rest):
    to_y, to_z, whole = rest[:4], rest[4:8], rest[8]
    total, rows, width = xs.shape
    y, z = place[1], place[2]
    for n, source in enumerate((xs, hs)):
        flat = source[pl.ds(0, total)].reshape(total * rows, width)
        whole[pl.ds(2 * n, 2)] = flat.T.reshape((2,) + whole.shape[1:])
    for d in range(4):
        for g in range(4):
            to_y[d][g] = whole[g, lax.rem(y + d, 4)]
            for i in range(4):
                to_z[d][g, i] = whole[g, i, lax.rem(z + d, 4)]


def as_rows(value):
    high = value.astype(jnp.bfloat16)
    rest = value - high.astype(jnp.float32)
    middle = rest.astype(jnp.bfloat16)
    low = (rest - middle.astype(jnp.float32)).astype(jnp.bfloat16)
    at = lax.broadcasted_iota(jnp.int32, (EXTRA, value.shape[1]), 0)
    out = jnp.zeros(at.shape, jnp.float32)
    for n, part in enumerate((high, middle, low)):
        out = jnp.where(at == n, part.astype(jnp.float32), out)
    return out.astype(jnp.bfloat16)


def from_rows(block):
    return jnp.sum(block.astype(jnp.float32), axis=0, keepdims=True)


def combine_kernel(place, *rest):
    lefts = (rest[:4], rest[4:8])
    dy, dz = rest[8:10]
    arrivals = (rest[10:13], rest[13:16])
    own_y, own_z, bias, *sends = rest[16:-2]
    left_all, right = rest[-2:]
    y, z = place[1], place[2]
    total, rows, half = dy.shape
    n = total * rows
    fine = left_all.shape[2]
    ones = jnp.ones((EXTRA, 4 * n), jnp.bfloat16)
    for side, (mine, other, own) in enumerate(((dy, z, own_y), (dz, y, own_z))):
        for d in range(4):
            block = mine if d == 0 else arrivals[side][d - 1]
            right[pl.ds(d * n, n)] = block[...].reshape(n, half)
            for g in range(4):
                left_all[g, :, :, pl.ds(d * n, n)] = lefts[side][d][g]
        sums = dot(ones, right[...])[:1]
        bias[:, pl.ds(side * half, half)] = sums
        extra = as_rows(sums)
        for d in range(4):
            left = left_all[:, lax.rem(other + d, 4)].reshape(4 * fine, 4 * n)
            part = dot(left, right[...])
            if d == 0:
                own[...] = part.reshape(4, fine, half)
            else:
                to = sends[3 * side + d - 1]
                to[pl.ds(0, 4 * fine)] = part.astype(jnp.bfloat16)
                to[pl.ds(4 * fine, EXTRA)] = extra


def finish_kernel(place, own_y, own_z, bias, *rest):
    arrivals, keep, kept_bias, give = rest[:6], rest[6], rest[7], rest[8]
    xh = place[3]
    fine, half = own_y.shape[1:]
    for side, own in enumerate((own_y, own_z)):
        cols = pl.ds(side * half, half)
        blocks = arrivals[3 * side : 3 * side + 3]
        for n in range(2):
            mine, other = 2 * n + xh, 2 * n + 1 - xh
            kept, given = own[mine], own[other]
            for block in blocks:
                kept += block[pl.ds(pl.multiple_of(mine * fine, fine), fine)].astype(jnp.float32)
                given += block[pl.ds(pl.multiple_of(other * fine, fine), fine)].astype(jnp.float32)
            keep[n, :, cols] = kept
            give[pl.ds(n * fine, fine), cols] = given.astype(jnp.bfloat16)
        total = bias[:, cols]
        for block in blocks:
            total += from_rows(block[pl.ds(4 * fine, EXTRA)])
        kept_bias[:, cols] = total
        give[pl.ds(2 * fine, EXTRA), cols] = as_rows(total)


def last_kernel(place, keep, bias, arrived, grad_i, grad_r, grad_b):
    fine = keep.shape[1]
    for n, out in enumerate((grad_i, grad_r)):
        out[...] = keep[n] + arrived[pl.ds(n * fine, fine)].astype(jnp.float32)
    width = grad_b.shape[1]
    cols = pl.ds(pl.multiple_of(((place[3] * 4 + place[1]) * 4 + place[2]) * width, width), width)
    grad_b[...] = bias[:, cols] + from_rows(arrived[pl.ds(2 * fine, EXTRA), cols])


def shape(dims, kind):
    return pltpu.VMEM(dims, kind)


def near(array):
    return pltpu.with_memory_space_constraint(array, pltpu.VMEM)


def local(inputs, input_weight, recurrent_weight, gate_bias, lengths, cotangent):
    total, rows, width = inputs.shape
    gated = 4 * width
    stages = lax.axis_size("pipe")
    stage = lax.axis_index("pipe")
    blocks = total // BLOCK
    ticks = blocks + stages - 1
    lens = near(jnp.broadcast_to(lengths[:, None], (rows, width)))
    cot, inputs, gate_bias = near(cotangent[0]), near(inputs), near(gate_bias)
    params = pltpu.CompilerParams(vmem_limit_bytes=LIMIT)
    bf16, f32 = jnp.bfloat16, jnp.float32

    flat, turned = shape((width, gated), bf16), shape((gated, width), bf16)
    kept_gates, kept_cells = shape((total, rows, gated), f32), shape((total + 1, rows, width), f32)
    one = shape((rows, width), f32)
    state = (flat, flat, shape((total, rows, width), bf16), kept_gates, kept_cells)
    fine, half = width // 32, gated // 2
    store = shape((total, rows, half), bf16)
    block = shape((BLOCK, rows, width), bf16)
    far = pltpu.HBM((gated, width), bf16)
    state += (shape((total + 1, rows, width), bf16), far, far)
    def forward(tick):
        first = tick == 0
        extra = (turned,) if tick == ticks - 1 else ()
        return pl.pallas_call(
            partial(forward_kernel, tick=tick, stages=stages),
            out_shape=(block,) + state + extra,
            in_specs=[SMEM] + [VMEM] * 3 + ([HBM] * 2 if first else [VMEM] * 7 + [HBM] * 2),
            out_specs=(VMEM,) * 7 + (HBM,) * 2 + (VMEM,) * len(extra),
            scratch_shapes=[
                pltpu.VMEM((BLOCK, rows, gated), f32),
                pltpu.VMEM((SLOTS, PANEL, width), bf16),
                pltpu.SemaphoreType.DMA((SLOTS,)),
                pltpu.SemaphoreType.DMA((2,)),
            ],
            input_output_aliases={} if first else {5 + n: 1 + n for n in range(8)},
            compiler_params=params,
            name="forward_tick",
        )

    place = jnp.stack([stage] + [lax.axis_index(a) for a in ("y", "z", "xh")]).astype(jnp.int32)
    for tick in range(ticks):
        got = [near(arrived), *held] if tick else [pltpu.with_memory_space_constraint(w[0], pltpu.HBM) for w in (input_weight, recurrent_weight)]
        emitted, *held = forward(tick)(place, inputs, gate_bias, lens, *got)
        if tick < ticks - 1:
            on = [s for s in range(stages - 1) if 0 <= tick - s < blocks]
            arrived = lax.ppermute(emitted, "pipe", [(s, s + 1) for s in on])

    _, _, xs, gates, cells, hs, wit_far, _, wrt = held

    def backward(tick):
        first = tick == 0
        aliases = {5: 3, 6: 4, 7: 6} if first else {4 + i: 1 + i for i in range(8)}
        return pl.pallas_call(
            partial(backward_kernel, tick=tick, stages=stages),
            out_shape=(block, store, store, kept_gates, kept_cells, turned, turned, one, one),
            in_specs=[SMEM] + [VMEM] * 3 + ([HBM] + [VMEM] * 3 if first else [VMEM] * 8),
            out_specs=(VMEM,) * 9,
            scratch_shapes=[pltpu.SemaphoreType.DMA((1,))] if first else [],
            input_output_aliases=aliases,
            compiler_params=params,
            name="backward_tick",
        )

    def simple(kernel, name, outs, count, scratch=()):
        return pl.pallas_call(
            kernel,
            out_shape=outs,
            in_specs=[SMEM] + [VMEM] * count,
            out_specs=jax.tree.map(lambda _: VMEM, outs),
            scratch_shapes=scratch,
            compiler_params=params,
            name=name,
        )

    final_hidden, final_cell = hs[total], cells[total]
    held = [pltpu.with_memory_space_constraint(wit_far, pltpu.HBM), gates, cells, wrt]
    arrived = emitted
    routes = [[(i, (i + d) % 4) for i in range(4)] for d in range(1, 4)]

    def passed(made):
        return [near(lax.ppermute(made[n], "y" if n < 3 else "z", routes[n % 3])) for n in range(6)]

    group = shape((4, 4, fine, total * rows), bf16)
    lefts = []
    for tick in range(ticks):
        lower, *held = backward(tick)(place, cot, near(arrived), lens, *held)
        if tick == 0:
            xs, hs, lower = lax.optimization_barrier((xs, hs, lower))
            spread = simple(prepare_kernel, "prepare", (group,) * 8, 2, [pltpu.VMEM((4, 4, 4, fine, total * rows), bf16)])(
                place, near(xs), near(hs)
            )
        if tick < ticks - 1:
            on = [s for s in range(1, stages) if 0 <= tick - (stages - 1 - s) < blocks]
            arrived = lax.ppermute(lower, "pipe", [(s, s - 1) for s in on])
            if 1 <= tick <= 3:
                pair = lax.optimization_barrier((spread[tick], spread[4 + tick], lower))[:2]
                pair = [lax.ppermute(v, axis, routes[tick - 1]) for v, axis in zip(pair, ("y", "z"))]
                arrived, *pair = lax.optimization_barrier((arrived, *pair))
                lefts.append([near(v) for v in pair])
    dy, dz = held[:2]
    part, whole = shape((4 * fine + EXTRA, half), bf16), shape((4, fine, half), f32)
    mine_y, mine_z, bias, *sends = simple(
        combine_kernel,
        "combine",
        (whole, whole, shape((1, gated), f32)) + (part,) * 6,
        16,
        [pltpu.VMEM((4, 4, fine, 4 * total * rows), bf16), pltpu.VMEM((4 * total * rows, half), bf16)],
    )(place, spread[0], *(v for v, _ in lefts), spread[4], *(v for _, v in lefts), dy, dz, *passed([dy] * 3 + [dz] * 3))
    got = passed(sends[3:] + sends[:3])
    keep, bias, give = simple(
        finish_kernel,
        "finish",
        (shape((2, fine, gated), f32), shape((1, gated), f32), shape((2 * fine + EXTRA, gated), bf16)),
        9,
    )(place, mine_y, mine_z, bias, *got[3:], *got[:3])
    other = near(lax.ppermute(give, "xh", [(0, 1), (1, 0)]))
    made = jax.ShapeDtypeStruct
    grad_i, grad_r, grad_b = simple(
        last_kernel,
        "last",
        (made((fine, gated), f32), made((fine, gated), f32), made((1, gated // 32), f32)),
        3,
    )(place, keep, bias, other)
    return (grad_i[None], grad_r[None], grad_b, final_hidden[None], final_cell[None])


def solution(mesh):
    fine = Mesh(mesh.devices.reshape(2, 4, 4, 4), ("xh", "y", "z", "pipe"))
    return jax.shard_map(
        local,
        mesh=fine,
        in_specs=(
            P(None, DP, None),
            P("pipe", None, None),
            P("pipe", None, None),
            P("pipe", None),
            P(DP),
            P("pipe", None, DP, None),
        ),
        out_specs=(
            P("pipe", DP, None),
            P("pipe", DP, None),
            P("pipe", DP),
            P("pipe", DP, None),
            P("pipe", DP, None),
        ),
        check_vma=False,
    )
```

```python
from functools import partial

import jax
import jax.numpy as jnp
from jax import lax
from jax.experimental import pallas as pl
from jax.experimental.pallas import tpu as pltpu
from jax.sharding import Mesh, PartitionSpec as P

BLOCK = 4
LAG = 2
WIDE = 1024
COLS = 512
FORWARD_STEPS = 2
CHUNK = 256
PANEL = 256
SLOTS = 4
EXTRA = 16
DP = ("xh", "y", "z")
VMEM = pl.BlockSpec(memory_space=pltpu.VMEM)
SMEM = pl.BlockSpec(memory_space=pltpu.SMEM)
HBM = pl.BlockSpec(memory_space=pltpu.HBM)
LIMIT = 8 * 2**20


def squash(value):
    return 0.5 * jnp.tanh(0.5 * value) + 0.5


def dot(a, b):
    return jnp.dot(a, b, preferred_element_type=jnp.float32)


def shifted(at, by):
    return at + by if isinstance(at, int) else pl.multiple_of(at + by, CHUNK)


def over_columns(column, width, steps):
    run = width // steps

    def body(step, carry):
        for j in range(0, run, CHUNK):
            column(j if steps == 1 else pl.multiple_of(step * run + j, CHUNK))
        return carry

    if steps == 1:
        body(0, 0)
    else:
        lax.fori_loop(0, steps, body, 0)


def turn(share, shares, pairs, stage, sems):
    panels = pairs[0][1].shape[0] // PANEL
    groups = panels // SLOTS
    low = share * 2 * groups // shares
    high = (share + 1) * 2 * groups // shares

    for n, (source, target) in enumerate(pairs):

        def copy(at, slot, target=target):
            at = pl.multiple_of(at * PANEL, PANEL)
            return pltpu.make_async_copy(stage.at[slot], target.at[pl.ds(at, PANEL)], sems.at[slot])

        def body(group, carry, source=source, copy=copy):
            def move(slot, carry):
                at = group * SLOTS + slot
                stage[slot] = source[:, pl.ds(pl.multiple_of(at * PANEL, PANEL), PANEL)].T
                copy(at, slot).start()
                return carry

            def settle(slot, carry):
                copy(group * SLOTS + slot, slot).wait()
                return carry

            lax.fori_loop(0, SLOTS, move, 0)
            lax.fori_loop(0, SLOTS, settle, 0)
            return carry

        begin, end = (jnp.clip(v - n * groups, 0, groups) for v in (low, high))
        lax.fori_loop(begin, end, body, 0)


def forward_kernel(place, own, bias, lens, *rest, tick, stages):
    if tick == 0:
        (wi_in, wr_in), rest = rest[:2], rest[2:]
    else:
        arrived, rest = rest[0], rest[9:]
    emitted, wi, wr, xs, gates, cells, hs, wit_far, wrt_far = rest[:9]
    proj, staged, sems, load_sems = rest[-4:]
    span, rows, width = emitted.shape
    stage = place[0]
    blocks = own.shape[0] // span
    at = tick - LAG * stage
    active = (at >= 0) & (at < blocks)
    fs = at * span
    idle = LAG * (stages - 1)
    last = tick == blocks + idle - 1
    pairs = ((wr, wrt_far), (wi, wit_far))
    if tick == 0:
        load_wi = pltpu.make_async_copy(wi_in, wi, load_sems.at[0])
        load_wr = pltpu.make_async_copy(wr_in, wr, load_sems.at[1])
        load_wi.start()
        load_wr.start()
        load_wi.wait()

    @pl.when(active)
    def _():
        if tick == 0:
            xs[pl.ds(fs, span)] = own[pl.ds(fs, span)]
        else:

            @pl.when(stage == 0)
            def _():
                xs[pl.ds(fs, span)] = own[pl.ds(fs, span)]

            @pl.when(stage > 0)
            def _():
                xs[pl.ds(fs, span)] = arrived[...]

        x = xs[pl.ds(fs, span)].reshape(span * rows, width)

        def project(n, carry):
            cols = pl.ds(pl.multiple_of(n * WIDE, WIDE), WIDE)
            proj[:, :, cols] = (dot(x, wi[:, cols]) + bias[:, cols]).reshape(span, rows, WIDE)
            return carry

        lax.fori_loop(0, 4 * width // WIDE, project, 0)

    if tick == 0:
        load_wr.wait()

    turns = (0, 1, idle + blocks - 2, idle + blocks - 1)
    if tick in turns:
        late = turns.index(tick) // 2

        @pl.when((stage < stages // 2) == (late == 1))
        def _():
            turn(turns.index(tick) % 2, 2, pairs, staged, sems)

    if last:
        load = pltpu.make_async_copy(wrt_far, rest[9], load_sems.at[0])
        load.start()

    @pl.when(active)
    def _():
        @pl.when(fs == 0)
        def _():
            hs[0] = jnp.zeros((rows, width), jnp.bfloat16)
            cells[0] = jnp.zeros((rows, width), jnp.float32)

        def frame(t, carry):
            fr = fs + t
            h = hs[fr]

            def column(j):
                part = pl.ds(j, CHUNK)

                def pre(gate):
                    col = pl.ds(shifted(j, gate * width), CHUNK)
                    return proj[t, :, col] + dot(h, wr[:, col])

                alive = fr < lens[:, part]
                i, f, g, o = squash(pre(0)), squash(pre(1)), jnp.tanh(pre(2)), squash(pre(3))
                c = cells[fr, :, part]
                new_c = f * c + i * g
                new_h = (o * jnp.tanh(new_c)).astype(jnp.bfloat16)
                old_h = hs[fr, :, part]
                for gate, value in enumerate((i, f, g, o)):
                    gates[fr, :, pl.ds(shifted(j, gate * width), CHUNK)] = value
                cells[fr + 1, :, part] = jnp.where(alive, new_c, c)
                hs[fr + 1, :, part] = jnp.where(alive, new_h, old_h)
                emitted[t, :, part] = jnp.where(alive, new_h, jnp.zeros_like(new_h))

            over_columns(column, width, FORWARD_STEPS)
            return carry

        lax.fori_loop(0, span, frame, 0)

    if last:
        load.wait()


def block_at(tick, stage, stages, blocks):
    offset = tick - LAG * (stages - 1 - stage)
    return blocks - 1 - offset, (offset >= 0) & (offset < blocks)


def backward_kernel(place, cot, arrived, lens, *rest, tick, stages):
    if tick == 0:
        wit_far, gates_in, cells_in, wrt_in, lower, dy, dz, gates, cells, wit, wrt, dh, dc, sem = rest
        load = pltpu.make_async_copy(wit_far, wit, sem.at[0])
        load.start()
    else:
        lower, dy, dz, gates, cells, wit, wrt, dh, dc = rest[8:]
    span, rows, width = arrived.shape
    total = gates.shape[0]
    half = 2 * width
    stage = place[0]
    blocks = total // span
    at, active = block_at(tick, stage, stages, blocks)
    fs = at * span

    @pl.when(active)
    def _():
        @pl.when(fs + span == total)
        def _():
            dh[...] = jnp.zeros((rows, width), jnp.float32)
            dc[...] = jnp.zeros((rows, width), jnp.float32)

        def frame(n, carry):
            t = span - 1 - n
            fr = fs + t
            acc = None
            for j in range(0, width, CHUNK):
                part = pl.ds(j, CHUNK)
                alive = fr < lens[:, part]
                i = gates[fr, :, pl.ds(j, CHUNK)]
                f = gates[fr, :, pl.ds(width + j, CHUNK)]
                g = gates[fr, :, pl.ds(2 * width + j, CHUNK)]
                o = gates[fr, :, pl.ds(3 * width + j, CHUNK)]
                u = jnp.where(stage == stages - 1, 0.0, arrived[t, :, part].astype(jnp.float32))
                e = jnp.where(alive, dh[:, part] + u + cot[fr, :, part].astype(jnp.float32), 0.0)
                k = jnp.tanh(cells[fr + 1, :, part])
                old_dc = dc[:, part]
                dcell = jnp.where(alive, old_dc, 0.0) + e * o * (1.0 - k * k)
                parts = (
                    dcell * g * i * (1.0 - i),
                    dcell * cells[fr, :, part] * f * (1.0 - f),
                    dcell * i * (1.0 - g * g),
                    e * k * o * (1.0 - o),
                )
                dc[:, part] = jnp.where(alive, 0.0, old_dc) + dcell * f
                dh[:, part] = jnp.where(alive, 0.0, dh[:, part])
                for gate, value in enumerate(parts):
                    col = pl.ds(gate * width + j, CHUNK)
                    d = value.astype(jnp.bfloat16)
                    if gate < 2:
                        dy[fr, :, col] = d
                    else:
                        dz[fr, :, pl.ds(gate * width + j - half, CHUNK)] = d
                    term = dot(d, wrt[col, :])
                    acc = term if acc is None else acc + term
            dh[...] = dh[...] + acc
            return carry

        lax.fori_loop(0, span, frame, 0)

    if tick == 0:
        load.wait()
    if tick < blocks + LAG * (stages - 1) - 1:

        @pl.when(active & (stage > 0))
        def _():
            left, right = (v[pl.ds(fs, span)].reshape(span * rows, half) for v in (dy, dz))

            def descend(n, carry):
                cols = pl.ds(pl.multiple_of(n * CHUNK, CHUNK), CHUNK)
                u = dot(left, wit[pl.ds(0, half), cols]) + dot(right, wit[pl.ds(half, half), cols])
                lower[:, :, cols] = u.astype(jnp.bfloat16).reshape(span, rows, CHUNK)
                return carry

            lax.fori_loop(0, width // CHUNK, descend, 0)


def prepare_kernel(place, xs, hs, *rest):
    to_y, to_z, whole = rest[:4], rest[4:8], rest[8]
    total, rows, width = xs.shape
    y, z = place[1], place[2]
    for n, source in enumerate((xs, hs)):
        flat = source[pl.ds(0, total)].reshape(total * rows, width)
        whole[pl.ds(2 * n, 2)] = flat.T.reshape((2,) + whole.shape[1:])
    for d in range(4):
        for g in range(4):
            to_y[d][g] = whole[g, lax.rem(y + d, 4)]
            for i in range(4):
                to_z[d][g, i] = whole[g, i, lax.rem(z + d, 4)]


def as_rows(value):
    high = value.astype(jnp.bfloat16)
    rest = value - high.astype(jnp.float32)
    middle = rest.astype(jnp.bfloat16)
    low = (rest - middle.astype(jnp.float32)).astype(jnp.bfloat16)
    at = lax.broadcasted_iota(jnp.int32, (EXTRA, value.shape[1]), 0)
    out = jnp.zeros(at.shape, jnp.float32)
    for n, part in enumerate((high, middle, low)):
        out = jnp.where(at == n, part.astype(jnp.float32), out)
    return out.astype(jnp.bfloat16)


def from_rows(block):
    return jnp.sum(block.astype(jnp.float32), axis=0, keepdims=True)


def combine_kernel(place, *rest):
    lefts = (rest[:4], rest[4:8])
    dy, dz = rest[8:10]
    arrivals = (rest[10:13], rest[13:16])
    own_y, own_z, bias, *sends = rest[16:-2]
    left_all, right = rest[-2:]
    y, z = place[1], place[2]
    total, rows, half = dy.shape
    n = total * rows
    fine = left_all.shape[2]
    ones = jnp.ones((EXTRA, 4 * n), jnp.bfloat16)
    for side, (mine, other, own) in enumerate(((dy, z, own_y), (dz, y, own_z))):
        for d in range(4):
            block = mine if d == 0 else arrivals[side][d - 1]
            right[pl.ds(d * n, n)] = block[...].reshape(n, half)
            for g in range(4):
                left_all[g, :, :, pl.ds(d * n, n)] = lefts[side][d][g]

        def columns(step, carry, side=side, other=other, own=own):
            at = pl.multiple_of(step * COLS, COLS)
            cols = pl.ds(at, COLS)
            block = right[:, cols]
            sums = dot(ones, block)[:1]
            bias[:, pl.ds(pl.multiple_of(at + side * half, COLS), COLS)] = sums
            extra = as_rows(sums)
            for d in range(4):
                left = left_all[:, lax.rem(other + d, 4)].reshape(4 * fine, 4 * n)
                part = dot(left, block)
                if d == 0:
                    own[:, :, cols] = part.reshape(4, fine, COLS)
                else:
                    to = sends[3 * side + d - 1]
                    to[pl.ds(0, 4 * fine), cols] = part.astype(jnp.bfloat16)
                    to[pl.ds(4 * fine, EXTRA), cols] = extra
            return carry

        lax.fori_loop(0, half // COLS, columns, 0)


def finish_kernel(place, own_y, own_z, bias, *rest):
    arrivals, keep, kept_bias, give = rest[:6], rest[6], rest[7], rest[8]
    xh = place[3]
    fine, half = own_y.shape[1:]
    for side, own in enumerate((own_y, own_z)):
        cols = pl.ds(side * half, half)
        blocks = arrivals[3 * side : 3 * side + 3]
        for n in range(2):
            mine, other = 2 * n + xh, 2 * n + 1 - xh
            kept, given = own[mine], own[other]
            for block in blocks:
                kept += block[pl.ds(pl.multiple_of(mine * fine, fine), fine)].astype(jnp.float32)
                given += block[pl.ds(pl.multiple_of(other * fine, fine), fine)].astype(jnp.float32)
            keep[n, :, cols] = kept
            give[pl.ds(n * fine, fine), cols] = given.astype(jnp.bfloat16)
        total = bias[:, cols]
        for block in blocks:
            total += from_rows(block[pl.ds(4 * fine, EXTRA)])
        kept_bias[:, cols] = total
        give[pl.ds(2 * fine, EXTRA), cols] = as_rows(total)


def last_kernel(place, keep, bias, arrived, grad_i, grad_r, grad_b):
    fine = keep.shape[1]
    for n, out in enumerate((grad_i, grad_r)):
        out[...] = keep[n] + arrived[pl.ds(n * fine, fine)].astype(jnp.float32)
    width = grad_b.shape[1]
    cols = pl.ds(pl.multiple_of(((place[3] * 4 + place[1]) * 4 + place[2]) * width, width), width)
    grad_b[...] = bias[:, cols] + from_rows(arrived[pl.ds(2 * fine, EXTRA), cols])


def shape(dims, kind):
    return pltpu.VMEM(dims, kind)


def near(array):
    return pltpu.with_memory_space_constraint(array, pltpu.VMEM)


def local(inputs, input_weight, recurrent_weight, gate_bias, lengths, cotangent):
    total, rows, width = inputs.shape
    gated = 4 * width
    stages = lax.axis_size("pipe")
    stage = lax.axis_index("pipe")
    blocks = total // BLOCK
    ticks = blocks + LAG * (stages - 1)
    lens = near(jnp.broadcast_to(lengths[:, None], (rows, width)))
    cot, inputs, gate_bias = near(cotangent[0]), near(inputs), near(gate_bias)
    params = pltpu.CompilerParams(vmem_limit_bytes=LIMIT)
    bf16, f32 = jnp.bfloat16, jnp.float32

    flat, turned = shape((width, gated), bf16), shape((gated, width), bf16)
    kept_gates, kept_cells = shape((total, rows, gated), f32), shape((total + 1, rows, width), f32)
    one = shape((rows, width), f32)
    state = (flat, flat, shape((total, rows, width), bf16), kept_gates, kept_cells)
    fine, half = width // 32, gated // 2
    store = shape((total, rows, half), bf16)
    block = shape((BLOCK, rows, width), bf16)
    far = pltpu.HBM((gated, width), bf16)
    state += (shape((total + 1, rows, width), bf16), far, far)
    def forward(tick):
        first = tick == 0
        extra = (turned,) if tick == ticks - 1 else ()
        return pl.pallas_call(
            partial(forward_kernel, tick=tick, stages=stages),
            out_shape=(block,) + state + extra,
            in_specs=[SMEM] + [VMEM] * 3 + ([HBM] * 2 if first else [VMEM] * 7 + [HBM] * 2),
            out_specs=(VMEM,) * 7 + (HBM,) * 2 + (VMEM,) * len(extra),
            scratch_shapes=[
                pltpu.VMEM((BLOCK, rows, gated), f32),
                pltpu.VMEM((SLOTS, PANEL, width), bf16),
                pltpu.SemaphoreType.DMA((SLOTS,)),
                pltpu.SemaphoreType.DMA((2,)),
            ],
            input_output_aliases={} if first else {5 + n: 1 + n for n in range(8)},
            compiler_params=params,
            name="forward_tick",
        )

    place = jnp.stack([stage] + [lax.axis_index(a) for a in ("y", "z", "xh")]).astype(jnp.int32)
    landed = {}
    for tick in range(ticks):
        if tick == 0:
            got = [pltpu.with_memory_space_constraint(w[0], pltpu.HBM) for w in (input_weight, recurrent_weight)]
        else:
            got = [landed.get(tick, emitted), *held]
        emitted, *held = forward(tick)(place, inputs, gate_bias, lens, *got)
        on = [s for s in range(stages - 1) if 0 <= tick - LAG * s < blocks]
        if on:
            landed[tick + LAG] = near(lax.ppermute(emitted, "pipe", [(s, s + 1) for s in on]))

    _, _, xs, gates, cells, hs, wit_far, _, wrt = held

    def backward(tick):
        first = tick == 0
        aliases = {5: 3, 6: 4, 7: 6} if first else {4 + i: 1 + i for i in range(8)}
        return pl.pallas_call(
            partial(backward_kernel, tick=tick, stages=stages),
            out_shape=(block, store, store, kept_gates, kept_cells, turned, turned, one, one),
            in_specs=[SMEM] + [VMEM] * 3 + ([HBM] + [VMEM] * 3 if first else [VMEM] * 8),
            out_specs=(VMEM,) * 9,
            scratch_shapes=[pltpu.SemaphoreType.DMA((1,))] if first else [],
            input_output_aliases=aliases,
            compiler_params=params,
            name="backward_tick",
        )

    def simple(kernel, name, outs, count, scratch=()):
        return pl.pallas_call(
            kernel,
            out_shape=outs,
            in_specs=[SMEM] + [VMEM] * count,
            out_specs=jax.tree.map(lambda _: VMEM, outs),
            scratch_shapes=scratch,
            compiler_params=params,
            name=name,
        )

    final_hidden, final_cell = hs[total], cells[total]
    held = [pltpu.with_memory_space_constraint(wit_far, pltpu.HBM), gates, cells, wrt]
    routes = [[(i, (i + d) % 4) for i in range(4)] for d in range(1, 4)]

    def passed(made):
        return [near(lax.ppermute(made[n], "y" if n < 3 else "z", routes[n % 3])) for n in range(6)]

    group = shape((4, 4, fine, total * rows), bf16)
    lefts, landed, lower = [], {}, emitted
    for tick in range(ticks):
        lower, *held = backward(tick)(place, cot, landed.get(tick, lower), lens, *held)
        if tick == 0:
            xs, hs, lower = lax.optimization_barrier((xs, hs, lower))
            spread = simple(prepare_kernel, "prepare", (group,) * 8, 2, [pltpu.VMEM((4, 4, 4, fine, total * rows), bf16)])(
                place, near(xs), near(hs)
            )
        on = [s for s in range(1, stages) if 0 <= tick - LAG * (stages - 1 - s) < blocks]
        if on:
            landed[tick + LAG] = near(lax.ppermute(lower, "pipe", [(s, s - 1) for s in on]))
        if 1 <= tick <= 6:
            axis, d = ("y", tick) if tick < 4 else ("z", tick - 3)
            piece, _ = lax.optimization_barrier((spread[tick if tick < 4 else tick + 1], lower))
            piece = lax.ppermute(piece, axis, routes[d - 1])
            pair = lax.optimization_barrier((landed[tick + LAG], piece))
            landed[tick + LAG], piece = map(near, pair)
            lefts.append(piece)
    dy, dz = held[:2]
    part, whole = shape((4 * fine + EXTRA, half), bf16), shape((4, fine, half), f32)
    mine_y, mine_z, bias, *sends = simple(
        combine_kernel,
        "combine",
        (whole, whole, shape((1, gated), f32)) + (part,) * 6,
        16,
        [pltpu.VMEM((4, 4, fine, 4 * total * rows), bf16), pltpu.VMEM((4 * total * rows, half), bf16)],
    )(place, spread[0], *lefts[:3], spread[4], *lefts[3:], dy, dz, *passed([dy] * 3 + [dz] * 3))
    got = passed(sends[3:] + sends[:3])
    keep, bias, give = simple(
        finish_kernel,
        "finish",
        (shape((2, fine, gated), f32), shape((1, gated), f32), shape((2 * fine + EXTRA, gated), bf16)),
        9,
    )(place, mine_y, mine_z, bias, *got[3:], *got[:3])
    other = near(lax.ppermute(give, "xh", [(0, 1), (1, 0)]))
    made = jax.ShapeDtypeStruct
    grad_i, grad_r, grad_b = simple(
        last_kernel,
        "last",
        (made((fine, gated), f32), made((fine, gated), f32), made((1, gated // 32), f32)),
        3,
    )(place, keep, bias, other)
    return (grad_i[None], grad_r[None], grad_b, final_hidden[None], final_cell[None])


def solution(mesh):
    fine = Mesh(mesh.devices.reshape(2, 4, 4, 4), ("xh", "y", "z", "pipe"))
    return jax.shard_map(
        local,
        mesh=fine,
        in_specs=(
            P(None, DP, None),
            P("pipe", None, None),
            P("pipe", None, None),
            P("pipe", None),
            P(DP),
            P("pipe", None, DP, None),
        ),
        out_specs=(
            P("pipe", DP, None),
            P("pipe", DP, None),
            P("pipe", DP),
            P("pipe", DP, None),
            P("pipe", DP, None),
        ),
        check_vma=False,
    )
```

```python
from functools import partial

import jax
import jax.numpy as jnp
from jax import lax
from jax.experimental import pallas as pl
from jax.experimental.pallas import tpu as pltpu
from jax.sharding import Mesh, PartitionSpec as P

BLOCK = 4
LAG = 2
WIDE = 1024
COLS = 512
WHOLE = (2,)
CHUNK = 256
PANEL = 256
SLOTS = 4
EXTRA = 16
DP = ("xh", "y", "z")
VMEM = pl.BlockSpec(memory_space=pltpu.VMEM)
SMEM = pl.BlockSpec(memory_space=pltpu.SMEM)
HBM = pl.BlockSpec(memory_space=pltpu.HBM)
LIMIT = 8 * 2**20


def squash(value):
    return 0.5 * jnp.tanh(0.5 * value) + 0.5


def dot(a, b):
    return jnp.dot(a, b, preferred_element_type=jnp.float32)


def shifted(at, by):
    return at + by if isinstance(at, int) else pl.multiple_of(at + by, CHUNK)


def over_columns(column, width, steps):
    run = width // steps

    def body(step, carry):
        for j in range(0, run, CHUNK):
            column(j if steps == 1 else pl.multiple_of(step * run + j, CHUNK))
        return carry

    if steps == 1:
        body(0, 0)
    else:
        lax.fori_loop(0, steps, body, 0)


def turn(share, shares, pairs, stage, sems):
    panels = pairs[0][1].shape[0] // PANEL
    groups = panels // SLOTS
    low = share * 2 * groups // shares
    high = (share + 1) * 2 * groups // shares

    for n, (source, target) in enumerate(pairs):

        def copy(at, slot, target=target):
            at = pl.multiple_of(at * PANEL, PANEL)
            return pltpu.make_async_copy(stage.at[slot], target.at[pl.ds(at, PANEL)], sems.at[slot])

        def body(group, carry, source=source, copy=copy):
            def move(slot, carry):
                at = group * SLOTS + slot
                stage[slot] = source[:, pl.ds(pl.multiple_of(at * PANEL, PANEL), PANEL)].T
                copy(at, slot).start()
                return carry

            def settle(slot, carry):
                copy(group * SLOTS + slot, slot).wait()
                return carry

            lax.fori_loop(0, SLOTS, move, 0)
            lax.fori_loop(0, SLOTS, settle, 0)
            return carry

        begin, end = (jnp.clip(v - n * groups, 0, groups) for v in (low, high))
        lax.fori_loop(begin, end, body, 0)


def forward_kernel(place, own, bias, lens, *rest, tick, stages):
    if tick == 0:
        (wi_in, wr_in), rest = rest[:2], rest[2:]
    else:
        arrived, rest = rest[0], rest[9:]
    emitted, wi, wr, xs, gates, cells, hs, wit_far, wrt_far = rest[:9]
    proj, staged, sems, load_sems = rest[-4:]
    span, rows, width = emitted.shape
    stage = place[0]
    blocks = own.shape[0] // span
    at = tick - LAG * stage
    active = (at >= 0) & (at < blocks)
    fs = at * span
    idle = LAG * (stages - 1)
    last = tick == blocks + idle - 1
    pairs = ((wr, wrt_far), (wi, wit_far))
    if tick == 0:
        load_wi = pltpu.make_async_copy(wi_in, wi, load_sems.at[0])
        load_wr = pltpu.make_async_copy(wr_in, wr, load_sems.at[1])
        load_wi.start()
        load_wr.start()
        load_wi.wait()

    @pl.when(active)
    def _():
        if tick == 0:
            xs[pl.ds(fs, span)] = own[pl.ds(fs, span)]
        else:

            @pl.when(stage == 0)
            def _():
                xs[pl.ds(fs, span)] = own[pl.ds(fs, span)]

            @pl.when(stage > 0)
            def _():
                xs[pl.ds(fs, span)] = arrived[...]

        x = xs[pl.ds(fs, span)].reshape(span * rows, width)

        def project(n, carry):
            cols = pl.ds(pl.multiple_of(n * WIDE, WIDE), WIDE)
            proj[:, :, cols] = (dot(x, wi[:, cols]) + bias[:, cols]).reshape(span, rows, WIDE)
            return carry

        lax.fori_loop(0, 4 * width // WIDE, project, 0)

    if tick == 0:

        @pl.when(jnp.logical_not(active))
        def _():
            load_wr.wait()

    turns = (0, 1, idle + blocks - 2, idle + blocks - 1)
    if tick in turns:
        late = turns.index(tick) // 2

        @pl.when((stage < stages // 2) == (late == 1))
        def _():
            turn(turns.index(tick) % 2, 2, pairs, staged, sems)

    if last:
        load = pltpu.make_async_copy(wrt_far, rest[9], load_sems.at[0])
        load.start()

    @pl.when(active)
    def _():
        @pl.when(fs == 0)
        def _():
            hs[0] = jnp.zeros((rows, width), jnp.bfloat16)
            cells[0] = jnp.zeros((rows, width), jnp.float32)

        def frame(t, carry, start=False):
            fr = fs + t
            h = hs[fr]

            def column(j):
                part = pl.ds(j, CHUNK)

                def pre(gate):
                    col = pl.ds(shifted(j, gate * width), CHUNK)
                    return proj[t, :, col] if start else proj[t, :, col] + dot(h, wr[:, col])

                alive = fr < lens[:, part]
                i, f, g, o = squash(pre(0)), squash(pre(1)), jnp.tanh(pre(2)), squash(pre(3))
                c = cells[fr, :, part]
                new_c = f * c + i * g
                new_h = (o * jnp.tanh(new_c)).astype(jnp.bfloat16)
                old_h = hs[fr, :, part]
                for gate, value in enumerate((i, f, g, o)):
                    gates[fr, :, pl.ds(shifted(j, gate * width), CHUNK)] = value
                cells[fr + 1, :, part] = jnp.where(alive, new_c, c)
                hs[fr + 1, :, part] = jnp.where(alive, new_h, old_h)
                emitted[t, :, part] = jnp.where(alive, new_h, jnp.zeros_like(new_h))

            over_columns(column, width, 1 if start or tick in WHOLE else 2)
            return carry

        if tick == 0:
            frame(0, 0, start=True)
            load_wr.wait()
        lax.fori_loop(1 if tick == 0 else 0, span, frame, 0)

    if last:
        load.wait()


def block_at(tick, stage, stages, blocks):
    offset = tick - LAG * (stages - 1 - stage)
    return blocks - 1 - offset, (offset >= 0) & (offset < blocks)


def backward_kernel(place, cot, arrived, lens, *rest, tick, stages):
    if tick == 0:
        wit_far, gates_in, cells_in, wrt_in, lower, dy, dz, gates, cells, wit, wrt, dh, dc, sem = rest
        load = pltpu.make_async_copy(wit_far, wit, sem.at[0])
        load.start()
    else:
        lower, dy, dz, gates, cells, wit, wrt, dh, dc = rest[8:]
    span, rows, width = arrived.shape
    total = gates.shape[0]
    half = 2 * width
    stage = place[0]
    blocks = total // span
    at, active = block_at(tick, stage, stages, blocks)
    fs = at * span

    @pl.when(active)
    def _():
        @pl.when(fs + span == total)
        def _():
            dh[...] = jnp.zeros((rows, width), jnp.float32)
            dc[...] = jnp.zeros((rows, width), jnp.float32)

        def frame(n, carry, end=False):
            t = span - 1 - n
            fr = fs + t
            acc = None
            for j in range(0, width, CHUNK):
                part = pl.ds(j, CHUNK)
                alive = fr < lens[:, part]
                i = gates[fr, :, pl.ds(j, CHUNK)]
                f = gates[fr, :, pl.ds(width + j, CHUNK)]
                g = gates[fr, :, pl.ds(2 * width + j, CHUNK)]
                o = gates[fr, :, pl.ds(3 * width + j, CHUNK)]
                u = jnp.where(stage == stages - 1, 0.0, arrived[t, :, part].astype(jnp.float32))
                e = jnp.where(alive, dh[:, part] + u + cot[fr, :, part].astype(jnp.float32), 0.0)
                k = jnp.tanh(cells[fr + 1, :, part])
                old_dc = dc[:, part]
                dcell = jnp.where(alive, old_dc, 0.0) + e * o * (1.0 - k * k)
                parts = (
                    dcell * g * i * (1.0 - i),
                    dcell * cells[fr, :, part] * f * (1.0 - f),
                    dcell * i * (1.0 - g * g),
                    e * k * o * (1.0 - o),
                )
                dc[:, part] = jnp.where(alive, 0.0, old_dc) + dcell * f
                dh[:, part] = jnp.where(alive, 0.0, dh[:, part])
                for gate, value in enumerate(parts):
                    col = pl.ds(gate * width + j, CHUNK)
                    d = value.astype(jnp.bfloat16)
                    if gate < 2:
                        dy[fr, :, col] = d
                    else:
                        dz[fr, :, pl.ds(gate * width + j - half, CHUNK)] = d
                    if not end:
                        term = dot(d, wrt[col, :])
                        acc = term if acc is None else acc + term
            if not end:
                dh[...] = dh[...] + acc
            return carry

        final = tick == blocks + LAG * (stages - 1) - 1
        lax.fori_loop(0, span - 1 if final else span, frame, 0)
        if final:
            frame(span - 1, 0, end=True)


    if tick == 0:
        load.wait()
    if tick < blocks + LAG * (stages - 1) - 1:

        @pl.when(active & (stage > 0))
        def _():
            left, right = (v[pl.ds(fs, span)].reshape(span * rows, half) for v in (dy, dz))

            def descend(n, carry):
                cols = pl.ds(pl.multiple_of(n * CHUNK, CHUNK), CHUNK)
                u = dot(left, wit[pl.ds(0, half), cols]) + dot(right, wit[pl.ds(half, half), cols])
                lower[:, :, cols] = u.astype(jnp.bfloat16).reshape(span, rows, CHUNK)
                return carry

            lax.fori_loop(0, width // CHUNK, descend, 0)


def prepare_kernel(place, xs, hs, *rest):
    to_y, to_z, whole = rest[:4], rest[4:8], rest[8]
    total, rows, width = xs.shape
    y, z = place[1], place[2]
    for n, source in enumerate((xs, hs)):
        flat = source[pl.ds(0, total)].reshape(total * rows, width)
        whole[pl.ds(2 * n, 2)] = flat.T.reshape((2,) + whole.shape[1:])
    for d in range(4):
        for g in range(4):
            to_y[d][g] = whole[g, lax.rem(y + d, 4)]
            for i in range(4):
                to_z[d][g, i] = whole[g, i, lax.rem(z + d, 4)]


def as_rows(value):
    high = value.astype(jnp.bfloat16)
    rest = value - high.astype(jnp.float32)
    middle = rest.astype(jnp.bfloat16)
    low = (rest - middle.astype(jnp.float32)).astype(jnp.bfloat16)
    at = lax.broadcasted_iota(jnp.int32, (EXTRA, value.shape[1]), 0)
    out = jnp.zeros(at.shape, jnp.float32)
    for n, part in enumerate((high, middle, low)):
        out = jnp.where(at == n, part.astype(jnp.float32), out)
    return out.astype(jnp.bfloat16)


def from_rows(block):
    return jnp.sum(block.astype(jnp.float32), axis=0, keepdims=True)


def combine_kernel(place, *rest):
    lefts = (rest[:4], rest[4:8])
    dy, dz = rest[8:10]
    arrivals = (rest[10:13], rest[13:16])
    own_y, own_z, bias, *sends = rest[16:-2]
    left_all, right = rest[-2:]
    y, z = place[1], place[2]
    total, rows, half = dy.shape
    n = total * rows
    fine = left_all.shape[2]
    ones = jnp.ones((EXTRA, 4 * n), jnp.bfloat16)
    for side, (mine, other, own) in enumerate(((dy, z, own_y), (dz, y, own_z))):
        for d in range(4):
            block = mine if d == 0 else arrivals[side][d - 1]
            right[pl.ds(d * n, n)] = block[...].reshape(n, half)
            for g in range(4):
                left_all[g, :, :, pl.ds(d * n, n)] = lefts[side][d][g]

        def columns(step, carry, side=side, other=other, own=own):
            at = pl.multiple_of(step * COLS, COLS)
            cols = pl.ds(at, COLS)
            block = right[:, cols]
            sums = dot(ones, block)[:1]
            bias[:, pl.ds(pl.multiple_of(at + side * half, COLS), COLS)] = sums
            extra = as_rows(sums)
            for d in range(4):
                left = left_all[:, lax.rem(other + d, 4)].reshape(4 * fine, 4 * n)
                part = dot(left, block)
                if d == 0:
                    own[:, :, cols] = part.reshape(4, fine, COLS)
                else:
                    to = sends[3 * side + d - 1]
                    to[pl.ds(0, 4 * fine), cols] = part.astype(jnp.bfloat16)
                    to[pl.ds(4 * fine, EXTRA), cols] = extra
            return carry

        lax.fori_loop(0, half // COLS, columns, 0)


def finish_kernel(place, own_y, own_z, bias, *rest):
    arrivals, keep, kept_bias, give = rest[:6], rest[6], rest[7], rest[8]
    xh = place[3]
    fine, half = own_y.shape[1:]
    for side, own in enumerate((own_y, own_z)):
        cols = pl.ds(side * half, half)
        blocks = arrivals[3 * side : 3 * side + 3]
        for n in range(2):
            mine, other = 2 * n + xh, 2 * n + 1 - xh
            kept, given = own[mine], own[other]
            for block in blocks:
                kept += block[pl.ds(pl.multiple_of(mine * fine, fine), fine)].astype(jnp.float32)
                given += block[pl.ds(pl.multiple_of(other * fine, fine), fine)].astype(jnp.float32)
            keep[n, :, cols] = kept
            give[pl.ds(n * fine, fine), cols] = given.astype(jnp.bfloat16)
        total = bias[:, cols]
        for block in blocks:
            total += from_rows(block[pl.ds(4 * fine, EXTRA)])
        kept_bias[:, cols] = total
        give[pl.ds(2 * fine, EXTRA), cols] = as_rows(total)


def last_kernel(place, keep, bias, arrived, grad_i, grad_r, grad_b):
    fine = keep.shape[1]
    for n, out in enumerate((grad_i, grad_r)):
        out[...] = keep[n] + arrived[pl.ds(n * fine, fine)].astype(jnp.float32)
    width = grad_b.shape[1]
    cols = pl.ds(pl.multiple_of(((place[3] * 4 + place[1]) * 4 + place[2]) * width, width), width)
    grad_b[...] = bias[:, cols] + from_rows(arrived[pl.ds(2 * fine, EXTRA), cols])


def shape(dims, kind):
    return pltpu.VMEM(dims, kind)


def near(array):
    return pltpu.with_memory_space_constraint(array, pltpu.VMEM)


def local(inputs, input_weight, recurrent_weight, gate_bias, lengths, cotangent):
    total, rows, width = inputs.shape
    gated = 4 * width
    stages = lax.axis_size("pipe")
    stage = lax.axis_index("pipe")
    blocks = total // BLOCK
    ticks = blocks + LAG * (stages - 1)
    lens = near(jnp.broadcast_to(lengths[:, None], (rows, width)))
    cot, inputs, gate_bias = near(cotangent[0]), near(inputs), near(gate_bias)
    params = pltpu.CompilerParams(vmem_limit_bytes=LIMIT)
    bf16, f32 = jnp.bfloat16, jnp.float32

    flat, turned = shape((width, gated), bf16), shape((gated, width), bf16)
    kept_gates, kept_cells = shape((total, rows, gated), f32), shape((total + 1, rows, width), f32)
    one = shape((rows, width), f32)
    state = (flat, flat, shape((total, rows, width), bf16), kept_gates, kept_cells)
    fine, half = width // 32, gated // 2
    store = shape((total, rows, half), bf16)
    block = shape((BLOCK, rows, width), bf16)
    far = pltpu.HBM((gated, width), bf16)
    state += (shape((total + 1, rows, width), bf16), far, far)
    def forward(tick):
        first = tick == 0
        extra = (turned,) if tick == ticks - 1 else ()
        return pl.pallas_call(
            partial(forward_kernel, tick=tick, stages=stages),
            out_shape=(block,) + state + extra,
            in_specs=[SMEM] + [VMEM] * 3 + ([HBM] * 2 if first else [VMEM] * 7 + [HBM] * 2),
            out_specs=(VMEM,) * 7 + (HBM,) * 2 + (VMEM,) * len(extra),
            scratch_shapes=[
                pltpu.VMEM((BLOCK, rows, gated), f32),
                pltpu.VMEM((SLOTS, PANEL, width), bf16),
                pltpu.SemaphoreType.DMA((SLOTS,)),
                pltpu.SemaphoreType.DMA((2,)),
            ],
            input_output_aliases={} if first else {5 + n: 1 + n for n in range(8)},
            compiler_params=params,
            name="forward_tick",
        )

    place = jnp.stack([stage] + [lax.axis_index(a) for a in ("y", "z", "xh")]).astype(jnp.int32)
    landed = {}
    for tick in range(ticks):
        if tick == 0:
            got = [pltpu.with_memory_space_constraint(w[0], pltpu.HBM) for w in (input_weight, recurrent_weight)]
        else:
            got = [landed.get(tick, emitted), *held]
        emitted, *held = forward(tick)(place, inputs, gate_bias, lens, *got)
        on = [s for s in range(stages - 1) if 0 <= tick - LAG * s < blocks]
        if on:
            landed[tick + LAG] = near(lax.ppermute(emitted, "pipe", [(s, s + 1) for s in on]))

    _, _, xs, gates, cells, hs, wit_far, _, wrt = held

    def backward(tick):
        first = tick == 0
        aliases = {5: 3, 6: 4, 7: 6} if first else {4 + i: 1 + i for i in range(8)}
        return pl.pallas_call(
            partial(backward_kernel, tick=tick, stages=stages),
            out_shape=(block, store, store, kept_gates, kept_cells, turned, turned, one, one),
            in_specs=[SMEM] + [VMEM] * 3 + ([HBM] + [VMEM] * 3 if first else [VMEM] * 8),
            out_specs=(VMEM,) * 9,
            scratch_shapes=[pltpu.SemaphoreType.DMA((1,))] if first else [],
            input_output_aliases=aliases,
            compiler_params=params,
            name="backward_tick",
        )

    def simple(kernel, name, outs, count, scratch=()):
        return pl.pallas_call(
            kernel,
            out_shape=outs,
            in_specs=[SMEM] + [VMEM] * count,
            out_specs=jax.tree.map(lambda _: VMEM, outs),
            scratch_shapes=scratch,
            compiler_params=params,
            name=name,
        )

    held = [pltpu.with_memory_space_constraint(wit_far, pltpu.HBM), gates, cells, wrt]
    routes = [[(i, (i + d) % 4) for i in range(4)] for d in range(1, 4)]

    def passed(made):
        return [near(lax.ppermute(made[n], "y" if n < 3 else "z", routes[n % 3])) for n in range(6)]

    group = shape((4, 4, fine, total * rows), bf16)
    lefts, landed, lower = [], {}, emitted
    for tick in range(ticks):
        lower, *held = backward(tick)(place, cot, landed.get(tick, lower), lens, *held)
        if tick == 0:
            xs, hs, lower = lax.optimization_barrier((xs, hs, lower))
            spread = simple(prepare_kernel, "prepare", (group,) * 8, 2, [pltpu.VMEM((4, 4, 4, fine, total * rows), bf16)])(
                place, near(xs), near(hs)
            )
        on = [s for s in range(1, stages) if 0 <= tick - LAG * (stages - 1 - s) < blocks]
        if on:
            landed[tick + LAG] = near(lax.ppermute(lower, "pipe", [(s, s - 1) for s in on]))
        if 1 <= tick <= 6:
            axis, d = ("y", tick) if tick < 4 else ("z", tick - 3)
            piece, _ = lax.optimization_barrier((spread[tick if tick < 4 else tick + 1], lower))
            piece = lax.ppermute(piece, axis, routes[d - 1])
            pair = lax.optimization_barrier((landed[tick + LAG], piece))
            landed[tick + LAG], piece = map(near, pair)
            lefts.append(piece)
    dy, dz = held[:2]
    final_hidden, final_cell = hs[total], held[3][total]
    part, whole = shape((4 * fine + EXTRA, half), bf16), shape((4, fine, half), f32)
    mine_y, mine_z, bias, *sends = simple(
        combine_kernel,
        "combine",
        (whole, whole, shape((1, gated), f32)) + (part,) * 6,
        16,
        [pltpu.VMEM((4, 4, fine, 4 * total * rows), bf16), pltpu.VMEM((4 * total * rows, half), bf16)],
    )(place, spread[0], *lefts[:3], spread[4], *lefts[3:], dy, dz, *passed([dy] * 3 + [dz] * 3))
    got = passed(sends[3:] + sends[:3])
    keep, bias, give = simple(
        finish_kernel,
        "finish",
        (shape((2, fine, gated), f32), shape((1, gated), f32), shape((2 * fine + EXTRA, gated), bf16)),
        9,
    )(place, mine_y, mine_z, bias, *got[3:], *got[:3])
    other = near(lax.ppermute(give, "xh", [(0, 1), (1, 0)]))
    made = jax.ShapeDtypeStruct
    grad_i, grad_r, grad_b = simple(
        last_kernel,
        "last",
        (made((fine, gated), f32), made((fine, gated), f32), made((1, gated // 32), f32)),
        3,
    )(place, keep, bias, other)
    return (grad_i[None], grad_r[None], grad_b, final_hidden[None], final_cell[None])


def solution(mesh):
    fine = Mesh(mesh.devices.reshape(2, 4, 4, 4), ("xh", "y", "z", "pipe"))
    return jax.shard_map(
        local,
        mesh=fine,
        in_specs=(
            P(None, DP, None),
            P("pipe", None, None),
            P("pipe", None, None),
            P("pipe", None),
            P(DP),
            P("pipe", None, DP, None),
        ),
        out_specs=(
            P("pipe", DP, None),
            P("pipe", DP, None),
            P("pipe", DP),
            P("pipe", DP, None),
            P("pipe", DP, None),
        ),
        check_vma=False,
    )
```

```python
from functools import partial

import jax
import jax.numpy as jnp
from jax import lax
from jax.experimental import pallas as pl
from jax.experimental.pallas import tpu as pltpu
from jax.sharding import Mesh, PartitionSpec as P

BLOCK = 4
LAG = 2
WIDE = 1024
COLS = 256
WHOLE = ()
CHUNK = 256
PANEL = 256
SLOTS = 4
EXTRA = 16
DP = ("xh", "y", "z")
VMEM = pl.BlockSpec(memory_space=pltpu.VMEM)
SMEM = pl.BlockSpec(memory_space=pltpu.SMEM)
HBM = pl.BlockSpec(memory_space=pltpu.HBM)
LIMIT = 8 * 2**20


def squash(value):
    return 0.5 * jnp.tanh(0.5 * value) + 0.5


def dot(a, b):
    return jnp.dot(a, b, preferred_element_type=jnp.float32)


def shifted(at, by):
    return at + by if isinstance(at, int) else pl.multiple_of(at + by, CHUNK)


def over_columns(column, width, steps):
    run = width // steps

    def body(step, carry):
        for j in range(0, run, CHUNK):
            column(j if steps == 1 else pl.multiple_of(step * run + j, CHUNK))
        return carry

    if steps == 1:
        body(0, 0)
    else:
        lax.fori_loop(0, steps, body, 0)


def turn(share, shares, pairs, stage, sems):
    panels = pairs[0][1].shape[0] // PANEL
    groups = panels // SLOTS
    low = share * 2 * groups // shares
    high = (share + 1) * 2 * groups // shares

    for n, (source, target) in enumerate(pairs):

        def copy(at, slot, target=target):
            at = pl.multiple_of(at * PANEL, PANEL)
            return pltpu.make_async_copy(stage.at[slot], target.at[pl.ds(at, PANEL)], sems.at[slot])

        def body(group, carry, source=source, copy=copy):
            def move(slot, carry):
                at = group * SLOTS + slot
                stage[slot] = source[:, pl.ds(pl.multiple_of(at * PANEL, PANEL), PANEL)].T
                copy(at, slot).start()
                return carry

            def settle(slot, carry):
                copy(group * SLOTS + slot, slot).wait()
                return carry

            lax.fori_loop(0, SLOTS, move, 0)
            lax.fori_loop(0, SLOTS, settle, 0)
            return carry

        begin, end = (jnp.clip(v - n * groups, 0, groups) for v in (low, high))
        lax.fori_loop(begin, end, body, 0)


def forward_kernel(place, own, bias, lens, *rest, tick, stages):
    if tick == 0:
        (wi_in, wr_in), rest = rest[:2], rest[2:]
    else:
        arrived, rest = rest[0], rest[9:]
    emitted, wi, wr, xs, gates, cells, hs, wit_far, wrt_far = rest[:9]
    proj, staged, sems, load_sems = rest[-4:]
    span, rows, width = emitted.shape
    stage = place[0]
    blocks = own.shape[0] // span
    at = tick - LAG * stage
    active = (at >= 0) & (at < blocks)
    fs = at * span
    idle = LAG * (stages - 1)
    last = tick == blocks + idle - 1
    pairs = ((wr, wrt_far), (wi, wit_far))
    if tick == 0:
        load_wi = pltpu.make_async_copy(wi_in, wi, load_sems.at[0])
        load_wr = pltpu.make_async_copy(wr_in, wr, load_sems.at[1])
        load_wi.start()
        load_wr.start()
        load_wi.wait()

    @pl.when(active)
    def _():
        if tick == 0:
            xs[pl.ds(fs, span)] = own[pl.ds(fs, span)]
        else:

            @pl.when(stage == 0)
            def _():
                xs[pl.ds(fs, span)] = own[pl.ds(fs, span)]

            @pl.when(stage > 0)
            def _():
                xs[pl.ds(fs, span)] = arrived[...]

        x = xs[pl.ds(fs, span)].reshape(span * rows, width)

        def project(n, carry):
            cols = pl.ds(pl.multiple_of(n * WIDE, WIDE), WIDE)
            proj[:, :, cols] = (dot(x, wi[:, cols]) + bias[:, cols]).reshape(span, rows, WIDE)
            return carry

        lax.fori_loop(0, 4 * width // WIDE, project, 0)

    if tick == 0:

        @pl.when(jnp.logical_not(active))
        def _():
            load_wr.wait()

    top = stages - 1
    turns = {
        0: (stage >= top - 1, 0),
        1: (stage == top, 1),
        idle + blocks - 2: (stage < top, jnp.where(stage == top - 1, 1, 0)),
        idle + blocks - 1: (stage < top - 1, 1),
    }
    if tick in turns:
        here, share = turns[tick]

        @pl.when(here)
        def _():
            turn(share, 2, pairs, staged, sems)

    if last:
        load = pltpu.make_async_copy(wrt_far, rest[9], load_sems.at[0])
        load.start()

    @pl.when(active)
    def _():
        @pl.when(fs == 0)
        def _():
            hs[0] = jnp.zeros((rows, width), jnp.bfloat16)
            cells[0] = jnp.zeros((rows, width), jnp.float32)

        def frame(t, carry, start=False):
            fr = fs + t
            h = hs[fr]

            def column(j):
                part = pl.ds(j, CHUNK)

                def pre(gate):
                    col = pl.ds(shifted(j, gate * width), CHUNK)
                    return proj[t, :, col] if start else proj[t, :, col] + dot(h, wr[:, col])

                alive = fr < lens[:, part]
                i, f, g, o = squash(pre(0)), squash(pre(1)), jnp.tanh(pre(2)), squash(pre(3))
                c = cells[fr, :, part]
                new_c = f * c + i * g
                new_h = (o * jnp.tanh(new_c)).astype(jnp.bfloat16)
                old_h = hs[fr, :, part]
                for gate, value in enumerate((i, f, g, o)):
                    gates[fr, :, pl.ds(shifted(j, gate * width), CHUNK)] = value
                cells[fr + 1, :, part] = jnp.where(alive, new_c, c)
                hs[fr + 1, :, part] = jnp.where(alive, new_h, old_h)
                emitted[t, :, part] = jnp.where(alive, new_h, jnp.zeros_like(new_h))

            over_columns(column, width, 1 if start or tick in WHOLE else 2)
            return carry

        if tick == 0:
            frame(0, 0, start=True)
            load_wr.wait()
        lax.fori_loop(1 if tick == 0 else 0, span, frame, 0)

    if last:
        load.wait()


def block_at(tick, stage, stages, blocks):
    offset = tick - LAG * (stages - 1 - stage)
    return blocks - 1 - offset, (offset >= 0) & (offset < blocks)


def backward_kernel(place, cot, arrived, lens, *rest, tick, stages):
    if tick == 0:
        wit_far, gates_in, cells_in, wrt_in, lower, dy, dz, gates, cells, wit, wrt, dh, dc, sem = rest
        load = pltpu.make_async_copy(wit_far, wit, sem.at[0])
        load.start()
    else:
        lower, dy, dz, gates, cells, wit, wrt, dh, dc = rest[8:]
    span, rows, width = arrived.shape
    total = gates.shape[0]
    half = 2 * width
    stage = place[0]
    blocks = total // span
    at, active = block_at(tick, stage, stages, blocks)
    fs = at * span

    @pl.when(active)
    def _():
        @pl.when(fs + span == total)
        def _():
            dh[...] = jnp.zeros((rows, width), jnp.float32)
            dc[...] = jnp.zeros((rows, width), jnp.float32)

        def frame(n, carry, end=False):
            t = span - 1 - n
            fr = fs + t
            acc = None
            for j in range(0, width, CHUNK):
                part = pl.ds(j, CHUNK)
                alive = fr < lens[:, part]
                i = gates[fr, :, pl.ds(j, CHUNK)]
                f = gates[fr, :, pl.ds(width + j, CHUNK)]
                g = gates[fr, :, pl.ds(2 * width + j, CHUNK)]
                o = gates[fr, :, pl.ds(3 * width + j, CHUNK)]
                u = jnp.where(stage == stages - 1, 0.0, arrived[t, :, part].astype(jnp.float32))
                e = jnp.where(alive, dh[:, part] + u + cot[fr, :, part].astype(jnp.float32), 0.0)
                k = jnp.tanh(cells[fr + 1, :, part])
                old_dc = dc[:, part]
                dcell = jnp.where(alive, old_dc, 0.0) + e * o * (1.0 - k * k)
                parts = (
                    dcell * g * i * (1.0 - i),
                    dcell * cells[fr, :, part] * f * (1.0 - f),
                    dcell * i * (1.0 - g * g),
                    e * k * o * (1.0 - o),
                )
                dc[:, part] = jnp.where(alive, 0.0, old_dc) + dcell * f
                dh[:, part] = jnp.where(alive, 0.0, dh[:, part])
                for gate, value in enumerate(parts):
                    col = pl.ds(gate * width + j, CHUNK)
                    d = value.astype(jnp.bfloat16)
                    if gate < 2:
                        dy[fr, :, col] = d
                    else:
                        dz[fr, :, pl.ds(gate * width + j - half, CHUNK)] = d
                    if not end:
                        term = dot(d, wrt[col, :])
                        acc = term if acc is None else acc + term
            if not end:
                dh[...] = dh[...] + acc
            return carry

        final = tick == blocks + LAG * (stages - 1) - 1
        lax.fori_loop(0, span - 1 if final else span, frame, 0)
        if final:
            frame(span - 1, 0, end=True)


    if tick == 0:
        load.wait()
    if tick < blocks + LAG * (stages - 1) - 1:

        @pl.when(active & (stage > 0))
        def _():
            left, right = (v[pl.ds(fs, span)].reshape(span * rows, half) for v in (dy, dz))

            def descend(n, carry):
                cols = pl.ds(pl.multiple_of(n * CHUNK, CHUNK), CHUNK)
                u = dot(left, wit[pl.ds(0, half), cols]) + dot(right, wit[pl.ds(half, half), cols])
                lower[:, :, cols] = u.astype(jnp.bfloat16).reshape(span, rows, CHUNK)
                return carry

            lax.fori_loop(0, width // CHUNK, descend, 0)


def prepare_kernel(place, xs, hs, *rest):
    to_y, to_z, whole = rest[:4], rest[4:8], rest[8]
    total, rows, width = xs.shape
    y, z = place[1], place[2]
    for n, source in enumerate((xs, hs)):
        flat = source[pl.ds(0, total)].reshape(total * rows, width)
        whole[pl.ds(2 * n, 2)] = flat.T.reshape((2,) + whole.shape[1:])
    for d in range(4):
        for g in range(4):
            to_y[d][g] = whole[g, lax.rem(y + d, 4)]
            for i in range(4):
                to_z[d][g, i] = whole[g, i, lax.rem(z + d, 4)]


def as_rows(value):
    high = value.astype(jnp.bfloat16)
    rest = value - high.astype(jnp.float32)
    middle = rest.astype(jnp.bfloat16)
    low = (rest - middle.astype(jnp.float32)).astype(jnp.bfloat16)
    at = lax.broadcasted_iota(jnp.int32, (EXTRA, value.shape[1]), 0)
    out = jnp.zeros(at.shape, jnp.float32)
    for n, part in enumerate((high, middle, low)):
        out = jnp.where(at == n, part.astype(jnp.float32), out)
    return out.astype(jnp.bfloat16)


def from_rows(block):
    return jnp.sum(block.astype(jnp.float32), axis=0, keepdims=True)


def combine_kernel(place, *rest):
    lefts = (rest[:4], rest[4:8])
    dy, dz = rest[8:10]
    arrivals = (rest[10:13], rest[13:16])
    own_y, own_z, bias, *outs = rest[16:-2]
    left_all, right = rest[-2:]
    y, z = place[1], place[2]
    total, rows, half = dy.shape
    n = total * rows
    fine = left_all.shape[2]
    ones = jnp.ones((EXTRA, 4 * n), jnp.bfloat16)
    for side, (mine, other, own) in enumerate(((dy, z, own_y), (dz, y, own_z))):
        for d in range(4):
            block = mine if d == 0 else arrivals[side][d - 1]
            right[pl.ds(d * n, n)] = block[...].reshape(n, half)
            for g in range(4):
                left_all[g, :, :, pl.ds(d * n, n)] = lefts[side][d][g]

        def columns(step, carry, side=side, other=other, own=own):
            at = pl.multiple_of(step * COLS, COLS)
            cols = pl.ds(at, COLS)
            block = right[:, cols]
            sums = dot(ones, block)[:1]
            bias[:, pl.ds(pl.multiple_of(at + side * half, COLS), COLS)] = sums
            up, down, first, second = outs[4 * side : 4 * side + 4]
            for d in range(4):
                left = left_all[:, lax.rem(other + d, 4)].reshape(4 * fine, 4 * n)
                part = dot(left, block)
                if d == 0:
                    own[:, :, cols] = part.reshape(4, fine, COLS)
                elif d == 2:
                    first[:, cols] = part[: 2 * fine].astype(jnp.bfloat16)
                    second[pl.ds(0, 2 * fine), cols] = part[2 * fine :].astype(jnp.bfloat16)
                    second[pl.ds(2 * fine, EXTRA), cols] = as_rows(sums)
                else:
                    to = up if d == 1 else down
                    to[:, cols] = part
            return carry

        lax.fori_loop(0, half // COLS, columns, 0)


def relay_kernel(place, bias, *rest):
    outs = rest[8:]
    for side in range(2):
        up, down, first, second = rest[4 * side : 4 * side + 4]
        ahead, behind = outs[2 * side : 2 * side + 2]
        n, half = first.shape
        def columns(step, carry, side=side, up=up, down=down, first=first, second=second, ahead=ahead, behind=behind):
            start = pl.multiple_of(step * COLS, COLS)
            cols = pl.ds(start, COLS)
            sums = bias[:, pl.ds(pl.multiple_of(side * half + start, COLS), COLS)]
            top, bottom = pl.ds(0, n), pl.ds(n, n)
            ahead[top, cols] = (up[top, cols] + first[:, cols].astype(jnp.float32)).astype(jnp.bfloat16)
            ahead[bottom, cols] = up[bottom, cols].astype(jnp.bfloat16)
            ahead[pl.ds(2 * n, EXTRA), cols] = as_rows(sums)
            behind[top, cols] = down[top, cols].astype(jnp.bfloat16)
            behind[bottom, cols] = (down[bottom, cols] + second[top, cols].astype(jnp.float32)).astype(jnp.bfloat16)
            behind[pl.ds(2 * n, EXTRA), cols] = as_rows(sums + from_rows(second[pl.ds(n, EXTRA), cols]))
            return carry

        lax.fori_loop(0, half // COLS, columns, 0)


def finish_kernel(place, own_y, own_z, bias, *rest):
    arrivals, keep, kept_bias, give = rest[:4], rest[4], rest[5], rest[6]
    xh = place[3]
    fine, half = own_y.shape[1:]
    for side, own in enumerate((own_y, own_z)):
        cols = pl.ds(side * half, half)
        blocks = arrivals[2 * side : 2 * side + 2]
        for n in range(2):
            mine, other = 2 * n + xh, 2 * n + 1 - xh
            kept, given = own[mine], own[other]
            for block in blocks:
                kept += block[pl.ds(pl.multiple_of(mine * fine, fine), fine)].astype(jnp.float32)
                given += block[pl.ds(pl.multiple_of(other * fine, fine), fine)].astype(jnp.float32)
            keep[n, :, cols] = kept
            give[pl.ds(n * fine, fine), cols] = given.astype(jnp.bfloat16)
        total = bias[:, cols]
        for block in blocks:
            total += from_rows(block[pl.ds(4 * fine, EXTRA)])
        kept_bias[:, cols] = total
        give[pl.ds(2 * fine, EXTRA), cols] = as_rows(total)


def last_kernel(place, keep, bias, arrived, grad_i, grad_r, grad_b):
    fine = keep.shape[1]
    for n, out in enumerate((grad_i, grad_r)):
        out[...] = keep[n] + arrived[pl.ds(n * fine, fine)].astype(jnp.float32)
    width = grad_b.shape[1]
    cols = pl.ds(pl.multiple_of(((place[3] * 4 + place[1]) * 4 + place[2]) * width, width), width)
    grad_b[...] = bias[:, cols] + from_rows(arrived[pl.ds(2 * fine, EXTRA), cols])


def shape(dims, kind):
    return pltpu.VMEM(dims, kind)


def near(array):
    return pltpu.with_memory_space_constraint(array, pltpu.VMEM)


def local(inputs, input_weight, recurrent_weight, gate_bias, lengths, cotangent):
    total, rows, width = inputs.shape
    gated = 4 * width
    stages = lax.axis_size("pipe")
    stage = lax.axis_index("pipe")
    blocks = total // BLOCK
    ticks = blocks + LAG * (stages - 1)
    lens = near(jnp.broadcast_to(lengths[:, None], (rows, width)))
    cot, inputs, gate_bias = near(cotangent[0]), near(inputs), near(gate_bias)
    params = pltpu.CompilerParams(vmem_limit_bytes=LIMIT)
    bf16, f32 = jnp.bfloat16, jnp.float32

    flat, turned = shape((width, gated), bf16), shape((gated, width), bf16)
    kept_gates, kept_cells = shape((total, rows, gated), f32), shape((total + 1, rows, width), f32)
    one = shape((rows, width), f32)
    state = (flat, flat, shape((total, rows, width), bf16), kept_gates, kept_cells)
    fine, half = width // 32, gated // 2
    store = shape((total, rows, half), bf16)
    block = shape((BLOCK, rows, width), bf16)
    far = pltpu.HBM((gated, width), bf16)
    state += (shape((total + 1, rows, width), bf16), far, far)
    def forward(tick):
        first = tick == 0
        extra = (turned,) if tick == ticks - 1 else ()
        return pl.pallas_call(
            partial(forward_kernel, tick=tick, stages=stages),
            out_shape=(block,) + state + extra,
            in_specs=[SMEM] + [VMEM] * 3 + ([HBM] * 2 if first else [VMEM] * 7 + [HBM] * 2),
            out_specs=(VMEM,) * 7 + (HBM,) * 2 + (VMEM,) * len(extra),
            scratch_shapes=[
                pltpu.VMEM((BLOCK, rows, gated), f32),
                pltpu.VMEM((SLOTS, PANEL, width), bf16),
                pltpu.SemaphoreType.DMA((SLOTS,)),
                pltpu.SemaphoreType.DMA((2,)),
            ],
            input_output_aliases={} if first else {5 + n: 1 + n for n in range(8)},
            compiler_params=params,
            name="forward_tick",
        )

    place = jnp.stack([stage] + [lax.axis_index(a) for a in ("y", "z", "xh")]).astype(jnp.int32)
    landed = {}
    for tick in range(ticks):
        if tick == 0:
            got = [pltpu.with_memory_space_constraint(w[0], pltpu.HBM) for w in (input_weight, recurrent_weight)]
        else:
            got = [landed.get(tick, emitted), *held]
        emitted, *held = forward(tick)(place, inputs, gate_bias, lens, *got)
        on = [s for s in range(stages - 1) if 0 <= tick - LAG * s < blocks]
        if on:
            landed[tick + LAG] = near(lax.ppermute(emitted, "pipe", [(s, s + 1) for s in on]))

    _, _, xs, gates, cells, hs, wit_far, _, wrt = held

    def backward(tick):
        first = tick == 0
        aliases = {5: 3, 6: 4, 7: 6} if first else {4 + i: 1 + i for i in range(8)}
        return pl.pallas_call(
            partial(backward_kernel, tick=tick, stages=stages),
            out_shape=(block, store, store, kept_gates, kept_cells, turned, turned, one, one),
            in_specs=[SMEM] + [VMEM] * 3 + ([HBM] + [VMEM] * 3 if first else [VMEM] * 8),
            out_specs=(VMEM,) * 9,
            scratch_shapes=[pltpu.SemaphoreType.DMA((1,))] if first else [],
            input_output_aliases=aliases,
            compiler_params=params,
            name="backward_tick",
        )

    def simple(kernel, name, outs, count, scratch=()):
        return pl.pallas_call(
            kernel,
            out_shape=outs,
            in_specs=[SMEM] + [VMEM] * count,
            out_specs=jax.tree.map(lambda _: VMEM, outs),
            scratch_shapes=scratch,
            compiler_params=params,
            name=name,
        )

    held = [pltpu.with_memory_space_constraint(wit_far, pltpu.HBM), gates, cells, wrt]
    routes = [[(i, (i + d) % 4) for i in range(4)] for d in range(1, 4)]

    def passed(made):
        return [near(lax.ppermute(made[n], "y" if n < 3 else "z", routes[n % 3])) for n in range(6)]

    group = shape((4, 4, fine, total * rows), bf16)
    lefts, landed, lower = [], {}, emitted
    for tick in range(ticks):
        lower, *held = backward(tick)(place, cot, landed.get(tick, lower), lens, *held)
        if tick == 0:
            xs, hs, lower = lax.optimization_barrier((xs, hs, lower))
            spread = simple(prepare_kernel, "prepare", (group,) * 8, 2, [pltpu.VMEM((4, 4, 4, fine, total * rows), bf16)])(
                place, near(xs), near(hs)
            )
        on = [s for s in range(1, stages) if 0 <= tick - LAG * (stages - 1 - s) < blocks]
        if on:
            landed[tick + LAG] = near(lax.ppermute(lower, "pipe", [(s, s - 1) for s in on]))
        if 1 <= tick <= 6:
            axis, d = ("y", tick) if tick < 4 else ("z", tick - 3)
            piece, _ = lax.optimization_barrier((spread[tick if tick < 4 else tick + 1], lower))
            piece = lax.ppermute(piece, axis, routes[d - 1])
            pair = lax.optimization_barrier((landed[tick + LAG], piece))
            landed[tick + LAG], piece = map(near, pair)
            lefts.append(piece)
    dy, dz = held[:2]
    final_hidden, final_cell = hs[total], held[3][total]
    whole, far_part = shape((4, fine, half), f32), shape((4 * fine, half), f32)
    pieces = (far_part, far_part, shape((2 * fine, half), bf16), shape((2 * fine + EXTRA, half), bf16))
    mine_y, mine_z, bias, *made = simple(
        combine_kernel,
        "combine",
        (whole, whole, shape((1, gated), f32)) + pieces * 2,
        16,
        [pltpu.VMEM((4, 4, fine, 4 * total * rows), bf16), pltpu.VMEM((4 * total * rows, half), bf16)],
    )(place, spread[0], *lefts[:3], spread[4], *lefts[3:], dy, dz, *passed([dy] * 3 + [dz] * 3))

    def both_ways(ahead_z, behind_z, ahead_y, behind_y):
        sent = ((ahead_z, "z", 0), (behind_z, "z", 2), (ahead_y, "y", 0), (behind_y, "y", 2))
        return [near(lax.ppermute(v, axis, routes[d])) for v, axis, d in sent]

    got = both_ways(made[2], made[3], made[6], made[7])
    part = shape((4 * fine + EXTRA, half), bf16)
    sends = simple(relay_kernel, "relay", (part,) * 4, 9)(place, bias, *made[:2], *got[:2], *made[4:6], *got[2:])
    keep, bias, give = simple(
        finish_kernel,
        "finish",
        (shape((2, fine, gated), f32), shape((1, gated), f32), shape((2 * fine + EXTRA, gated), bf16)),
        7,
    )(place, mine_y, mine_z, bias, *both_ways(*sends))
    other = near(lax.ppermute(give, "xh", [(0, 1), (1, 0)]))
    made = jax.ShapeDtypeStruct
    grad_i, grad_r, grad_b = simple(
        last_kernel,
        "last",
        (made((fine, gated), f32), made((fine, gated), f32), made((1, gated // 32), f32)),
        3,
    )(place, keep, bias, other)
    return (grad_i[None], grad_r[None], grad_b, final_hidden[None], final_cell[None])


def solution(mesh):
    fine = Mesh(mesh.devices.reshape(2, 4, 4, 4), ("xh", "y", "z", "pipe"))
    return jax.shard_map(
        local,
        mesh=fine,
        in_specs=(
            P(None, DP, None),
            P("pipe", None, None),
            P("pipe", None, None),
            P("pipe", None),
            P(DP),
            P("pipe", None, DP, None),
        ),
        out_specs=(
            P("pipe", DP, None),
            P("pipe", DP, None),
            P("pipe", DP),
            P("pipe", DP, None),
            P("pipe", DP, None),
        ),
        check_vma=False,
    )
```

```python
from functools import partial

import jax
import jax.numpy as jnp
from jax import lax
from jax.experimental import pallas as pl
from jax.experimental.pallas import tpu as pltpu
from jax.sharding import Mesh, PartitionSpec as P

BLOCK = 4
LAG = 2
WIDE = 1024
COLS = 256
WHOLE = ()
CHUNK = 256
PANEL = 256
SLOTS = 4
EXTRA = 16
DP = ("xh", "y", "z")
VMEM = pl.BlockSpec(memory_space=pltpu.VMEM)
SMEM = pl.BlockSpec(memory_space=pltpu.SMEM)
HBM = pl.BlockSpec(memory_space=pltpu.HBM)
LIMIT = 8 * 2**20


def squash(value):
    return 0.5 * jnp.tanh(0.5 * value) + 0.5


def dot(a, b):
    return jnp.dot(a, b, preferred_element_type=jnp.float32)


def shifted(at, by):
    return at + by if isinstance(at, int) else pl.multiple_of(at + by, CHUNK)


def over_columns(column, width, steps):
    run = width // steps

    def body(step, carry):
        for j in range(0, run, CHUNK):
            column(j if steps == 1 else pl.multiple_of(step * run + j, CHUNK))
        return carry

    if steps == 1:
        body(0, 0)
    else:
        lax.fori_loop(0, steps, body, 0)


def turn(share, shares, pairs, stage, sems):
    panels = pairs[0][1].shape[0] // PANEL
    groups = panels // SLOTS
    low = share * 2 * groups // shares
    high = (share + 1) * 2 * groups // shares

    for n, (source, target) in enumerate(pairs):

        def copy(at, slot, target=target):
            at = pl.multiple_of(at * PANEL, PANEL)
            return pltpu.make_async_copy(stage.at[slot], target.at[pl.ds(at, PANEL)], sems.at[slot])

        def body(group, carry, source=source, copy=copy):
            def move(slot, carry):
                at = group * SLOTS + slot
                stage[slot] = source[:, pl.ds(pl.multiple_of(at * PANEL, PANEL), PANEL)].T
                copy(at, slot).start()
                return carry

            def settle(slot, carry):
                copy(group * SLOTS + slot, slot).wait()
                return carry

            lax.fori_loop(0, SLOTS, move, 0)
            lax.fori_loop(0, SLOTS, settle, 0)
            return carry

        begin, end = (jnp.clip(v - n * groups, 0, groups) for v in (low, high))
        lax.fori_loop(begin, end, body, 0)


def forward_kernel(place, *rest, tick, stages):
    if tick == 0:
        (lengths, own, bias_in, wi_in, wr_in), rest = rest[:5], rest[5:]
        bias, lens = rest[9:11]
    else:
        (bias, lens, arrived), rest = rest[:3], rest[11:]
    emitted, wi, wr, xs, gates, cells, hs, wit_far, wrt_far = rest[:9]
    proj, staged, sems, load_sems = rest[-4:]
    span, rows, width = emitted.shape
    stage = place[0]
    blocks = xs.shape[0] // span
    at = tick - LAG * stage
    active = (at >= 0) & (at < blocks)
    fs = at * span
    idle = LAG * (stages - 1)
    last = tick == blocks + idle - 1
    pairs = ((wr, wrt_far), (wi, wit_far))
    if tick == 0:
        load_wi = pltpu.make_async_copy(wi_in, wi, load_sems.at[0])
        load_wr = pltpu.make_async_copy(wr_in, wr, load_sems.at[1])
        load_own = pltpu.make_async_copy(own, xs, load_sems.at[2])
        load_bias = pltpu.make_async_copy(bias_in, bias, load_sems.at[3])
        for load in (load_own, load_bias, load_wi, load_wr):
            load.start()
        at_row = lax.broadcasted_iota(jnp.int32, lens.shape, 0)
        known = jnp.zeros(lens.shape, jnp.int32)
        for n in range(rows):
            known = jnp.where(at_row == n, lengths[n], known)
        lens[...] = known
        for load in (load_own, load_bias, load_wi):
            load.wait()

    @pl.when(active)
    def _():
        if tick > 0:

            @pl.when(stage > 0)
            def _():
                xs[pl.ds(fs, span)] = arrived[...]

        x = xs[pl.ds(fs, span)].reshape(span * rows, width)

        def project(n, carry):
            cols = pl.ds(pl.multiple_of(n * WIDE, WIDE), WIDE)
            proj[:, :, cols] = (dot(x, wi[:, cols]) + bias[:, cols]).reshape(span, rows, WIDE)
            return carry

        lax.fori_loop(0, 4 * width // WIDE, project, 0)

    if tick == 0:

        @pl.when(jnp.logical_not(active))
        def _():
            load_wr.wait()

    top = stages - 1
    turns = {
        0: (stage >= top - 1, 0),
        1: (stage == top, 1),
        idle + blocks - 2: (stage < top, jnp.where(stage == top - 1, 1, 0)),
        idle + blocks - 1: (stage < top - 1, 1),
    }
    if tick in turns:
        here, share = turns[tick]

        @pl.when(here)
        def _():
            turn(share, 2, pairs, staged, sems)

    if last:
        load = pltpu.make_async_copy(wrt_far, rest[9], load_sems.at[0])
        load.start()

    @pl.when(active)
    def _():
        @pl.when(fs == 0)
        def _():
            hs[0] = jnp.zeros((rows, width), jnp.bfloat16)
            cells[0] = jnp.zeros((rows, width), jnp.float32)

        def frame(t, carry, start=False):
            fr = fs + t
            h = hs[fr]

            def column(j):
                part = pl.ds(j, CHUNK)

                def pre(gate):
                    col = pl.ds(shifted(j, gate * width), CHUNK)
                    return proj[t, :, col] if start else proj[t, :, col] + dot(h, wr[:, col])

                alive = fr < lens[:, part]
                i, f, g, o = squash(pre(0)), squash(pre(1)), jnp.tanh(pre(2)), squash(pre(3))
                c = cells[fr, :, part]
                new_c = f * c + i * g
                new_h = (o * jnp.tanh(new_c)).astype(jnp.bfloat16)
                old_h = hs[fr, :, part]
                for gate, value in enumerate((i, f, g, o)):
                    gates[fr, :, pl.ds(shifted(j, gate * width), CHUNK)] = value
                cells[fr + 1, :, part] = jnp.where(alive, new_c, c)
                hs[fr + 1, :, part] = jnp.where(alive, new_h, old_h)
                emitted[t, :, part] = jnp.where(alive, new_h, jnp.zeros_like(new_h))

            over_columns(column, width, 1 if start or tick in WHOLE else 2)
            return carry

        if tick == 0:
            frame(0, 0, start=True)
            load_wr.wait()
        lax.fori_loop(1 if tick == 0 else 0, span, frame, 0)

    if last:
        load.wait()


def block_at(tick, stage, stages, blocks):
    offset = tick - LAG * (stages - 1 - stage)
    return blocks - 1 - offset, (offset >= 0) & (offset < blocks)


def backward_kernel(place, cot, arrived, lens, *rest, tick, stages):
    if tick == 0:
        wit_far, gates_in, cells_in, wrt_in, lower, dy, dz, gates, cells, wit, wrt, dh, dc, sem = rest
        load = pltpu.make_async_copy(wit_far, wit, sem.at[0])
        load.start()
    else:
        lower, dy, dz, gates, cells, wit, wrt, dh, dc = rest[8:]
    span, rows, width = arrived.shape
    total = gates.shape[0]
    half = 2 * width
    stage = place[0]
    blocks = total // span
    at, active = block_at(tick, stage, stages, blocks)
    fs = at * span

    @pl.when(active)
    def _():
        @pl.when(fs + span == total)
        def _():
            dh[...] = jnp.zeros((rows, width), jnp.float32)
            dc[...] = jnp.zeros((rows, width), jnp.float32)

        def frame(n, carry, end=False):
            t = span - 1 - n
            fr = fs + t
            acc = None
            for j in range(0, width, CHUNK):
                part = pl.ds(j, CHUNK)
                alive = fr < lens[:, part]
                i = gates[fr, :, pl.ds(j, CHUNK)]
                f = gates[fr, :, pl.ds(width + j, CHUNK)]
                g = gates[fr, :, pl.ds(2 * width + j, CHUNK)]
                o = gates[fr, :, pl.ds(3 * width + j, CHUNK)]
                u = jnp.where(stage == stages - 1, 0.0, arrived[t, :, part].astype(jnp.float32))
                e = jnp.where(alive, dh[:, part] + u + cot[fr, :, part].astype(jnp.float32), 0.0)
                k = jnp.tanh(cells[fr + 1, :, part])
                old_dc = dc[:, part]
                dcell = jnp.where(alive, old_dc, 0.0) + e * o * (1.0 - k * k)
                parts = (
                    dcell * g * i * (1.0 - i),
                    dcell * cells[fr, :, part] * f * (1.0 - f),
                    dcell * i * (1.0 - g * g),
                    e * k * o * (1.0 - o),
                )
                dc[:, part] = jnp.where(alive, 0.0, old_dc) + dcell * f
                dh[:, part] = jnp.where(alive, 0.0, dh[:, part])
                for gate, value in enumerate(parts):
                    col = pl.ds(gate * width + j, CHUNK)
                    d = value.astype(jnp.bfloat16)
                    if gate < 2:
                        dy[fr, :, col] = d
                    else:
                        dz[fr, :, pl.ds(gate * width + j - half, CHUNK)] = d
                    if not end:
                        term = dot(d, wrt[col, :])
                        acc = term if acc is None else acc + term
            if not end:
                dh[...] = dh[...] + acc
            return carry

        final = tick == blocks + LAG * (stages - 1) - 1
        lax.fori_loop(0, span - 1 if final else span, frame, 0)
        if final:
            frame(span - 1, 0, end=True)


    if tick == 0:
        load.wait()
    if tick < blocks + LAG * (stages - 1) - 1:

        @pl.when(active & (stage > 0))
        def _():
            left, right = (v[pl.ds(fs, span)].reshape(span * rows, half) for v in (dy, dz))

            def descend(n, carry):
                cols = pl.ds(pl.multiple_of(n * CHUNK, CHUNK), CHUNK)
                u = dot(left, wit[pl.ds(0, half), cols]) + dot(right, wit[pl.ds(half, half), cols])
                lower[:, :, cols] = u.astype(jnp.bfloat16).reshape(span, rows, CHUNK)
                return carry

            lax.fori_loop(0, width // CHUNK, descend, 0)


def prepare_kernel(place, xs, hs, *rest):
    to_y, to_z, whole = rest[:4], rest[4:8], rest[8]
    total, rows, width = xs.shape
    y, z = place[1], place[2]
    for n, source in enumerate((xs, hs)):
        flat = source[pl.ds(0, total)].reshape(total * rows, width)
        whole[pl.ds(2 * n, 2)] = flat.T.reshape((2,) + whole.shape[1:])
    for d in range(4):
        for g in range(4):
            to_y[d][g] = whole[g, lax.rem(y + d, 4)]
            for i in range(4):
                to_z[d][g, i] = whole[g, i, lax.rem(z + d, 4)]


def as_rows(value):
    high = value.astype(jnp.bfloat16)
    rest = value - high.astype(jnp.float32)
    middle = rest.astype(jnp.bfloat16)
    low = (rest - middle.astype(jnp.float32)).astype(jnp.bfloat16)
    at = lax.broadcasted_iota(jnp.int32, (EXTRA, value.shape[1]), 0)
    out = jnp.zeros(at.shape, jnp.float32)
    for n, part in enumerate((high, middle, low)):
        out = jnp.where(at == n, part.astype(jnp.float32), out)
    return out.astype(jnp.bfloat16)


def from_rows(block):
    return jnp.sum(block.astype(jnp.float32), axis=0, keepdims=True)


def combine_kernel(place, *rest):
    lefts = (rest[:4], rest[4:8])
    dy, dz = rest[8:10]
    arrivals = (rest[10:13], rest[13:16])
    own_y, own_z, bias, *outs = rest[16:-2]
    left_all, right = rest[-2:]
    y, z = place[1], place[2]
    total, rows, half = dy.shape
    n = total * rows
    fine = left_all.shape[2]
    ones = jnp.ones((EXTRA, 4 * n), jnp.bfloat16)
    for side, (mine, other, own) in enumerate(((dy, z, own_y), (dz, y, own_z))):
        for d in range(4):
            block = mine if d == 0 else arrivals[side][d - 1]
            right[pl.ds(d * n, n)] = block[...].reshape(n, half)
            for g in range(4):
                left_all[g, :, :, pl.ds(d * n, n)] = lefts[side][d][g]

        def columns(step, carry, side=side, other=other, own=own):
            at = pl.multiple_of(step * COLS, COLS)
            cols = pl.ds(at, COLS)
            block = right[:, cols]
            sums = dot(ones, block)[:1]
            bias[:, pl.ds(pl.multiple_of(at + side * half, COLS), COLS)] = sums
            up, down, first, second = outs[4 * side : 4 * side + 4]
            for d in range(4):
                left = left_all[:, lax.rem(other + d, 4)].reshape(4 * fine, 4 * n)
                part = dot(left, block)
                if d == 0:
                    own[:, :, cols] = part.reshape(4, fine, COLS)
                elif d == 2:
                    first[:, cols] = part[: 2 * fine].astype(jnp.bfloat16)
                    second[pl.ds(0, 2 * fine), cols] = part[2 * fine :].astype(jnp.bfloat16)
                    second[pl.ds(2 * fine, EXTRA), cols] = as_rows(sums)
                else:
                    to = up if d == 1 else down
                    to[:, cols] = part
            return carry

        lax.fori_loop(0, half // COLS, columns, 0)


def relay_kernel(place, bias, *rest):
    outs = rest[8:]
    for side in range(2):
        up, down, first, second = rest[4 * side : 4 * side + 4]
        ahead, behind = outs[2 * side : 2 * side + 2]
        n, half = first.shape
        def columns(step, carry, side=side, up=up, down=down, first=first, second=second, ahead=ahead, behind=behind):
            start = pl.multiple_of(step * COLS, COLS)
            cols = pl.ds(start, COLS)
            sums = bias[:, pl.ds(pl.multiple_of(side * half + start, COLS), COLS)]
            top, bottom = pl.ds(0, n), pl.ds(n, n)
            ahead[top, cols] = (up[top, cols] + first[:, cols].astype(jnp.float32)).astype(jnp.bfloat16)
            ahead[bottom, cols] = up[bottom, cols].astype(jnp.bfloat16)
            ahead[pl.ds(2 * n, EXTRA), cols] = as_rows(sums)
            behind[top, cols] = down[top, cols].astype(jnp.bfloat16)
            behind[bottom, cols] = (down[bottom, cols] + second[top, cols].astype(jnp.float32)).astype(jnp.bfloat16)
            behind[pl.ds(2 * n, EXTRA), cols] = as_rows(sums + from_rows(second[pl.ds(n, EXTRA), cols]))
            return carry

        lax.fori_loop(0, half // COLS, columns, 0)


def finish_kernel(place, own, bias, ahead, behind, keep, kept_bias, give, *, side):
    blocks = (ahead, behind)
    xh = place[3]
    fine, half = own.shape[1:]
    for n in range(2):
        mine, other = 2 * n + xh, 2 * n + 1 - xh
        kept, given = own[mine], own[other]
        for block in blocks:
            kept += block[pl.ds(pl.multiple_of(mine * fine, fine), fine)].astype(jnp.float32)
            given += block[pl.ds(pl.multiple_of(other * fine, fine), fine)].astype(jnp.float32)
        keep[n] = kept
        give[pl.ds(n * fine, fine)] = given.astype(jnp.bfloat16)
    total = bias[:, pl.ds(side * half, half)]
    for block in blocks:
        total += from_rows(block[pl.ds(4 * fine, EXTRA)])
    kept_bias[...] = total
    give[pl.ds(2 * fine, EXTRA)] = as_rows(total)


def last_kernel(place, *rest):
    sides = (rest[:3], rest[3:6])
    grad_i, grad_r, grad_b = rest[6:]
    xh = place[3]
    for side, (keep, bias, arrived) in enumerate(sides):
        fine, half = keep.shape[1:]
        for n, out in enumerate((grad_i, grad_r)):
            out[:, pl.ds(side * half, half)] = keep[n] + arrived[pl.ds(n * fine, fine)].astype(jnp.float32)

        @pl.when(xh == side)
        def _():
            width = grad_b.shape[1]
            cols = pl.ds(pl.multiple_of((place[1] * 4 + place[2]) * width, width), width)
            grad_b[...] = bias[:, cols] + from_rows(arrived[pl.ds(2 * fine, EXTRA), cols])


def shape(dims, kind):
    return pltpu.VMEM(dims, kind)


def near(array):
    return pltpu.with_memory_space_constraint(array, pltpu.VMEM)


def local(inputs, input_weight, recurrent_weight, gate_bias, lengths, cotangent):
    total, rows, width = inputs.shape
    gated = 4 * width
    stages = lax.axis_size("pipe")
    stage = lax.axis_index("pipe")
    blocks = total // BLOCK
    ticks = blocks + LAG * (stages - 1)
    cot = near(cotangent[0])
    params = pltpu.CompilerParams(vmem_limit_bytes=LIMIT)
    bf16, f32 = jnp.bfloat16, jnp.float32

    flat, turned = shape((width, gated), bf16), shape((gated, width), bf16)
    kept_gates, kept_cells = shape((total, rows, gated), f32), shape((total + 1, rows, width), f32)
    one = shape((rows, width), f32)
    state = (flat, flat, shape((total, rows, width), bf16), kept_gates, kept_cells)
    fine, half = width // 32, gated // 2
    store = shape((total, rows, half), bf16)
    block = shape((BLOCK, rows, width), bf16)
    far = pltpu.HBM((gated, width), bf16)
    state += (shape((total + 1, rows, width), bf16), far, far)
    def forward(tick):
        first = tick == 0
        extra = (turned,) if tick == ticks - 1 else ()
        if first:
            extra = (shape((1, gated), f32), shape((rows, width), jnp.int32))
        return pl.pallas_call(
            partial(forward_kernel, tick=tick, stages=stages),
            out_shape=(block,) + state + extra,
            in_specs=[SMEM] * 2 + [HBM] * 4 if first else [SMEM] + [VMEM] * 9 + [HBM] * 2,
            out_specs=(VMEM,) * 7 + (HBM,) * 2 + (VMEM,) * len(extra),
            scratch_shapes=[
                pltpu.VMEM((BLOCK, rows, gated), f32),
                pltpu.VMEM((SLOTS, PANEL, width), bf16),
                pltpu.SemaphoreType.DMA((SLOTS,)),
                pltpu.SemaphoreType.DMA((4,)),
            ],
            input_output_aliases={} if first else {4 + n: 1 + n for n in range(8)},
            compiler_params=params,
            name="forward_tick",
        )

    place = jnp.stack([stage] + [lax.axis_index(a) for a in ("y", "z", "xh")]).astype(jnp.int32)
    landed = {}
    for tick in range(ticks):
        if tick == 0:
            far_args = (inputs, gate_bias, input_weight[0], recurrent_weight[0])
            got = [lengths, *(pltpu.with_memory_space_constraint(v, pltpu.HBM) for v in far_args)]
        else:
            got = [bias, lens, landed.get(tick, emitted), *held]
        emitted, *held = forward(tick)(place, *got)
        if tick == 0:
            held, (bias, lens) = held[:8], held[8:]
        on = [s for s in range(stages - 1) if 0 <= tick - LAG * s < blocks]
        if on:
            landed[tick + LAG] = near(lax.ppermute(emitted, "pipe", [(s, s + 1) for s in on]))

    _, _, xs, gates, cells, hs, wit_far, _, wrt = held

    def backward(tick):
        first = tick == 0
        aliases = {5: 3, 6: 4, 7: 6} if first else {4 + i: 1 + i for i in range(8)}
        return pl.pallas_call(
            partial(backward_kernel, tick=tick, stages=stages),
            out_shape=(block, store, store, kept_gates, kept_cells, turned, turned, one, one),
            in_specs=[SMEM] + [VMEM] * 3 + ([HBM] + [VMEM] * 3 if first else [VMEM] * 8),
            out_specs=(VMEM,) * 9,
            scratch_shapes=[pltpu.SemaphoreType.DMA((1,))] if first else [],
            input_output_aliases=aliases,
            compiler_params=params,
            name="backward_tick",
        )

    def simple(kernel, name, outs, count, scratch=()):
        return pl.pallas_call(
            kernel,
            out_shape=outs,
            in_specs=[SMEM] + [VMEM] * count,
            out_specs=jax.tree.map(lambda _: VMEM, outs),
            scratch_shapes=scratch,
            compiler_params=params,
            name=name,
        )

    held = [pltpu.with_memory_space_constraint(wit_far, pltpu.HBM), gates, cells, wrt]
    routes = [[(i, (i + d) % 4) for i in range(4)] for d in range(1, 4)]

    def passed(made):
        return [near(lax.ppermute(made[n], "y" if n < 3 else "z", routes[n % 3])) for n in range(6)]

    group = shape((4, 4, fine, total * rows), bf16)
    lefts, landed, lower = [], {}, emitted
    for tick in range(ticks):
        lower, *held = backward(tick)(place, cot, landed.get(tick, lower), lens, *held)
        if tick == 0:
            xs, hs, lower = lax.optimization_barrier((xs, hs, lower))
            spread = simple(prepare_kernel, "prepare", (group,) * 8, 2, [pltpu.VMEM((4, 4, 4, fine, total * rows), bf16)])(
                place, near(xs), near(hs)
            )
        on = [s for s in range(1, stages) if 0 <= tick - LAG * (stages - 1 - s) < blocks]
        if on:
            landed[tick + LAG] = near(lax.ppermute(lower, "pipe", [(s, s - 1) for s in on]))
        if 1 <= tick <= 6:
            axis, d = ("y", tick) if tick < 4 else ("z", tick - 3)
            piece, _ = lax.optimization_barrier((spread[tick if tick < 4 else tick + 1], lower))
            piece = lax.ppermute(piece, axis, routes[d - 1])
            pair = lax.optimization_barrier((landed[tick + LAG], piece))
            landed[tick + LAG], piece = map(near, pair)
            lefts.append(piece)
    dy, dz = held[:2]
    final_hidden, final_cell = hs[total], held[3][total]
    whole, far_part = shape((4, fine, half), f32), shape((4 * fine, half), f32)
    pieces = (far_part, far_part, shape((2 * fine, half), bf16), shape((2 * fine + EXTRA, half), bf16))
    mine_y, mine_z, bias, *made = simple(
        combine_kernel,
        "combine",
        (whole, whole, shape((1, gated), f32)) + pieces * 2,
        16,
        [pltpu.VMEM((4, 4, fine, 4 * total * rows), bf16), pltpu.VMEM((4 * total * rows, half), bf16)],
    )(place, spread[0], *lefts[:3], spread[4], *lefts[3:], dy, dz, *passed([dy] * 3 + [dz] * 3))

    def both_ways(ahead_z, behind_z, ahead_y, behind_y):
        sent = ((ahead_z, "z", 0), (behind_z, "z", 2), (ahead_y, "y", 0), (behind_y, "y", 2))
        return [near(lax.ppermute(v, axis, routes[d])) for v, axis, d in sent]

    got = both_ways(made[2], made[3], made[6], made[7])
    part = shape((4 * fine + EXTRA, half), bf16)
    sends = simple(relay_kernel, "relay", (part,) * 4, 9)(place, bias, *made[:2], *got[:2], *made[4:6], *got[2:])
    got = both_ways(*sends)
    done = []
    for side, mine in enumerate((mine_y, mine_z)):
        keep, total_bias, give = simple(
            partial(finish_kernel, side=side),
            "finish",
            (shape((2, fine, half), f32), shape((1, half), f32), shape((2 * fine + EXTRA, half), bf16)),
            4,
        )(place, mine, bias, *got[2 * side : 2 * side + 2])
        done += [keep, total_bias, near(lax.ppermute(give, "xh", [(0, 1), (1, 0)]))]
    made = jax.ShapeDtypeStruct
    grad_i, grad_r, grad_b = simple(
        last_kernel,
        "last",
        (made((fine, gated), f32), made((fine, gated), f32), made((1, gated // 32), f32)),
        6,
    )(place, *done)
    return (grad_i[None], grad_r[None], grad_b, final_hidden[None], final_cell[None])


def solution(mesh):
    fine = Mesh(mesh.devices.reshape(2, 4, 4, 4), ("xh", "y", "z", "pipe"))
    return jax.shard_map(
        local,
        mesh=fine,
        in_specs=(
            P(None, DP, None),
            P("pipe", None, None),
            P("pipe", None, None),
            P("pipe", None),
            P(DP),
            P("pipe", None, DP, None),
        ),
        out_specs=(
            P("pipe", DP, None),
            P("pipe", DP, None),
            P("pipe", DP),
            P("pipe", DP, None),
            P("pipe", DP, None),
        ),
        check_vma=False,
    )
```

```python
from functools import partial

import jax
import jax.numpy as jnp
from jax import lax
from jax.experimental import pallas as pl
from jax.experimental.pallas import tpu as pltpu
from jax.sharding import Mesh, PartitionSpec as P

BLOCK = 4
LAG = 2
WIDE = 1024
COLS = 256
WHOLE = ()
CHUNK = 256
PANEL = 256
SLOTS = 4
EXTRA = 16
DP = ("xh", "y", "z")
VMEM = pl.BlockSpec(memory_space=pltpu.VMEM)
SMEM = pl.BlockSpec(memory_space=pltpu.SMEM)
HBM = pl.BlockSpec(memory_space=pltpu.HBM)
LIMIT = 8 * 2**20


def squash(value):
    return 0.5 * jnp.tanh(0.5 * value) + 0.5


def dot(a, b):
    return jnp.dot(a, b, preferred_element_type=jnp.float32)


def shifted(at, by):
    return at + by if isinstance(at, int) else pl.multiple_of(at + by, CHUNK)


def over_columns(column, width, steps):
    run = width // steps

    def body(step, carry):
        for j in range(0, run, CHUNK):
            column(j if steps == 1 else pl.multiple_of(step * run + j, CHUNK))
        return carry

    if steps == 1:
        body(0, 0)
    else:
        lax.fori_loop(0, steps, body, 0)


def turn(share, shares, pairs, stage, sems):
    panels = pairs[0][1].shape[0] // PANEL
    groups = panels // SLOTS
    low = share * 2 * groups // shares
    high = (share + 1) * 2 * groups // shares

    for n, (source, target) in enumerate(pairs):

        def copy(at, slot, target=target):
            at = pl.multiple_of(at * PANEL, PANEL)
            return pltpu.make_async_copy(stage.at[slot], target.at[pl.ds(at, PANEL)], sems.at[slot])

        def body(group, carry, source=source, copy=copy):
            def move(slot, carry):
                at = group * SLOTS + slot
                stage[slot] = source[:, pl.ds(pl.multiple_of(at * PANEL, PANEL), PANEL)].T
                copy(at, slot).start()
                return carry

            def settle(slot, carry):
                copy(group * SLOTS + slot, slot).wait()
                return carry

            lax.fori_loop(0, SLOTS, move, 0)
            lax.fori_loop(0, SLOTS, settle, 0)
            return carry

        begin, end = (jnp.clip(v - n * groups, 0, groups) for v in (low, high))
        lax.fori_loop(begin, end, body, 0)


def forward_kernel(place, *rest, tick, stages):
    if tick == 0:
        (lengths, own, bias_in, wi_in, wr_in), rest = rest[:5], rest[5:]
        bias, lens = rest[9:11]
    else:
        (bias, lens, arrived), rest = rest[:3], rest[11:]
    emitted, wi, wr, xs, gates, cells, hs, wit_far, wrt_far = rest[:9]
    proj, staged, sems, load_sems = rest[-4:]
    span, rows, width = emitted.shape
    stage = place[0]
    blocks = xs.shape[0] // span
    at = tick - LAG * stage
    active = (at >= 0) & (at < blocks)
    fs = at * span
    idle = LAG * (stages - 1)
    last = tick == blocks + idle - 1
    pairs = ((wr, wrt_far), (wi, wit_far))
    if tick == 0:
        load_wi = pltpu.make_async_copy(wi_in, wi, load_sems.at[0])
        load_wr = pltpu.make_async_copy(wr_in, wr, load_sems.at[1])
        load_own = pltpu.make_async_copy(own, xs, load_sems.at[2])
        load_bias = pltpu.make_async_copy(bias_in, bias, load_sems.at[3])
        for load in (load_own, load_bias, load_wi, load_wr):
            load.start()
        at_row = lax.broadcasted_iota(jnp.int32, lens.shape, 0)
        known = jnp.zeros(lens.shape, jnp.int32)
        for n in range(rows):
            known = jnp.where(at_row == n, lengths[n], known)
        lens[...] = known
        for load in (load_own, load_bias, load_wi):
            load.wait()

    @pl.when(active)
    def _():
        if tick > 0:

            @pl.when(stage > 0)
            def _():
                xs[pl.ds(fs, span)] = arrived[...]

        x = xs[pl.ds(fs, span)].reshape(span * rows, width)

        def project(n, carry):
            cols = pl.ds(pl.multiple_of(n * WIDE, WIDE), WIDE)
            proj[:, :, cols] = (dot(x, wi[:, cols]) + bias[:, cols]).reshape(span, rows, WIDE)
            return carry

        lax.fori_loop(0, 4 * width // WIDE, project, 0)

    if tick == 0:

        @pl.when(jnp.logical_not(active))
        def _():
            load_wr.wait()

    top = stages - 1
    turns = {
        0: (stage >= top - 1, 0),
        1: (stage == top, 1),
        idle + blocks - 2: (stage < top, jnp.where(stage == top - 1, 1, 0)),
        idle + blocks - 1: (stage < top - 1, 1),
    }
    if tick in turns:
        here, share = turns[tick]

        @pl.when(here)
        def _():
            turn(share, 2, pairs, staged, sems)

    if last:
        load = pltpu.make_async_copy(wrt_far, rest[9], load_sems.at[0])
        load.start()

    @pl.when(active)
    def _():
        @pl.when(fs == 0)
        def _():
            hs[0] = jnp.zeros((rows, width), jnp.bfloat16)
            cells[0] = jnp.zeros((rows, width), jnp.float32)

        def frame(t, carry, start=False):
            fr = fs + t
            h = hs[fr]

            def column(j):
                part = pl.ds(j, CHUNK)

                def pre(gate):
                    col = pl.ds(shifted(j, gate * width), CHUNK)
                    return proj[t, :, col] if start else proj[t, :, col] + dot(h, wr[:, col])

                alive = fr < lens[:, part]
                i, f, g, o = squash(pre(0)), squash(pre(1)), jnp.tanh(pre(2)), squash(pre(3))
                c = cells[fr, :, part]
                new_c = f * c + i * g
                new_h = (o * jnp.tanh(new_c)).astype(jnp.bfloat16)
                old_h = hs[fr, :, part]
                for gate, value in enumerate((i, f, g, o)):
                    gates[fr, :, pl.ds(shifted(j, gate * width), CHUNK)] = value
                cells[fr + 1, :, part] = jnp.where(alive, new_c, c)
                hs[fr + 1, :, part] = jnp.where(alive, new_h, old_h)
                emitted[t, :, part] = jnp.where(alive, new_h, jnp.zeros_like(new_h))

            over_columns(column, width, 1 if start or tick in WHOLE else 2)
            return carry

        if tick == 0:
            frame(0, 0, start=True)
            load_wr.wait()
        lax.fori_loop(1 if tick == 0 else 0, span, frame, 0)

    if last:
        load.wait()


def block_at(tick, stage, stages, blocks):
    offset = tick - LAG * (stages - 1 - stage)
    return blocks - 1 - offset, (offset >= 0) & (offset < blocks)


def backward_kernel(place, cot, arrived, lens, *rest, tick, stages):
    if tick == 0:
        wit_far, gates_in, cells_in, wrt_in, lower, dy, dz, gates, cells, wit, wrt, dh, dc, sem = rest
        load = pltpu.make_async_copy(wit_far, wit, sem.at[0])
        load.start()
    else:
        lower, dy, dz, gates, cells, wit, wrt, dh, dc = rest[8:]
    span, rows, width = arrived.shape
    total = gates.shape[0]
    half = 2 * width
    stage = place[0]
    blocks = total // span
    at, active = block_at(tick, stage, stages, blocks)
    fs = at * span

    @pl.when(active)
    def _():
        @pl.when(fs + span == total)
        def _():
            dh[...] = jnp.zeros((rows, width), jnp.float32)
            dc[...] = jnp.zeros((rows, width), jnp.float32)

        def frame(n, carry, end=False):
            t = span - 1 - n
            fr = fs + t
            acc = None
            for j in range(0, width, CHUNK):
                part = pl.ds(j, CHUNK)
                alive = fr < lens[:, part]
                i = gates[fr, :, pl.ds(j, CHUNK)]
                f = gates[fr, :, pl.ds(width + j, CHUNK)]
                g = gates[fr, :, pl.ds(2 * width + j, CHUNK)]
                o = gates[fr, :, pl.ds(3 * width + j, CHUNK)]
                u = jnp.where(stage == stages - 1, 0.0, arrived[t, :, part].astype(jnp.float32))
                e = jnp.where(alive, dh[:, part] + u + cot[fr, :, part].astype(jnp.float32), 0.0)
                k = jnp.tanh(cells[fr + 1, :, part])
                old_dc = dc[:, part]
                dcell = jnp.where(alive, old_dc, 0.0) + e * o * (1.0 - k * k)
                parts = (
                    dcell * g * i * (1.0 - i),
                    dcell * cells[fr, :, part] * f * (1.0 - f),
                    dcell * i * (1.0 - g * g),
                    e * k * o * (1.0 - o),
                )
                dc[:, part] = jnp.where(alive, 0.0, old_dc) + dcell * f
                dh[:, part] = jnp.where(alive, 0.0, dh[:, part])
                for gate, value in enumerate(parts):
                    col = pl.ds(gate * width + j, CHUNK)
                    d = value.astype(jnp.bfloat16)
                    if gate < 2:
                        dy[fr, :, col] = d
                    else:
                        dz[fr, :, pl.ds(gate * width + j - half, CHUNK)] = d
                    if not end:
                        term = dot(d, wrt[col, :])
                        acc = term if acc is None else acc + term
            if not end:
                dh[...] = dh[...] + acc
            return carry

        final = tick == blocks + LAG * (stages - 1) - 1
        lax.fori_loop(0, span - 1 if final else span, frame, 0)
        if final:
            frame(span - 1, 0, end=True)


    if tick == 0:
        load.wait()
    if tick < blocks + LAG * (stages - 1) - 1:

        @pl.when(active & (stage > 0))
        def _():
            left, right = (v[pl.ds(fs, span)].reshape(span * rows, half) for v in (dy, dz))

            def descend(n, carry):
                cols = pl.ds(pl.multiple_of(n * CHUNK, CHUNK), CHUNK)
                u = dot(left, wit[pl.ds(0, half), cols]) + dot(right, wit[pl.ds(half, half), cols])
                lower[:, :, cols] = u.astype(jnp.bfloat16).reshape(span, rows, CHUNK)
                return carry

            lax.fori_loop(0, width // CHUNK, descend, 0)


def prepare_kernel(place, xs, hs, *rest):
    to_y, to_z, whole = rest[:4], rest[4:8], rest[8]
    total, rows, width = xs.shape
    y, z = place[1], place[2]
    for n, source in enumerate((xs, hs)):
        flat = source[pl.ds(0, total)].reshape(total * rows, width)
        whole[pl.ds(2 * n, 2)] = flat.T.reshape((2,) + whole.shape[1:])
    for d in range(4):
        for g in range(4):
            to_y[d][g] = whole[g, lax.rem(y + d, 4)]
            for i in range(4):
                to_z[d][g, i] = whole[g, i, lax.rem(z + d, 4)]


def as_rows(value):
    high = value.astype(jnp.bfloat16)
    rest = value - high.astype(jnp.float32)
    middle = rest.astype(jnp.bfloat16)
    low = (rest - middle.astype(jnp.float32)).astype(jnp.bfloat16)
    at = lax.broadcasted_iota(jnp.int32, (EXTRA, value.shape[1]), 0)
    out = jnp.zeros(at.shape, jnp.float32)
    for n, part in enumerate((high, middle, low)):
        out = jnp.where(at == n, part.astype(jnp.float32), out)
    return out.astype(jnp.bfloat16)


def from_rows(block):
    return jnp.sum(block.astype(jnp.float32), axis=0, keepdims=True)


def combine_kernel(place, *rest, side):
    lefts, mine, arrivals = rest[:4], rest[4], rest[5:8]
    own, bias, up, down, first, second, left_all, right = rest[8:]
    other = place[2 - side]
    total, rows, half = mine.shape
    n = total * rows
    fine = left_all.shape[2]
    ones = jnp.ones((EXTRA, 4 * n), jnp.bfloat16)
    for d in range(4):
        block = mine if d == 0 else arrivals[d - 1]
        right[pl.ds(d * n, n)] = block[...].reshape(n, half)
        for g in range(4):
            left_all[g, :, :, pl.ds(d * n, n)] = lefts[d][g]

    def columns(step, carry):
        cols = pl.ds(pl.multiple_of(step * COLS, COLS), COLS)
        block = right[:, cols]
        sums = dot(ones, block)[:1]
        bias[:, cols] = sums
        for d in range(4):
            left = left_all[:, lax.rem(other + d, 4)].reshape(4 * fine, 4 * n)
            part = dot(left, block)
            if d == 0:
                own[:, :, cols] = part.reshape(4, fine, COLS)
            elif d == 2:
                first[:, cols] = part[: 2 * fine].astype(jnp.bfloat16)
                second[pl.ds(0, 2 * fine), cols] = part[2 * fine :].astype(jnp.bfloat16)
                second[pl.ds(2 * fine, EXTRA), cols] = as_rows(sums)
            else:
                to = up if d == 1 else down
                to[:, cols] = part
        return carry

    lax.fori_loop(0, half // COLS, columns, 0)


def relay_kernel(place, bias, up, down, first, second, ahead, behind):
    n, half = first.shape
    top, bottom = pl.ds(0, n), pl.ds(n, n)

    def columns(step, carry):
        cols = pl.ds(pl.multiple_of(step * COLS, COLS), COLS)
        sums = bias[:, cols]
        ahead[top, cols] = (up[top, cols] + first[:, cols].astype(jnp.float32)).astype(jnp.bfloat16)
        ahead[bottom, cols] = up[bottom, cols].astype(jnp.bfloat16)
        ahead[pl.ds(2 * n, EXTRA), cols] = as_rows(sums)
        behind[top, cols] = down[top, cols].astype(jnp.bfloat16)
        behind[bottom, cols] = (down[bottom, cols] + second[top, cols].astype(jnp.float32)).astype(jnp.bfloat16)
        behind[pl.ds(2 * n, EXTRA), cols] = as_rows(sums + from_rows(second[pl.ds(n, EXTRA), cols]))
        return carry

    lax.fori_loop(0, half // COLS, columns, 0)


def finish_kernel(place, own, bias, ahead, behind, keep, kept_bias, give):
    blocks = (ahead, behind)
    xh = place[3]
    fine = own.shape[1]
    for n in range(2):
        mine, other = 2 * n + xh, 2 * n + 1 - xh
        kept, given = own[mine], own[other]
        for block in blocks:
            kept += block[pl.ds(pl.multiple_of(mine * fine, fine), fine)].astype(jnp.float32)
            given += block[pl.ds(pl.multiple_of(other * fine, fine), fine)].astype(jnp.float32)
        keep[n] = kept
        give[pl.ds(n * fine, fine)] = given.astype(jnp.bfloat16)
    total = bias[...]
    for block in blocks:
        total += from_rows(block[pl.ds(4 * fine, EXTRA)])
    kept_bias[...] = total
    give[pl.ds(2 * fine, EXTRA)] = as_rows(total)


def last_kernel(place, *rest):
    sides = (rest[:3], rest[3:6])
    grad_i, grad_r, grad_b = rest[6:]
    xh = place[3]
    for side, (keep, bias, arrived) in enumerate(sides):
        fine, half = keep.shape[1:]
        for n, out in enumerate((grad_i, grad_r)):
            out[:, pl.ds(side * half, half)] = keep[n] + arrived[pl.ds(n * fine, fine)].astype(jnp.float32)

        @pl.when(xh == side)
        def _():
            width = grad_b.shape[1]
            cols = pl.ds(pl.multiple_of((place[1] * 4 + place[2]) * width, width), width)
            grad_b[...] = bias[:, cols] + from_rows(arrived[pl.ds(2 * fine, EXTRA), cols])


def shape(dims, kind):
    return pltpu.VMEM(dims, kind)


def near(array):
    return pltpu.with_memory_space_constraint(array, pltpu.VMEM)


def local(inputs, input_weight, recurrent_weight, gate_bias, lengths, cotangent):
    total, rows, width = inputs.shape
    gated = 4 * width
    stages = lax.axis_size("pipe")
    stage = lax.axis_index("pipe")
    blocks = total // BLOCK
    ticks = blocks + LAG * (stages - 1)
    cot = near(cotangent[0])
    params = pltpu.CompilerParams(vmem_limit_bytes=LIMIT)
    bf16, f32 = jnp.bfloat16, jnp.float32

    flat, turned = shape((width, gated), bf16), shape((gated, width), bf16)
    kept_gates, kept_cells = shape((total, rows, gated), f32), shape((total + 1, rows, width), f32)
    one = shape((rows, width), f32)
    state = (flat, flat, shape((total, rows, width), bf16), kept_gates, kept_cells)
    fine, half = width // 32, gated // 2
    store = shape((total, rows, half), bf16)
    block = shape((BLOCK, rows, width), bf16)
    far = pltpu.HBM((gated, width), bf16)
    state += (shape((total + 1, rows, width), bf16), far, far)
    def forward(tick):
        first = tick == 0
        extra = (turned,) if tick == ticks - 1 else ()
        if first:
            extra = (shape((1, gated), f32), shape((rows, width), jnp.int32))
        return pl.pallas_call(
            partial(forward_kernel, tick=tick, stages=stages),
            out_shape=(block,) + state + extra,
            in_specs=[SMEM] * 2 + [HBM] * 4 if first else [SMEM] + [VMEM] * 9 + [HBM] * 2,
            out_specs=(VMEM,) * 7 + (HBM,) * 2 + (VMEM,) * len(extra),
            scratch_shapes=[
                pltpu.VMEM((BLOCK, rows, gated), f32),
                pltpu.VMEM((SLOTS, PANEL, width), bf16),
                pltpu.SemaphoreType.DMA((SLOTS,)),
                pltpu.SemaphoreType.DMA((4,)),
            ],
            input_output_aliases={} if first else {4 + n: 1 + n for n in range(8)},
            compiler_params=params,
            name="forward_tick",
        )

    place = jnp.stack([stage] + [lax.axis_index(a) for a in ("y", "z", "xh")]).astype(jnp.int32)
    landed = {}
    for tick in range(ticks):
        if tick == 0:
            far_args = (inputs, gate_bias, input_weight[0], recurrent_weight[0])
            got = [lengths, *(pltpu.with_memory_space_constraint(v, pltpu.HBM) for v in far_args)]
        else:
            got = [bias, lens, landed.get(tick, emitted), *held]
        emitted, *held = forward(tick)(place, *got)
        if tick == 0:
            held, (bias, lens) = held[:8], held[8:]
        on = [s for s in range(stages - 1) if 0 <= tick - LAG * s < blocks]
        if on:
            landed[tick + LAG] = near(lax.ppermute(emitted, "pipe", [(s, s + 1) for s in on]))

    _, _, xs, gates, cells, hs, wit_far, _, wrt = held

    def backward(tick):
        first = tick == 0
        aliases = {5: 3, 6: 4, 7: 6} if first else {4 + i: 1 + i for i in range(8)}
        return pl.pallas_call(
            partial(backward_kernel, tick=tick, stages=stages),
            out_shape=(block, store, store, kept_gates, kept_cells, turned, turned, one, one),
            in_specs=[SMEM] + [VMEM] * 3 + ([HBM] + [VMEM] * 3 if first else [VMEM] * 8),
            out_specs=(VMEM,) * 9,
            scratch_shapes=[pltpu.SemaphoreType.DMA((1,))] if first else [],
            input_output_aliases=aliases,
            compiler_params=params,
            name="backward_tick",
        )

    def simple(kernel, name, outs, count, scratch=()):
        return pl.pallas_call(
            kernel,
            out_shape=outs,
            in_specs=[SMEM] + [VMEM] * count,
            out_specs=jax.tree.map(lambda _: VMEM, outs),
            scratch_shapes=scratch,
            compiler_params=params,
            name=name,
        )

    held = [pltpu.with_memory_space_constraint(wit_far, pltpu.HBM), gates, cells, wrt]
    routes = [[(i, (i + d) % 4) for i in range(4)] for d in range(1, 4)]

    def passed(made):
        return [near(lax.ppermute(made[n], "y" if n < 3 else "z", routes[n % 3])) for n in range(6)]

    group = shape((4, 4, fine, total * rows), bf16)
    lefts, landed, lower = [], {}, emitted
    for tick in range(ticks):
        lower, *held = backward(tick)(place, cot, landed.get(tick, lower), lens, *held)
        if tick == 0:
            xs, hs, lower = lax.optimization_barrier((xs, hs, lower))
            spread = simple(prepare_kernel, "prepare", (group,) * 8, 2, [pltpu.VMEM((4, 4, 4, fine, total * rows), bf16)])(
                place, near(xs), near(hs)
            )
        on = [s for s in range(1, stages) if 0 <= tick - LAG * (stages - 1 - s) < blocks]
        if on:
            landed[tick + LAG] = near(lax.ppermute(lower, "pipe", [(s, s - 1) for s in on]))
        if 1 <= tick <= 6:
            axis, d = ("y", tick) if tick < 4 else ("z", tick - 3)
            piece, _ = lax.optimization_barrier((spread[tick if tick < 4 else tick + 1], lower))
            piece = lax.ppermute(piece, axis, routes[d - 1])
            pair = lax.optimization_barrier((landed[tick + LAG], piece))
            landed[tick + LAG], piece = map(near, pair)
            lefts.append(piece)
    dy, dz = held[:2]
    final_hidden, final_cell = hs[total], held[3][total]
    whole, far_part = shape((4, fine, half), f32), shape((4 * fine, half), f32)
    pieces = (far_part, far_part, shape((2 * fine, half), bf16), shape((2 * fine + EXTRA, half), bf16))
    part, bias_row = shape((4 * fine + EXTRA, half), bf16), shape((1, half), f32)
    room = [pltpu.VMEM((4, 4, fine, 4 * total * rows), bf16), pltpu.VMEM((4 * total * rows, half), bf16)]

    def ring(axis, ahead, behind):
        return [near(lax.ppermute(v, axis, routes[d])) for v, d in ((ahead, 0), (behind, 2))]

    arrivals, done = passed([dy] * 3 + [dz] * 3), []
    for side, (mine, axis) in enumerate(((dy, "z"), (dz, "y"))):
        three = slice(3 * side, 3 * side + 3)
        own, bias, up, down, *pair = simple(partial(combine_kernel, side=side), "combine", (whole, bias_row) + pieces, 8, room)(
            place, spread[4 * side], *lefts[three], mine, *arrivals[three]
        )
        pair = simple(relay_kernel, "relay", (part,) * 2, 5)(place, bias, up, down, *ring(axis, *pair))
        outs = (shape((2, fine, half), f32), bias_row, shape((2 * fine + EXTRA, half), bf16))
        keep, bias, give = simple(finish_kernel, "finish", outs, 4)(place, own, bias, *ring(axis, *pair))
        done += [keep, bias, near(lax.ppermute(give, "xh", [(0, 1), (1, 0)]))]
    made = jax.ShapeDtypeStruct
    grad_i, grad_r, grad_b = simple(
        last_kernel,
        "last",
        (made((fine, gated), f32), made((fine, gated), f32), made((1, gated // 32), f32)),
        6,
    )(place, *done)
    return (grad_i[None], grad_r[None], grad_b, final_hidden[None], final_cell[None])


def solution(mesh):
    fine = Mesh(mesh.devices.reshape(2, 4, 4, 4), ("xh", "y", "z", "pipe"))
    return jax.shard_map(
        local,
        mesh=fine,
        in_specs=(
            P(None, DP, None),
            P("pipe", None, None),
            P("pipe", None, None),
            P("pipe", None),
            P(DP),
            P("pipe", None, DP, None),
        ),
        out_specs=(
            P("pipe", DP, None),
            P("pipe", DP, None),
            P("pipe", DP),
            P("pipe", DP, None),
            P("pipe", DP, None),
        ),
        check_vma=False,
    )
```

```python
from functools import partial

import jax
import jax.numpy as jnp
from jax import lax
from jax.experimental import pallas as pl
from jax.experimental.pallas import tpu as pltpu
from jax.sharding import Mesh, PartitionSpec as P

BLOCK = 4
LAG = 2
WIDE = 1024
COLS = 256
WHOLE = ()
CHUNK = 256
PANEL = 256
SLOTS = 4
EXTRA = 16
DP = ("xh", "y", "z")
VMEM = pl.BlockSpec(memory_space=pltpu.VMEM)
SMEM = pl.BlockSpec(memory_space=pltpu.SMEM)
HBM = pl.BlockSpec(memory_space=pltpu.HBM)
LIMIT = 8 * 2**20


def squash(value):
    return 0.5 * jnp.tanh(0.5 * value) + 0.5


def dot(a, b):
    return jnp.dot(a, b, preferred_element_type=jnp.float32)


def shifted(at, by):
    return at + by if isinstance(at, int) else pl.multiple_of(at + by, CHUNK)


def over_columns(column, width, steps):
    run = width // steps

    def body(step, carry):
        for j in range(0, run, CHUNK):
            column(j if steps == 1 else pl.multiple_of(step * run + j, CHUNK))
        return carry

    if steps == 1:
        body(0, 0)
    else:
        lax.fori_loop(0, steps, body, 0)


def turn(share, shares, pairs, stage, sems):
    panels = pairs[0][1].shape[0] // PANEL
    groups = panels // SLOTS
    low = share * 2 * groups // shares
    high = (share + 1) * 2 * groups // shares

    for n, (source, target) in enumerate(pairs):

        def copy(at, slot, target=target):
            at = pl.multiple_of(at * PANEL, PANEL)
            return pltpu.make_async_copy(stage.at[slot], target.at[pl.ds(at, PANEL)], sems.at[slot])

        def body(group, carry, source=source, copy=copy):
            def move(slot, carry):
                at = group * SLOTS + slot
                stage[slot] = source[:, pl.ds(pl.multiple_of(at * PANEL, PANEL), PANEL)].T
                copy(at, slot).start()
                return carry

            def settle(slot, carry):
                copy(group * SLOTS + slot, slot).wait()
                return carry

            lax.fori_loop(0, SLOTS, move, 0)
            lax.fori_loop(0, SLOTS, settle, 0)
            return carry

        begin, end = (jnp.clip(v - n * groups, 0, groups) for v in (low, high))
        lax.fori_loop(begin, end, body, 0)


def forward_kernel(place, *rest, tick, stages):
    if tick == 0:
        (lengths, own, bias_in, wi_in, wr_in), rest = rest[:5], rest[5:]
        bias, lens = rest[9:11]
    else:
        (bias, lens, arrived), rest = rest[:3], rest[11:]
    emitted, wi, wr, xs, gates, cells, hs, wit_far, wrt_far = rest[:9]
    proj, staged, sems, load_sems = rest[-4:]
    span, rows, width = emitted.shape
    stage = place[0]
    blocks = xs.shape[0] // span
    at = tick - LAG * stage
    active = (at >= 0) & (at < blocks)
    fs = at * span
    idle = LAG * (stages - 1)
    last = tick == blocks + idle - 1
    pairs = ((wr, wrt_far), (wi, wit_far))
    if tick == 0:
        load_wi = pltpu.make_async_copy(wi_in, wi, load_sems.at[0])
        load_wr = pltpu.make_async_copy(wr_in, wr, load_sems.at[1])
        load_own = pltpu.make_async_copy(own, xs, load_sems.at[2])
        load_bias = pltpu.make_async_copy(bias_in, bias, load_sems.at[3])
        for load in (load_own, load_bias, load_wi, load_wr):
            load.start()
        at_row = lax.broadcasted_iota(jnp.int32, lens.shape, 0)
        known = jnp.zeros(lens.shape, jnp.int32)
        for n in range(rows):
            known = jnp.where(at_row == n, lengths[n], known)
        lens[...] = known
        for load in (load_own, load_bias, load_wi):
            load.wait()

    @pl.when(active)
    def _():
        if tick > 0:

            @pl.when(stage > 0)
            def _():
                xs[pl.ds(fs, span)] = arrived[...]

        x = xs[pl.ds(fs, span)].reshape(span * rows, width)

        def project(n, carry):
            cols = pl.ds(pl.multiple_of(n * WIDE, WIDE), WIDE)
            proj[:, :, cols] = (dot(x, wi[:, cols]) + bias[:, cols]).reshape(span, rows, WIDE)
            return carry

        lax.fori_loop(0, 4 * width // WIDE, project, 0)

    if tick == 0:

        @pl.when(jnp.logical_not(active))
        def _():
            load_wr.wait()

    top = stages - 1
    turns = {
        0: (stage >= top - 1, 0),
        1: (stage == top, 1),
        idle + blocks - 2: (stage < top, jnp.where(stage == top - 1, 1, 0)),
        idle + blocks - 1: (stage < top - 1, 1),
    }
    if tick in turns:
        here, share = turns[tick]

        @pl.when(here)
        def _():
            turn(share, 2, pairs, staged, sems)

    if last:
        load = pltpu.make_async_copy(wrt_far, rest[9], load_sems.at[0])
        load.start()

    @pl.when(active)
    def _():
        @pl.when(fs == 0)
        def _():
            hs[0] = jnp.zeros((rows, width), jnp.bfloat16)
            cells[0] = jnp.zeros((rows, width), jnp.float32)

        def frame(t, carry, start=False):
            fr = fs + t
            h = hs[fr]

            def column(j):
                part = pl.ds(j, CHUNK)

                def pre(gate):
                    col = pl.ds(shifted(j, gate * width), CHUNK)
                    return proj[t, :, col] if start else proj[t, :, col] + dot(h, wr[:, col])

                alive = fr < lens[:, part]
                i, f, g, o = squash(pre(0)), squash(pre(1)), jnp.tanh(pre(2)), squash(pre(3))
                c = cells[fr, :, part]
                new_c = f * c + i * g
                new_h = (o * jnp.tanh(new_c)).astype(jnp.bfloat16)
                old_h = hs[fr, :, part]
                for gate, value in enumerate((i, f, g, o)):
                    gates[fr, :, pl.ds(shifted(j, gate * width), CHUNK)] = value
                cells[fr + 1, :, part] = jnp.where(alive, new_c, c)
                hs[fr + 1, :, part] = jnp.where(alive, new_h, old_h)
                emitted[t, :, part] = jnp.where(alive, new_h, jnp.zeros_like(new_h))

            over_columns(column, width, 1 if start or tick in WHOLE else 2)
            return carry

        if tick == 0:
            frame(0, 0, start=True)
            load_wr.wait()
        lax.fori_loop(1 if tick == 0 else 0, span, frame, 0)

    if last:
        load.wait()


def block_at(tick, stage, stages, blocks):
    offset = tick - LAG * (stages - 1 - stage)
    return blocks - 1 - offset, (offset >= 0) & (offset < blocks)


def backward_kernel(place, cot, arrived, lens, *rest, tick, stages):
    if tick == 0:
        wit_far, gates_in, cells_in, wrt_in, lower, dy, dz, gates, cells, wit, wrt, dh, dc, sem = rest
        load = pltpu.make_async_copy(wit_far, wit, sem.at[0])
        load.start()
    else:
        lower, dy, dz, gates, cells, wit, wrt, dh, dc = rest[8:]
    span, rows, width = arrived.shape
    total = gates.shape[0]
    half = 2 * width
    stage = place[0]
    blocks = total // span
    at, active = block_at(tick, stage, stages, blocks)
    fs = at * span

    @pl.when(active)
    def _():
        @pl.when(fs + span == total)
        def _():
            dh[...] = jnp.zeros((rows, width), jnp.float32)
            dc[...] = jnp.zeros((rows, width), jnp.float32)

        def frame(n, carry, end=False):
            t = span - 1 - n
            fr = fs + t
            acc = None
            for j in range(0, width, CHUNK):
                part = pl.ds(j, CHUNK)
                alive = fr < lens[:, part]
                i = gates[fr, :, pl.ds(j, CHUNK)]
                f = gates[fr, :, pl.ds(width + j, CHUNK)]
                g = gates[fr, :, pl.ds(2 * width + j, CHUNK)]
                o = gates[fr, :, pl.ds(3 * width + j, CHUNK)]
                u = jnp.where(stage == stages - 1, 0.0, arrived[t, :, part].astype(jnp.float32))
                e = jnp.where(alive, dh[:, part] + u + cot[fr, :, part].astype(jnp.float32), 0.0)
                k = jnp.tanh(cells[fr + 1, :, part])
                old_dc = dc[:, part]
                dcell = jnp.where(alive, old_dc, 0.0) + e * o * (1.0 - k * k)
                parts = (
                    dcell * g * i * (1.0 - i),
                    dcell * cells[fr, :, part] * f * (1.0 - f),
                    dcell * i * (1.0 - g * g),
                    e * k * o * (1.0 - o),
                )
                dc[:, part] = jnp.where(alive, 0.0, old_dc) + dcell * f
                dh[:, part] = jnp.where(alive, 0.0, dh[:, part])
                for gate, value in enumerate(parts):
                    col = pl.ds(gate * width + j, CHUNK)
                    d = value.astype(jnp.bfloat16)
                    if gate < 2:
                        dy[fr, :, col] = d
                    else:
                        dz[fr, :, pl.ds(gate * width + j - half, CHUNK)] = d
                    if not end:
                        term = dot(d, wrt[col, :])
                        acc = term if acc is None else acc + term
            if not end:
                dh[...] = dh[...] + acc
            return carry

        final = tick == blocks + LAG * (stages - 1) - 1
        lax.fori_loop(0, span - 1 if final else span, frame, 0)
        if final:
            frame(span - 1, 0, end=True)


    if tick == 0:
        load.wait()
    if tick < blocks + LAG * (stages - 1) - 1:

        @pl.when(active & (stage > 0))
        def _():
            left, right = (v[pl.ds(fs, span)].reshape(span * rows, half) for v in (dy, dz))

            def descend(n, carry):
                cols = pl.ds(pl.multiple_of(n * CHUNK, CHUNK), CHUNK)
                u = dot(left, wit[pl.ds(0, half), cols]) + dot(right, wit[pl.ds(half, half), cols])
                lower[:, :, cols] = u.astype(jnp.bfloat16).reshape(span, rows, CHUNK)
                return carry

            lax.fori_loop(0, width // CHUNK, descend, 0)


def prepare_kernel(place, xs, hs, *rest):
    to_y, to_z, whole = rest[:4], rest[4:8], rest[8]
    total, rows, width = xs.shape
    y, z = place[1], place[2]
    for n, source in enumerate((xs, hs)):
        flat = source[pl.ds(0, total)].reshape(total * rows, width)
        whole[pl.ds(2 * n, 2)] = flat.T.reshape((2,) + whole.shape[1:])
    for d in range(4):
        for g in range(4):
            to_y[d][g] = whole[g, lax.rem(y + d, 4)]
            for i in range(4):
                to_z[d][g, i] = whole[g, i, lax.rem(z + d, 4)]


def as_rows(value):
    high = value.astype(jnp.bfloat16)
    rest = value - high.astype(jnp.float32)
    middle = rest.astype(jnp.bfloat16)
    low = (rest - middle.astype(jnp.float32)).astype(jnp.bfloat16)
    at = lax.broadcasted_iota(jnp.int32, (EXTRA, value.shape[1]), 0)
    out = jnp.zeros(at.shape, jnp.float32)
    for n, part in enumerate((high, middle, low)):
        out = jnp.where(at == n, part.astype(jnp.float32), out)
    return out.astype(jnp.bfloat16)


def from_rows(block):
    return jnp.sum(block.astype(jnp.float32), axis=0, keepdims=True)


def combine_kernel(place, *rest, side):
    lefts, mine, arrivals = rest[:4], rest[4], rest[5:8]
    own, bias, up, down, first, second, left_all, right = rest[8:]
    other = place[2 - side]
    total, rows, half = mine.shape
    n = total * rows
    fine = left_all.shape[2]
    ones = jnp.ones((EXTRA, 4 * n), jnp.bfloat16)
    for d in range(4):
        block = mine if d == 0 else arrivals[d - 1]
        right[pl.ds(d * n, n)] = block[...].reshape(n, half)
        for g in range(4):
            left_all[g, :, :, pl.ds(d * n, n)] = lefts[d][g]

    def columns(step, carry):
        cols = pl.ds(pl.multiple_of(step * COLS, COLS), COLS)
        block = right[:, cols]
        sums = dot(ones, block)[:1]
        bias[:, cols] = sums
        for d in range(4):
            left = left_all[:, lax.rem(other + d, 4)].reshape(4 * fine, 4 * n)
            part = dot(left, block)
            if d == 0:
                own[:, :, cols] = part.reshape(4, fine, COLS)
            elif d == 2:
                first[:, cols] = part[: 2 * fine].astype(jnp.bfloat16)
                second[pl.ds(0, 2 * fine), cols] = part[2 * fine :].astype(jnp.bfloat16)
                second[pl.ds(2 * fine, EXTRA), cols] = as_rows(sums)
            else:
                to = up if d == 1 else down
                to[:, cols] = part
        return carry

    lax.fori_loop(0, half // COLS, columns, 0)


def relay_kernel(place, bias, up, down, first, second, ahead, behind):
    n, half = first.shape
    top, bottom = pl.ds(0, n), pl.ds(n, n)

    def columns(step, carry):
        cols = pl.ds(pl.multiple_of(step * COLS, COLS), COLS)
        sums = bias[:, cols]
        ahead[top, cols] = (up[top, cols] + first[:, cols].astype(jnp.float32)).astype(jnp.bfloat16)
        ahead[bottom, cols] = up[bottom, cols].astype(jnp.bfloat16)
        ahead[pl.ds(2 * n, EXTRA), cols] = as_rows(sums)
        behind[top, cols] = down[top, cols].astype(jnp.bfloat16)
        behind[bottom, cols] = (down[bottom, cols] + second[top, cols].astype(jnp.float32)).astype(jnp.bfloat16)
        behind[pl.ds(2 * n, EXTRA), cols] = as_rows(sums + from_rows(second[pl.ds(n, EXTRA), cols]))
        return carry

    lax.fori_loop(0, half // COLS, columns, 0)


def finish_kernel(place, own, bias, ahead, behind, keep, kept_bias, give):
    blocks = (ahead, behind)
    xh = place[3]
    fine = own.shape[1]
    for n in range(2):
        mine, other = 2 * n + xh, 2 * n + 1 - xh
        kept, given = own[mine], own[other]
        for block in blocks:
            kept += block[pl.ds(pl.multiple_of(mine * fine, fine), fine)].astype(jnp.float32)
            given += block[pl.ds(pl.multiple_of(other * fine, fine), fine)].astype(jnp.float32)
        keep[n] = kept
        give[pl.ds(n * fine, fine)] = given.astype(jnp.bfloat16)
    total = bias[...]
    for block in blocks:
        total += from_rows(block[pl.ds(4 * fine, EXTRA)])
    kept_bias[...] = total
    give[pl.ds(2 * fine, EXTRA)] = as_rows(total)


def last_kernel(place, *rest):
    sides = (rest[:3], rest[3:6])
    grad_i, grad_r, grad_b = rest[6:]
    xh = place[3]
    for side, (keep, bias, arrived) in enumerate(sides):
        fine, half = keep.shape[1:]
        for n, out in enumerate((grad_i, grad_r)):
            out[:, pl.ds(side * half, half)] = keep[n] + arrived[pl.ds(n * fine, fine)].astype(jnp.float32)

        @pl.when(xh == side)
        def _():
            width = grad_b.shape[1]
            cols = pl.ds(pl.multiple_of((place[1] * 4 + place[2]) * width, width), width)
            grad_b[...] = bias[:, cols] + from_rows(arrived[pl.ds(2 * fine, EXTRA), cols])


def shape(dims, kind):
    return pltpu.VMEM(dims, kind)


def near(array):
    return pltpu.with_memory_space_constraint(array, pltpu.VMEM)


def local(inputs, input_weight, recurrent_weight, gate_bias, lengths, cotangent):
    total, rows, width = inputs.shape
    gated = 4 * width
    stages = lax.axis_size("pipe")
    stage = lax.axis_index("pipe")
    blocks = total // BLOCK
    ticks = blocks + LAG * (stages - 1)
    cot = near(cotangent[0])
    params = pltpu.CompilerParams(vmem_limit_bytes=LIMIT)
    bf16, f32 = jnp.bfloat16, jnp.float32

    flat, turned = shape((width, gated), bf16), shape((gated, width), bf16)
    kept_gates, kept_cells = shape((total, rows, gated), f32), shape((total + 1, rows, width), f32)
    one = shape((rows, width), f32)
    state = (flat, flat, shape((total, rows, width), bf16), kept_gates, kept_cells)
    fine, half = width // 32, gated // 2
    store = shape((total, rows, half), bf16)
    block = shape((BLOCK, rows, width), bf16)
    far = pltpu.HBM((gated, width), bf16)
    state += (shape((total + 1, rows, width), bf16), far, far)
    def forward(tick):
        first = tick == 0
        extra = (turned,) if tick == ticks - 1 else ()
        if first:
            extra = (shape((1, gated), f32), shape((rows, width), jnp.int32))
        return pl.pallas_call(
            partial(forward_kernel, tick=tick, stages=stages),
            out_shape=(block,) + state + extra,
            in_specs=[SMEM] * 2 + [HBM] * 4 if first else [SMEM] + [VMEM] * 9 + [HBM] * 2,
            out_specs=(VMEM,) * 7 + (HBM,) * 2 + (VMEM,) * len(extra),
            scratch_shapes=[
                pltpu.VMEM((BLOCK, rows, gated), f32),
                pltpu.VMEM((SLOTS, PANEL, width), bf16),
                pltpu.SemaphoreType.DMA((SLOTS,)),
                pltpu.SemaphoreType.DMA((4,)),
            ],
            input_output_aliases={} if first else {4 + n: 1 + n for n in range(8)},
            compiler_params=params,
            name="forward_tick",
        )

    place = jnp.stack([stage] + [lax.axis_index(a) for a in ("y", "z", "xh")]).astype(jnp.int32)
    landed = {}
    for tick in range(ticks):
        if tick == 0:
            far_args = (inputs, gate_bias, input_weight[0], recurrent_weight[0])
            got = [lengths, *(pltpu.with_memory_space_constraint(v, pltpu.HBM) for v in far_args)]
        else:
            got = [bias, lens, landed.get(tick, emitted), *held]
        emitted, *held = forward(tick)(place, *got)
        if tick == 0:
            held, (bias, lens) = held[:8], held[8:]
        on = [s for s in range(stages - 1) if 0 <= tick - LAG * s < blocks]
        if on:
            landed[tick + LAG] = near(lax.ppermute(emitted, "pipe", [(s, s + 1) for s in on]))

    _, _, xs, gates, cells, hs, wit_far, _, wrt = held

    def backward(tick):
        first = tick == 0
        aliases = {5: 3, 6: 4, 7: 6} if first else {4 + i: 1 + i for i in range(8)}
        return pl.pallas_call(
            partial(backward_kernel, tick=tick, stages=stages),
            out_shape=(block, store, store, kept_gates, kept_cells, turned, turned, one, one),
            in_specs=[SMEM] + [VMEM] * 3 + ([HBM] + [VMEM] * 3 if first else [VMEM] * 8),
            out_specs=(VMEM,) * 9,
            scratch_shapes=[pltpu.SemaphoreType.DMA((1,))] if first else [],
            input_output_aliases=aliases,
            compiler_params=params,
            name="backward_tick",
        )

    def simple(kernel, name, outs, count, scratch=()):
        return pl.pallas_call(
            kernel,
            out_shape=outs,
            in_specs=[SMEM] + [VMEM] * count,
            out_specs=jax.tree.map(lambda _: VMEM, outs),
            scratch_shapes=scratch,
            compiler_params=params,
            name=name,
        )

    held = [pltpu.with_memory_space_constraint(wit_far, pltpu.HBM), gates, cells, wrt]
    routes = [[(i, (i + d) % 4) for i in range(4)] for d in range(1, 4)]

    def passed(made):
        return [near(lax.ppermute(made[n], "y" if n < 3 else "z", routes[n % 3])) for n in range(6)]

    group = shape((4, 4, fine, total * rows), bf16)
    lefts, landed, lower = {}, {}, emitted
    for tick in range(ticks):
        lower, *held = backward(tick)(place, cot, landed.get(tick, lower), lens, *held)
        if tick == 0:
            xs, hs, lower = lax.optimization_barrier((xs, hs, lower))
            spread = simple(prepare_kernel, "prepare", (group,) * 8, 2, [pltpu.VMEM((4, 4, 4, fine, total * rows), bf16)])(
                place, near(xs), near(hs)
            )
        on = [s for s in range(1, stages) if 0 <= tick - LAG * (stages - 1 - s) < blocks]
        if on:
            landed[tick + LAG] = near(lax.ppermute(lower, "pipe", [(s, s - 1) for s in on]))
        if 1 <= tick <= 6:
            axis, d = (("y", 2), ("z", 2), ("y", 1), ("y", 3), ("z", 1), ("z", 3))[tick - 1]
            piece, _ = lax.optimization_barrier((spread[d if axis == "y" else 4 + d], lower))
            piece = lax.ppermute(piece, axis, routes[d - 1])
            pair = lax.optimization_barrier((landed[tick + LAG], piece))
            landed[tick + LAG], piece = map(near, pair)
            lefts[axis, d] = piece
    dy, dz = held[:2]
    final_hidden, final_cell = hs[total], held[3][total]
    whole, far_part = shape((4, fine, half), f32), shape((4 * fine, half), f32)
    pieces = (far_part, far_part, shape((2 * fine, half), bf16), shape((2 * fine + EXTRA, half), bf16))
    part, bias_row = shape((4 * fine + EXTRA, half), bf16), shape((1, half), f32)
    room = [pltpu.VMEM((4, 4, fine, 4 * total * rows), bf16), pltpu.VMEM((4 * total * rows, half), bf16)]

    def ring(axis, ahead, behind):
        return [near(lax.ppermute(v, axis, routes[d])) for v, d in ((ahead, 0), (behind, 2))]

    arrivals, done = passed([dy] * 3 + [dz] * 3), []
    for side, (mine, axis) in enumerate(((dy, "z"), (dz, "y"))):
        three = slice(3 * side, 3 * side + 3)
        near_side = [lefts["yz"[side], d] for d in range(1, 4)]
        own, bias, up, down, *pair = simple(partial(combine_kernel, side=side), "combine", (whole, bias_row) + pieces, 8, room)(
            place, spread[4 * side], *near_side, mine, *arrivals[three]
        )
        pair = simple(relay_kernel, "relay", (part,) * 2, 5)(place, bias, up, down, *ring(axis, *pair))
        outs = (shape((2, fine, half), f32), bias_row, shape((2 * fine + EXTRA, half), bf16))
        keep, bias, give = simple(finish_kernel, "finish", outs, 4)(place, own, bias, *ring(axis, *pair))
        done += [keep, bias, near(lax.ppermute(give, "xh", [(0, 1), (1, 0)]))]
    made = jax.ShapeDtypeStruct
    grad_i, grad_r, grad_b = simple(
        last_kernel,
        "last",
        (made((fine, gated), f32), made((fine, gated), f32), made((1, gated // 32), f32)),
        6,
    )(place, *done)
    return (grad_i[None], grad_r[None], grad_b, final_hidden[None], final_cell[None])


def solution(mesh):
    fine = Mesh(mesh.devices.reshape(2, 4, 4, 4), ("xh", "y", "z", "pipe"))
    return jax.shard_map(
        local,
        mesh=fine,
        in_specs=(
            P(None, DP, None),
            P("pipe", None, None),
            P("pipe", None, None),
            P("pipe", None),
            P(DP),
            P("pipe", None, DP, None),
        ),
        out_specs=(
            P("pipe", DP, None),
            P("pipe", DP, None),
            P("pipe", DP),
            P("pipe", DP, None),
            P("pipe", DP, None),
        ),
        check_vma=False,
    )
```
